32 devices in a mesh: grp: 2 (over y), bank: 4 (over z), seg: 4 (over x, core).
Axes of the slice: x: 2, y: 2, z: 4, core: 2. Of those that a mesh axis runs over, the one named last changes fastest.
Arguments:
- strain: bfloat16 [256, 2, 2, 2048], P(('grp', 'bank'), None, None, 'seg'), parts along dimension 0, may hold values from -3 to 3
- region_of: int32 [256], P(('grp', 'bank')), parts along dimension 0, may hold values from 0 to 3, as said below
- templates: bfloat16 [256, 2, 2048], P('bank', None, 'seg'), may hold values from -60 to 60
- reads: int32 [4, 4], replicated, may hold values from 0 to 15, as said below
- edges: int32 [256, 15], replicated, may hold values from 48 to 2000, as said below
Outputs:
- snr_power: float32 [16, 64, 256], P('seg', None, ('grp', 'bank')), parts along dimension 2
- chisq: float32 [16, 64, 256], P('seg', None, ('grp', 'bank')), parts along dimension 2
The draws below stay inside these ranges and needn't reach their ends.
There are 2 independent parts, one for each index of `grp`. The reference program is written for one: setup_inputs(seed, part) draws one part's arguments, and reference() takes and returns one part's arrays. A program takes and returns all parts, laid end to end along the dimension named above; an argument that names none is the same for every part. Nothing has to cross between parts.
Inputs may be any that keep to these rules, and one draw needn't show every extreme that they name: `region_of`: the 32 records of one index of bank name any one region at most 24 times, and in every draw one region is named exactly 24 times by the records of every index of bank. Region r reads only blocks held by indices r - 1, r and r + 1 of bank (block b is held by index b // 4); every region reads at least one block of each neighbouring index that exists. For each template the 15 interior edges rise strictly; the first bin starts at frequency 0 and the last ends at 2048.
All inputs are finite; a program needn't handle non-finite values.
Results may differ from the reference program's by a relative error of at most 0.008.
Values may be sent and summed in bfloat16 or wider, within the bound.
A program may use at most 128 MiB of HBM per device.

```python
import math
import jax
import jax.numpy as jnp
from jax import lax

FREQ_DEV = 512
TRIG_DEV = 32
BLOCK_TPL = 16
BLOCKS_DEV = 4
READS = 4
BINS = 16
LAGS = 16
NFREQ = 2048
REGIONS = 4
TRIGGERS = 128
CAP = 24
TPL = 64
TEMPLATES = 256
N_SEG = 4


def draw_region_of(key, part):
    key_hot, key_perm, key_mix = jax.random.split(key, 3)
    hottest = jax.random.randint(key_hot, (), 0, REGIONS)
    place = jnp.arange(TRIG_DEV, dtype=jnp.int32)[None, :]
    score = jax.random.randint(key_perm, (REGIONS, REGIONS - 1), 0, 4096) * (REGIONS - 1) + jnp.arange(REGIONS - 1, dtype=jnp.int32)[None, :]
    others = jnp.argsort(score, axis=1).astype(jnp.int32)
    others = jnp.mod(hottest + 1 + others, REGIONS)
    position = jnp.broadcast_to(jnp.mod(place - CAP, REGIONS - 1), (REGIONS, TRIG_DEV))
    picked = jnp.take_along_axis(others, position, axis=1)
    chosen = jnp.where(place < CAP, hottest, picked)
    mixing = jax.random.randint(key_mix, (REGIONS, TRIG_DEV), 0, 4096) * TRIG_DEV + place
    order = jnp.argsort(mixing, axis=1)
    return jnp.take_along_axis(chosen, order, axis=1).reshape(TRIGGERS).astype(jnp.int32)


def draw_templates(key, part):
    key_row, key_col, key_val = jax.random.split(key, 3)
    row_scale = jnp.exp(jax.random.uniform(key_row, (TEMPLATES, 1, 1), jnp.float32, math.log(0.3), math.log(3.0)))
    col_scale = jnp.exp(jax.random.uniform(key_col, (1, 1, NFREQ), jnp.float32, math.log(0.3), math.log(3.0)))
    position = jnp.arange(NFREQ, dtype=jnp.float32)[None, None, :] / NFREQ
    values = jnp.clip(jax.random.normal(key_val, (TEMPLATES, 2, NFREQ), jnp.float32), -4.0, 4.0)
    profile = 0.5 + position
    return (row_scale * col_scale * profile * values).astype(jnp.bfloat16)


def draw_reads(key, part):
    key_step, key_inner, key_order = jax.random.split(key, 3)
    region = jnp.arange(REGIONS, dtype=jnp.int32)[:, None]
    column = jnp.arange(READS, dtype=jnp.int32)[None, :]
    offset = jax.random.randint(key_step, (REGIONS, READS), -1, 2)
    offset = jnp.where(column == 0, -1, jnp.where(column == 1, 1, offset))
    holder = jnp.clip(region + offset, 0, REGIONS - 1)
    inner = jax.random.randint(key_inner, (REGIONS, READS), 0, BLOCKS_DEV)
    block_ids = holder * BLOCKS_DEV + inner
    score = jax.random.randint(key_order, (REGIONS, READS), 0, 1024) * READS + column
    order = jnp.argsort(score, axis=1)
    return jnp.take_along_axis(block_ids, order, axis=1).astype(jnp.int32)


def draw_edges(key, part):
    key_wide, key_jitter = jax.random.split(key, 2)
    narrow_width = NFREQ // (2 * BINS)
    jitter_reach = narrow_width // 4
    template_row = jnp.arange(TEMPLATES, dtype=jnp.int32)[:, None]
    bin_column = jnp.arange(BINS, dtype=jnp.int32)[None, :]
    wide_at = jax.random.randint(key_wide, (TEMPLATES, 1), 0, BINS)
    wide_at = jnp.where(template_row == 0, BINS - 1, jnp.where(template_row == 1, 0, wide_at))
    jitter = jax.random.randint(key_jitter, (TEMPLATES, BINS), -jitter_reach, jitter_reach + 1)
    jitter = jnp.where((template_row == 0) & (bin_column == 0), -jitter_reach, jitter)
    jitter = jnp.where((template_row == 1) & (bin_column == BINS - 1), -jitter_reach, jitter)
    is_wide = bin_column == wide_at
    widths = jnp.where(is_wide, 0, narrow_width + jitter).astype(jnp.int32)
    remaining = NFREQ - jnp.sum(widths, axis=1, keepdims=True)
    widths = jnp.where(is_wide, remaining, widths).astype(jnp.int32)
    bounds_out = jnp.cumsum(widths, axis=1)[:, :BINS - 1]
    return bounds_out.astype(jnp.int32)


def shard_levels(key, shape, shards, low, largest):
    gain = 1.0
    for dim, shards_of in shards:
        steps = jax.random.uniform(jax.random.fold_in(jax.random.fold_in(key, 6), dim), (shards_of,), jnp.float32, low / len(shards), largest / len(shards))
        gain = gain * jnp.repeat(jnp.exp(steps), shape[dim] // shards_of).reshape((-1,) + (1,) * (len(shape) - 1 - dim))
    return gain


def noise(stream_key, dims, deviation, bound, cuts=(), held_as=jnp.bfloat16):
    drawn = deviation * jax.random.normal(stream_key, dims, jnp.float32)
    if cuts:
        drawn = drawn * shard_levels(stream_key, dims, cuts, -0.22, 0.18)
    return jnp.clip(drawn, -bound, bound).astype(held_as)


def setup_inputs(seed: int = 0, part: int = 0) -> dict:
    arg_keys = jax.random.split(jax.random.key(seed), 6)
    part_keys = jax.random.split(jax.random.fold_in(arg_keys[5], part), 6)
    return {
        "strain": noise(part_keys[0], (TRIGGERS, 2, 2, NFREQ), 0.5, 3.0, ((0, 4), (3, 4))),
        "region_of": draw_region_of(jax.random.fold_in(jax.random.fold_in(arg_keys[5], part), 71), part),
        "templates": draw_templates(jax.random.fold_in(arg_keys[5], 71), part),
        "reads": draw_reads(jax.random.fold_in(arg_keys[5], 71), part),
        "edges": draw_edges(jax.random.fold_in(arg_keys[5], 71), part),
    }


def phase_table(freq_first, count, period):
    freq_idx = freq_first + jnp.arange(count, dtype=jnp.int32)
    lag_shift = jnp.arange(LAGS, dtype=jnp.int32) - LAGS // 2
    turns = jnp.mod(lag_shift[:, None] * freq_idx[None, :], period)
    phase_angle = turns.astype(jnp.float32) * (2.0 * math.pi / period)
    return jnp.cos(phase_angle), jnp.sin(phase_angle)


def phased(records, cosine_tab, sine_tab):
    real_part = records[:, :, 0, None, :].astype(jnp.float32)
    imag_part = records[:, :, 1, None, :].astype(jnp.float32)
    rot_real = real_part * cosine_tab - imag_part * sine_tab
    rot_imag = real_part * sine_tab + imag_part * cosine_tab
    return jnp.concatenate([rot_real, rot_imag], axis=-1).astype(jnp.bfloat16)


def bin_of_freq(bounds, freq_first, count):
    freq_idx = freq_first + jnp.arange(count, dtype=jnp.int32)
    bin_of = jnp.zeros((bounds.shape[0], count), jnp.int32)
    for level in range(BINS - 1):
        bin_of = bin_of + (freq_idx[None, :] >= bounds[:, level:level + 1]).astype(jnp.int32)
    return bin_of


def bin_power(region_tpl, bounds, freq_first):
    bin_of = bin_of_freq(bounds, freq_first, region_tpl.shape[-1])
    real_part = region_tpl[:, 0, :].astype(jnp.float32)
    imag_part = region_tpl[:, 1, :].astype(jnp.float32)
    squares = real_part * real_part + imag_part * imag_part
    return jnp.stack([jnp.sum(jnp.where(bin_of == level, squares, 0.0), axis=1) for level in range(BINS)], axis=1)


def template_matrix(region_tpl, bounds, freq_first):
    width = region_tpl.shape[-1]
    bin_of = bin_of_freq(bounds, freq_first, width)
    member = bin_of[:, None, :] == jnp.arange(BINS, dtype=jnp.int32)[None, :, None]
    nothing = jnp.zeros((), region_tpl.dtype)
    real_part = jnp.where(member, region_tpl[:, 0:1, :], nothing).reshape(-1, width)
    imag_part = jnp.where(member, region_tpl[:, 1:2, :], nothing).reshape(-1, width)
    upper_rows = jnp.concatenate([real_part, imag_part], axis=1)
    lower_rows = jnp.concatenate([-imag_part, real_part], axis=1)
    return jnp.concatenate([upper_rows, lower_rows], axis=0)


def statistics(totals, powers):
    columns = totals.shape[-1] // 2
    leading = totals.shape[:-1]
    real_part = totals[..., :columns].reshape(leading + (TPL, BINS))
    imag_part = totals[..., columns:].reshape(leading + (TPL, BINS))
    weight = powers[:, None, None, :, :] + 1e-6
    norm_sq = jnp.sum(weight, axis=-1)
    full_re = jnp.sum(real_part, axis=-1)
    full_im = jnp.sum(imag_part, axis=-1)
    signal = jnp.sum((full_re * full_re + full_im * full_im) / norm_sq, axis=1)
    expected = weight / norm_sq[..., None]
    diff_re = real_part - expected * full_re[..., None]
    diff_im = imag_part - expected * full_im[..., None]
    chi_terms = jnp.sum(jnp.sum((diff_re * diff_re + diff_im * diff_im) / weight, axis=-1), axis=1) / (2 * BINS - 2)
    return signal, chi_terms


def reference(strain, region_of, templates, reads, edges):
    blocks = templates.reshape(-1, BLOCK_TPL, 2, NFREQ)
    bound_blocks = edges.reshape(-1, BLOCK_TPL, BINS - 1)
    tables = [phase_table(slice_at * FREQ_DEV, FREQ_DEV, 2 * NFREQ) for slice_at in range(N_SEG)]

    def region_parts(block_ids):
        region_tpl = jnp.take(blocks, block_ids, axis=0).reshape(TPL, 2, NFREQ)
        bounds = jnp.take(bound_blocks, block_ids, axis=0).reshape(TPL, BINS - 1)
        stacked = jnp.stack([template_matrix(region_tpl[:, :, slice_at * FREQ_DEV:(slice_at + 1) * FREQ_DEV], bounds, slice_at * FREQ_DEV) for slice_at in range(N_SEG)])
        return stacked.astype(jnp.float32), bin_power(region_tpl, bounds, 0)

    matrices, powers = lax.map(region_parts, reads)

    def one_record(record_pair):
        record, region = record_pair
        own_mats = matrices[region]
        totals = jnp.zeros((2 * LAGS, 2 * TPL * BINS), jnp.float32)
        for slice_at in range(N_SEG):
            cosine_tab, sine_tab = tables[slice_at]
            rotated = phased(record[None, :, :, slice_at * FREQ_DEV:(slice_at + 1) * FREQ_DEV], cosine_tab, sine_tab)
            flat_rows = rotated.reshape(2 * LAGS, -1).astype(jnp.float32)
            partial_value = jnp.dot(flat_rows, own_mats[slice_at].T, preferred_element_type=jnp.float32, precision=lax.Precision.HIGHEST)
            rounded = lax.optimization_barrier(partial_value.astype(jnp.bfloat16))
            totals = totals + rounded.astype(jnp.float32)
        signal, chi_terms = statistics(totals.reshape(1, 2, LAGS, -1), powers[region][None])
        return signal[0], chi_terms[0]

    signal, chi_terms = lax.map(one_record, (strain, region_of))
    return (jnp.transpose(signal, (1, 2, 0)), jnp.transpose(chi_terms, (1, 2, 0)))
```

```python
import functools
import math

import jax
import jax.numpy as jnp
import numpy as np
from jax import lax
from jax.experimental import pallas as pl
from jax.experimental.pallas import tpu as pltpu
from jax.sharding import PartitionSpec as P

BLOCK_TPL = 16
BINS = 16
LAGS = 16
TPL = 64
CHUNK = 128
SLOTS = 4
F32 = jnp.float32
BF16 = jnp.bfloat16
NT = (((1,), (1,)), ((), ()))
TN = (((0,), (0,)), ((), ()))
HIGH = lax.Precision.HIGHEST


def round_up(value, step):
    return -(-value // step) * step


def phase_tables(seg_count, nfreq):
    period = 2 * nfreq
    lag = np.arange(LAGS, dtype=np.int64) - LAGS // 2
    turns = np.mod(lag[:, None] * np.arange(nfreq, dtype=np.int64)[None, :], period)
    angle = turns * (2.0 * math.pi / period)
    shape = (seg_count, LAGS // seg_count, nfreq)
    return (
        jnp.asarray(np.cos(angle).reshape(shape), F32),
        jnp.asarray(np.sin(angle).reshape(shape), F32),
    )


def exchange_kernel(
    cap, rec, hot_pad, rest_pad,
    planes_ref, strain_ref, reg_hbm, edges_hbm, cos_ref, sin_ref,
    tpl_all, power_all, code_ref, count_ref, hot_lhs, rest_lhs, hot_sel, rest_sel, rest_reg, scalars,
    strain_all, power_own, bounds_ref, cos_own, sin_own, reg_ref, edges_ref,
    tpl_send, tpl_recv, pow_send, pow_recv, str_send, str_recv, local_sem,
):
    banks, segs = tpl_all.shape[:2]
    grp, bank, seg = lax.axis_index("grp"), lax.axis_index("bank"), lax.axis_index("seg")
    rows, width = planes_ref.shape[1:]
    nfreq = segs * width
    lags = cos_own.shape[0]
    mesh_id = pl.DeviceIdType.MESH
    half = segs // 2
    far = lax.rem(seg + half, segs)
    near = seg + 1 - 2 * lax.rem(seg, 2)
    far_near = lax.rem(near + half, segs)
    mine, other = grp, 1 - grp
    to_far, to_near, to_twin = {"seg": far}, {"seg": near}, {"grp": other}

    small = [
        pltpu.make_async_copy(cos_ref.at[seg], cos_own, local_sem.at[3]),
        pltpu.make_async_copy(sin_ref.at[seg], sin_own, local_sem.at[4]),
        pltpu.make_async_copy(edges_hbm, edges_ref, local_sem.at[5]),
        pltpu.make_async_copy(reg_hbm, reg_ref, local_sem.at[6]),
    ]
    for copy in small:
        copy.start()
    barrier = pltpu.get_barrier_semaphore()
    for off in range(1, banks):
        pl.semaphore_signal(
            barrier, inc=1, device_id={"bank": lax.rem(bank + off, banks)}, device_id_type=mesh_id
        )
    for where in (to_far, to_near, to_twin):
        pl.semaphore_signal(barrier, inc=1, device_id=where, device_id_type=mesh_id)
    pl.semaphore_wait(barrier, banks + 2)

    started = []

    def push(src, dst, send, recv, where):
        copy = pltpu.make_async_remote_copy(
            src_ref=src, dst_ref=dst, send_sem=send, recv_sem=recv,
            device_id=where, device_id_type=mesh_id,
        )
        copy.start()
        started.append(copy)

    def landed(slot, recv):
        pltpu.make_async_remote_copy(
            src_ref=slot, dst_ref=slot, send_sem=recv, recv_sem=recv,
            device_id=to_near, device_id_type=mesh_id,
        ).wait_recv()

    def source(off):
        return lax.rem(bank - off + banks, banks)

    Z, X, Y_OWN, Y_FAR, N_MINE, N_OTHER, N_FAR_MINE, N_FAR_OTHER = range(8)
    holds = {
        Z: (seg, mine), X: (far, mine), Y_OWN: (seg, other), Y_FAR: (far, other),
        N_MINE: (near, mine), N_OTHER: (near, other),
        N_FAR_MINE: (far_near, mine), N_FAR_OTHER: (far_near, other),
    }
    relays = {
        Z: ((X, to_far), (Y_OWN, to_twin), (N_MINE, to_near)),
        X: ((Y_FAR, to_twin), (N_FAR_MINE, to_near)),
        Y_OWN: ((N_OTHER, to_near),),
        Y_FAR: ((N_FAR_OTHER, to_near),),
    }

    def relay(kind, off):
        place, plane = holds[kind]
        slot = tpl_all.at[source(off), place, plane]
        landed(slot, tpl_recv.at[kind, off])
        for way, where in relays.get(kind, ()):
            push(slot, slot, tpl_send.at[way, off], tpl_recv.at[way, off], where)

    P_Z, P_X, P_N, P_FAR_N = range(4)
    pow_holds = {P_Z: seg, P_X: far, P_N: near, P_FAR_N: far_near}
    pow_relays = {P_Z: ((P_X, to_far), (P_N, to_near)), P_X: ((P_FAR_N, to_near),)}

    def pow_relay(kind, off):
        slot = power_all.at[source(off), pow_holds[kind]]
        landed(slot, pow_recv.at[kind, off])
        for way, where in pow_relays.get(kind, ()):
            push(slot, slot, pow_send.at[way, off], pow_recv.at[way, off], where)

    own_plane = planes_ref.at[mine]
    own_slot = tpl_all.at[bank, seg, mine]
    for off in range(1, banks):
        push(
            own_plane, own_slot, tpl_send.at[Z, off], tpl_recv.at[Z, off],
            {"bank": lax.rem(bank + off, banks)},
        )
    push(own_plane, own_slot, tpl_send.at[X, 0], tpl_recv.at[X, 0], to_far)
    own_strain = strain_all.at[0, seg]
    push(strain_ref, own_strain, str_send.at[0], str_recv.at[0], to_far)
    push(strain_ref, own_strain, str_send.at[1], str_recv.at[1], to_near)
    push(own_plane, own_slot, tpl_send.at[N_MINE, 0], tpl_recv.at[N_MINE, 0], to_near)
    push(
        planes_ref.at[other], tpl_all.at[bank, seg, other],
        tpl_send.at[N_OTHER, 0], tpl_recv.at[N_OTHER, 0], to_near,
    )
    own_copies = [
        pltpu.make_async_copy(planes_ref, tpl_all.at[bank, seg], local_sem.at[0]),
        pltpu.make_async_copy(strain_ref, own_strain, local_sem.at[1]),
    ]
    for copy in own_copies:
        copy.start()
    for copy in small:
        copy.wait()

    total_rows = edges_ref.shape[1]
    eye = jnp.where(
        lax.broadcasted_iota(jnp.int32, (128, 128), 0) == lax.broadcasted_iota(jnp.int32, (128, 128), 1),
        1.0, 0.0,
    )
    for first in range(0, total_rows, 128):
        bounds_ref[first : first + 128, :] = lax.dot_general(
            eye, edges_ref[:, first : first + 128].astype(F32), NT,
            precision=HIGH, preferred_element_type=F32,
        )

    def bin_index(bounds, first):
        freq = (
            lax.broadcasted_iota(jnp.int32, (bounds.shape[0], width), 1) + first
        ).astype(F32)
        bin_of = jnp.zeros((bounds.shape[0], width), F32)
        for level in range(BINS - 1):
            bin_of = jnp.where(freq >= bounds[:, level : level + 1], level + 1.0, bin_of)
        return bin_of

    bin_of = bin_index(bounds_ref[pl.ds(pl.multiple_of(bank * rows, 8), rows), :], seg * width)
    real_part = planes_ref[0].astype(F32)
    imag_part = planes_ref[1].astype(F32)
    squares = real_part * real_part + imag_part * imag_part
    ones = jnp.ones((8, width), F32)
    for pair in range(BINS // 2):
        picked = jnp.concatenate(
            [jnp.where(bin_of == float(2 * pair + p), squares, 0.0) for p in range(2)], axis=0
        )
        line = lax.dot_general(ones, picked, NT, precision=HIGH, preferred_element_type=F32)
        power_own[pair : pair + 1, :] = line[0:1, :]
    own_power = pltpu.make_async_copy(power_own, power_all.at[bank, seg], local_sem.at[2])
    own_power.start()
    for off in range(1, banks):
        push(
            power_own, power_all.at[bank, seg], pow_send.at[P_Z, off], pow_recv.at[P_Z, off],
            {"bank": lax.rem(bank + off, banks)},
        )
    push(power_own, power_all.at[bank, seg], pow_send.at[P_X, 0], pow_recv.at[P_X, 0], to_far)
    push(power_own, power_all.at[bank, seg], pow_send.at[P_N, 0], pow_recv.at[P_N, 0], to_near)

    def fill_codes(first, last):
        def one(step, carry):
            at = pl.multiple_of(step * BLOCK_TPL, BLOCK_TPL)
            bounds = bounds_ref[pl.ds(at, BLOCK_TPL), :]
            for s in range(segs):
                bin_of = bin_index(bounds, s * width)
                slot = bin_of - SLOTS * jnp.floor(bin_of * (1.0 / SLOTS))
                for c in range(width // CHUNK):
                    here = slice(c * CHUNK, (c + 1) * CHUNK)
                    past = bin_of[:, here] - bin_of[:, c * CHUNK : c * CHUNK + 1]
                    code = slot[:, here] + SLOTS * jnp.floor(past * (1.0 / SLOTS))
                    code_ref[
                        pl.ds(at, BLOCK_TPL), s * width + c * CHUNK : s * width + (c + 1) * CHUNK
                    ] = code.astype(BF16)
            return carry

        lax.fori_loop(first, last, one, 0)

    chunks = nfreq // CHUNK
    row = lax.broadcasted_iota(jnp.int32, (2 * chunks, 2 * TPL), 0)
    mark = jnp.where(row < chunks, row, row - chunks + 1) * CHUNK
    low_lane = lax.broadcasted_iota(jnp.int32, (2 * chunks, 2 * TPL), 1) < TPL
    most = jnp.zeros((chunks, 2 * TPL), F32)
    for pair in range(total_rows // (2 * TPL)):
        count = jnp.zeros((2 * chunks, 2 * TPL), F32)
        for level in range(BINS - 1):
            edge = edges_ref[level : level + 1, pair * 2 * TPL : (pair + 1) * 2 * TPL]
            count = count + jnp.where(edge <= mark, 1.0, 0.0)
        most = jnp.maximum(most, count[chunks:] - count[:chunks])
        count = jnp.where(row == 2 * chunks - 1, float(BINS), count)
        moved = pltpu.roll(count, TPL, 1)
        count_ref[2 * pair] = jnp.where(low_lane, count, moved)
        count_ref[2 * pair + 1] = jnp.where(low_lane, moved, count)
    scalars[1] = jnp.max(most.astype(jnp.int32)) // SLOTS + 1

    blocks = total_rows // BLOCK_TPL
    for off in range(banks):
        if off:
            relay(Z, off)
            relay(X, off - 1)
        if off == 1:
            landed(strain_all.at[0, far], str_recv.at[0])
            push(
                strain_all.at[0, far], strain_all.at[0, far], str_send.at[2], str_recv.at[2], to_near
            )
        if off > 1:
            relay(Y_OWN, off - 1)
            relay(Y_FAR, off - 2)
        fill_codes(off * blocks // banks, (off + 1) * blocks // banks)
    relay(X, banks - 1)
    relay(Y_OWN, banks - 1)
    relay(Y_FAR, banks - 2)
    for off in range(1, banks):
        pow_relay(P_Z, off)
    landed(strain_all.at[0, near], str_recv.at[1])
    landed(strain_all.at[0, far_near], str_recv.at[2])
    own_copies[1].wait()

    row_idx = lax.broadcasted_iota(jnp.int32, (rec, rec), 0)
    col_idx = lax.broadcasted_iota(jnp.int32, (rec, rec), 1)
    reg_row = reg_ref[0:1, :]
    reg_col = jnp.sum(jnp.where(row_idx == col_idx, reg_row, 0), axis=1, keepdims=True)
    count_row = jnp.sum(jnp.where(reg_col == reg_row, 1, 0), axis=0, keepdims=True)
    hot = jnp.min(jnp.where(count_row >= cap, reg_row, 1 << 20), axis=1, keepdims=True)
    is_hot_col = jnp.where(reg_col == hot, 1, 0)
    is_hot_row = jnp.where(reg_row == hot, 1, 0)
    rank_row = jnp.sum(jnp.where(row_idx < col_idx, is_hot_col, 0), axis=0, keepdims=True)
    rest_row = col_idx[0:1, :] - rank_row
    scalars[0] = jnp.min(jnp.where(count_row >= cap, reg_row, 1 << 20))
    hot_pick = jnp.where(
        (lax.broadcasted_iota(jnp.int32, (hot_pad, rec), 0) == rank_row) & (is_hot_row == 1), 1, 0
    )
    rest_pick = jnp.where(
        (lax.broadcasted_iota(jnp.int32, (rest_pad, rec), 0) == rest_row) & (is_hot_row == 0), 1, 0
    )
    hot_sel[...] = hot_pick.astype(F32)
    rest_sel[...] = rest_pick.astype(F32)
    rest_reg[...] = jnp.broadcast_to(
        jnp.sum(rest_pick * (reg_row + 1), axis=1, keepdims=True) - 1, rest_reg.shape
    )
    lists = ((hot_pick, hot_lhs, hot_pad), (rest_pick, rest_lhs, rest_pad))
    for s in range(segs):
        if s == segs // 2:
            relay(Y_FAR, banks - 1)
            for off in range(banks):
                pow_relay(P_X, off)
        for pick, lhs_ref, pad in lists:
            sel = pick.astype(F32).astype(BF16)
            at = slice(s * width, (s + 1) * width)
            parts = []
            for c in range(2):
                parts.append(
                    jnp.concatenate(
                        [
                            jnp.dot(
                                sel,
                                strain_all[0, s, c, d * rec : (d + 1) * rec, :],
                                preferred_element_type=F32,
                            )
                            for d in range(2)
                        ],
                        axis=0,
                    )
                )
            real_part, imag_part = parts
            for lag in range(lags):
                cosine = cos_own[lag : lag + 1, at]
                sine = sin_own[lag : lag + 1, at]
                rot_re = (real_part * cosine - imag_part * sine).astype(BF16)
                rot_im = (real_part * sine + imag_part * cosine).astype(BF16)
                top = (2 * lag) * 2 * pad
                low = (2 * lag + 1) * 2 * pad
                for c in range(width // CHUNK):
                    here = slice(c * CHUNK, (c + 1) * CHUNK)
                    base = (s * width // CHUNK + c) * 2 * CHUNK
                    re_at, im_at = slice(base, base + CHUNK), slice(base + CHUNK, base + 2 * CHUNK)
                    lhs_ref[top : top + 2 * pad, re_at] = rot_re[:, here]
                    lhs_ref[top : top + 2 * pad, im_at] = rot_im[:, here]
                    lhs_ref[low : low + 2 * pad, re_at] = rot_im[:, here]
                    lhs_ref[low : low + 2 * pad, im_at] = -rot_re[:, here]
    for off in range(banks):
        for kind in (N_MINE, N_OTHER, N_FAR_MINE, N_FAR_OTHER):
            relay(kind, off)
        for kind in (P_N, P_FAR_N):
            pow_relay(kind, off)
    own_copies[0].wait()
    own_power.wait()
    for copy in started:
        copy.wait_send()


def follow_kernel(
    held_blocks,
    reads_ref, scalars_ref, hot_lhs, rest_lhs, hot_sel, rest_sel, rest_reg,
    tpl_ref, code_ref, power_ref, count_ref,
    snr_ref, chi_ref,
    close_ref, acc_ref, sum_ref, total_ref, hot_stat, rest_stat,
):
    regions = reads_ref.shape[0]
    segs, width = tpl_ref.shape[1], tpl_ref.shape[4]
    chunks = segs * width // CHUNK
    lags = snr_ref.shape[0]
    hot_pad, rest_pad = hot_sel.shape[0], rest_sel.shape[0]
    lane8 = lax.broadcasted_iota(jnp.int32, (8, 2 * TPL), 1)
    lane_c = lax.broadcasted_iota(jnp.int32, (2 * chunks, 2 * TPL), 1)
    upper = jnp.where(lax.broadcasted_iota(jnp.int32, (chunks, 2 * TPL), 1) < TPL, 0.0, 1.0)
    zero = jnp.zeros((), BF16)

    def blocks_of(region):
        ids = [reads_ref[region, i] for i in range(4)]
        return [(b // held_blocks, b % held_blocks, b) for b in ids]

    def region_tables(region, groups):
        weight = jnp.zeros((8, 2 * TPL), F32)
        count = jnp.zeros((2 * chunks, 2 * TPL), F32)
        for i, (bank, inner, _) in enumerate(blocks_of(region)):
            total = power_ref[bank, 0]
            for s in range(1, segs):
                total = total + power_ref[bank, s]
            shift = (i - inner + 2 * held_blocks) * BLOCK_TPL % (2 * TPL)
            weight = jnp.where(
                (lane8 % TPL) // BLOCK_TPL == i, pltpu.roll(total, shift, 1), weight
            )
            count = jnp.where(
                (lane_c % TPL) // BLOCK_TPL == i, pltpu.roll(count_ref[bank], shift, 1), count
            )
        weight = weight + 1e-06
        norm = jnp.sum(weight, axis=0, keepdims=True)
        inv_norm = 1.0 / (norm + pltpu.roll(norm, TPL, 1))
        inv_weight = 1.0 / weight
        for g in range(groups):
            first = count[:chunks] + float(SLOTS * g)
            last = jnp.minimum(count[chunks:], first + float(SLOTS))
            for a in range(2):
                close = jnp.zeros((chunks, 2 * TPL), F32)
                for m in range(BINS // SLOTS):
                    level = upper + float(SLOTS * m + 2 * a)
                    close = jnp.where(
                        (level >= first) & (level < last),
                        inv_weight[2 * m + a : 2 * m + a + 1], close,
                    )
                close_ref[2 * g + a] = close
        return inv_norm

    def matrix(blocks, s, at, code_at, g):
        code = jnp.concatenate(
            [code_ref[pl.ds(pl.multiple_of(b * BLOCK_TPL, BLOCK_TPL), BLOCK_TPL), code_at] for _, _, b in blocks], axis=0
        )
        planes = [
            jnp.concatenate(
                [tpl_ref[bank, s, c, pl.ds(pl.multiple_of(inner * BLOCK_TPL, BLOCK_TPL), BLOCK_TPL), at] for bank, inner, _ in blocks],
                axis=0,
            )
            for c in range(2)
        ]
        rows = []
        for slot in range(SLOTS):
            inside = code == (g * SLOTS + slot).astype(BF16) if not isinstance(g, int) else code == jnp.asarray(g * SLOTS + slot, BF16)
            rows.append(jnp.concatenate([jnp.where(inside, plane, zero) for plane in planes], axis=1))
        return jnp.concatenate(rows, axis=0)

    def step(lhs, close, rows, mat, first):
        part = lax.dot_general(lhs, mat, NT, preferred_element_type=F32)
        both = part[:, : 2 * TPL] + part[:, 2 * TPL :]
        total_ref[:rows] = both if first else total_ref[:rows] + both
        for a in range(2):
            here = part[:, a * 2 * TPL : (a + 1) * 2 * TPL]
            if not first:
                here = here + acc_ref[a, :rows]
            term = here * here * close[a]
            sum_here = term if first else sum_ref[a, :rows] + term
            sum_ref[a, :rows] = sum_here
            acc_ref[a, :rows] = jnp.where(close[a] > 0.0, 0.0, here)

    def run_fast(blocks, lhs_ref, rows):
        for c in range(chunks):
            s, q = c // (width // CHUNK), c % (width // CHUNK)
            mat = matrix(
                blocks, s, slice(q * CHUNK, (q + 1) * CHUNK), slice(c * CHUNK, (c + 1) * CHUNK), 0
            )
            close = [close_ref[a, c : c + 1, :] for a in range(2)]
            step(lhs_ref[:, c * 2 * CHUNK : (c + 1) * 2 * CHUNK], close, rows, mat, c == 0)

    def run_any(blocks, lhs_ref, rows, groups):
        total_ref[:rows] = jnp.zeros((rows, 2 * TPL), F32)
        for a in range(2):
            acc_ref[a, :rows] = jnp.zeros((rows, 2 * TPL), F32)
            sum_ref[a, :rows] = jnp.zeros((rows, 2 * TPL), F32)

        def one_chunk(c, carry):
            s, q = c // (width // CHUNK), c % (width // CHUNK)
            at = pl.ds(pl.multiple_of(q * CHUNK, CHUNK), CHUNK)
            code_at = pl.ds(pl.multiple_of(c * CHUNK, CHUNK), CHUNK)
            lhs_at = pl.ds(pl.multiple_of(c * 2 * CHUNK, 2 * CHUNK), 2 * CHUNK)

            def one_group(g, carry):
                mat = matrix(blocks, s, at, code_at, g)
                close = [close_ref[2 * g + a, pl.ds(c, 1), :] for a in range(2)]
                step(lhs_ref[:, lhs_at], close, rows, mat, False)
                return carry

            return lax.fori_loop(0, groups, one_group, carry)

        lax.fori_loop(0, chunks, one_chunk, 0)

    def run(region, lhs_ref, pad, store):
        rows = lhs_ref.shape[0]
        blocks = blocks_of(region)
        inv_norm = region_tables(region, BINS // SLOTS)

        @pl.when(scalars_ref[1] == 1)
        def fast():
            run_fast(blocks, lhs_ref, rows)

        @pl.when(scalars_ref[1] != 1)
        def general():
            run_any(blocks, lhs_ref, rows, scalars_ref[1])

        for lag in range(lags):
            top = lag * 4 * pad
            full = total_ref[top : top + 4 * pad]
            full = full + pltpu.roll(full, TPL, 1)
            energy = sum_ref[0, top : top + 4 * pad] + sum_ref[1, top : top + 4 * pad]
            signal = full * full * inv_norm
            signal = (signal[:pad] + signal[pad : 2 * pad]) + (signal[2 * pad : 3 * pad] + signal[3 * pad :])
            energy = (energy[:pad] + energy[pad : 2 * pad]) + (energy[2 * pad : 3 * pad] + energy[3 * pad :])
            energy = energy + pltpu.roll(energy, TPL, 1)
            store(lag, signal)
            store(lags + lag, (energy - signal) * (1.0 / (2 * BINS - 2)))

    def store_hot(at, value):
        hot_stat[at] = value

    rest_stat[...] = jnp.zeros_like(rest_stat)
    hot = scalars_ref[0]
    run(hot, hot_lhs, hot_pad, store_hot)

    def other(i, carry):
        region = lax.rem(hot + i, regions)

        def store_rest(at, value):
            rest_stat[at] = jnp.where(rest_reg[...] == region, value, rest_stat[at])

        run(region, rest_lhs, rest_pad, store_rest)
        return carry

    lax.fori_loop(1, regions, other, 0)

    for which, out_ref in enumerate((snr_ref, chi_ref)):
        for lag in range(lags):
            at = which * lags + lag
            value = lax.dot_general(
                hot_sel[...], hot_stat[at], TN, precision=HIGH, preferred_element_type=F32
            ) + lax.dot_general(
                rest_sel[...], rest_stat[at], TN, precision=HIGH, preferred_element_type=F32
            )
            out_ref[lag] = value[:, :TPL]


def per_device(strain, region_of, templates, reads, edges):
    region_count = lax.axis_size("bank")
    seg_count = lax.axis_size("seg")
    rec, _, _, width = strain.shape
    nfreq = width * seg_count
    held_rows = templates.shape[0]
    held_blocks = held_rows // BLOCK_TPL
    cap = 3 * rec // region_count
    hot_pad, rest_pad = round_up(cap, 8), round_up(rec - cap, 8)
    lags = LAGS // seg_count
    planes = jnp.transpose(templates, (1, 0, 2))
    strain_planes = jnp.transpose(strain, (2, 1, 0, 3)).reshape(2, 2 * rec, width)
    cos_tab, sin_tab = phase_tables(seg_count, nfreq)
    reg = region_of.reshape(1, rec)
    rows_hot, rows_rest = lags * 4 * hot_pad, lags * 4 * rest_pad
    vmem = pl.BlockSpec(memory_space=pltpu.VMEM)
    anyw = pl.BlockSpec(memory_space=pl.ANY)
    hbm = pl.BlockSpec(memory_space=pltpu.HBM)
    smem = pl.BlockSpec(memory_space=pltpu.SMEM)
    total_rows = edges.shape[0]

    def struct(shape, dtype):
        return jax.ShapeDtypeStruct(shape, dtype)

    dma = pltpu.SemaphoreType.DMA
    exchanged = pl.pallas_call(
        functools.partial(exchange_kernel, cap, rec, hot_pad, rest_pad),
        out_shape=(
            struct((region_count, seg_count) + planes.shape, BF16),
            struct((region_count, seg_count, BINS // 2, 2 * TPL), F32),
            struct((total_rows, nfreq), BF16),
            struct((region_count, 2 * nfreq // CHUNK, 2 * TPL), F32),
            struct((rows_hot, 2 * nfreq), BF16),
            struct((rows_rest, 2 * nfreq), BF16),
            struct((hot_pad, rec), F32),
            struct((rest_pad, rec), F32),
            struct((rest_pad, 2 * TPL), jnp.int32),
            struct((2,), jnp.int32),
        ),
        in_specs=[vmem, vmem, hbm, hbm, hbm, hbm],
        out_specs=(vmem,) * 9 + (smem,),
        scratch_shapes=[
            pltpu.VMEM((1, seg_count) + strain_planes.shape, BF16),
            pltpu.VMEM((BINS // 2, 2 * TPL), F32),
            pltpu.VMEM((total_rows, BINS - 1), F32),
            pltpu.VMEM((lags, nfreq), F32),
            pltpu.VMEM((lags, nfreq), F32),
            pltpu.VMEM((1, rec), jnp.int32),
            pltpu.VMEM((BINS - 1, total_rows), jnp.int32),
            dma((8, region_count)),
            dma((8, region_count)),
            dma((4, region_count)),
            dma((4, region_count)),
            dma((3,)),
            dma((3,)),
            dma((7,)),
        ],
        compiler_params=pltpu.CompilerParams(
            collective_id=0, has_side_effects=True, vmem_limit_bytes=24 * 1024 * 1024
        ),
        name="exchange",
    )(planes, strain_planes, reg, edges.T, cos_tab, sin_tab)
    tpl_all, power_all, code_all, count_all, *lists, scalars = exchanged
    out = struct((lags, rec, TPL), F32)
    rows_max = max(rows_hot, rows_rest)
    snr, chi = pl.pallas_call(
        functools.partial(follow_kernel, held_blocks),
        out_shape=(out, out),
        in_specs=[smem, smem] + [vmem] * 9,
        out_specs=(vmem, vmem),
        scratch_shapes=[
            pltpu.VMEM((2 * BINS // SLOTS, nfreq // CHUNK, 2 * TPL), F32),
            pltpu.VMEM((2, rows_max, 2 * TPL), F32),
            pltpu.VMEM((2, rows_max, 2 * TPL), F32),
            pltpu.VMEM((rows_max, 2 * TPL), F32),
            pltpu.VMEM((2 * lags, hot_pad, 2 * TPL), F32),
            pltpu.VMEM((2 * lags, rest_pad, 2 * TPL), F32),
        ],
        compiler_params=pltpu.CompilerParams(vmem_limit_bytes=24 * 1024 * 1024),
        name="follow",
    )(reads, scalars, *lists, tpl_all, code_all, power_all, count_all)
    return jnp.transpose(snr, (0, 2, 1)), jnp.transpose(chi, (0, 2, 1))


def solution(mesh):
    placed = (
        P(("grp", "bank"), None, None, "seg"),
        P(("grp", "bank")),
        P("bank", None, "seg"),
        P(),
        P(),
    )
    return jax.shard_map(
        per_device,
        mesh=mesh,
        in_specs=placed,
        out_specs=(P("seg", None, ("grp", "bank")), P("seg", None, ("grp", "bank"))),
        check_vma=False,
    )
```

```python
import functools
import math

import jax
import jax.numpy as jnp
import numpy as np
from jax import lax
from jax.experimental import pallas as pl
from jax.experimental.pallas import tpu as pltpu
from jax.sharding import PartitionSpec as P

BLOCK_TPL = 16
BINS = 16
LAGS = 16
TPL = 64
CHUNK = 128
SLOTS = 4
F32 = jnp.float32
BF16 = jnp.bfloat16
NT = (((1,), (1,)), ((), ()))
TN = (((0,), (0,)), ((), ()))
HIGH = lax.Precision.HIGHEST


def round_up(value, step):
    return -(-value // step) * step


def turn(lag, freq, period):
    quarter = period // 4
    moved = (freq * lag + quarter // 2) & (period - 1)
    quadrant = moved // quarter
    angle = (moved % quarter - quarter // 2).astype(F32) * (2.0 * math.pi / period)
    sq = angle * angle
    sine = angle * (1.0 + sq * (-1.0 / 6 + sq * (1.0 / 120 + sq * (-1.0 / 5040 + sq * (1.0 / 362880)))))
    cosine = 1.0 + sq * (-0.5 + sq * (1.0 / 24 + sq * (-1.0 / 720 + sq * (1.0 / 40320))))
    odd = quadrant % 2 == 1
    big, small = jnp.where(odd, sine, cosine), jnp.where(odd, cosine, sine)
    cos_out = jnp.where((quadrant == 1) | (quadrant == 2), -big, big)
    sin_out = jnp.where(quadrant >= 2, -small, small)
    return cos_out, sin_out


def follow_up_kernel(
    cap, rec, hot_pad, rest_pad, held_blocks,
    planes_ref, strain_ref, reg_hbm, edges_hbm, reads_hbm,
    snr_ref, chi_ref, most_ref,
    tpl_own, tpl_far, power_all, code_ref, bounds_ref, count_ref,
    hot_lhs, rest_lhs, hot_sel, rest_sel, rest_reg, hot_ref,
    strain_all, power_own, column_ref, cos_own, sin_own, picked_ref, reg_ref, edges_ref, reads_ref,
    hot_close, rest_close, hot_acc, hot_sum, hot_total, rest_acc, rest_sum, rest_total,
    hot_stat, rest_stat,
    tpl_send, tpl_recv, pow_send, pow_recv, str_send, str_recv, local_sem,
):
    banks, segs = power_all.shape[:2]
    grp, bank, seg = lax.axis_index("grp"), lax.axis_index("bank"), lax.axis_index("seg")
    width = planes_ref.shape[3]
    rows = held_blocks * BLOCK_TPL
    nfreq = segs * width
    lags = LAGS // segs
    mesh_id = pl.DeviceIdType.MESH
    half = segs // 2
    far = lax.rem(seg + half, segs)
    near = seg + 1 - 2 * lax.rem(seg, 2)
    far_near = lax.rem(near + half, segs)
    mine, other = grp, 1 - grp
    to_far, to_near, to_twin = {"seg": far}, {"seg": near}, {"grp": other}

    up_ok, down_ok = bank < banks - 1, bank > 0

    small = [
        pltpu.make_async_copy(edges_hbm, edges_ref, local_sem.at[3]),
        pltpu.make_async_copy(reg_hbm, reg_ref, local_sem.at[4]),
        pltpu.make_async_copy(reads_hbm, reads_ref, local_sem.at[5]),
    ]
    for copy in small:
        copy.start()
    barrier = pltpu.get_barrier_semaphore()

    def greet(where):
        pl.semaphore_signal(barrier, inc=1, device_id=where, device_id_type=mesh_id)

    for where in (to_far, to_near, to_twin):
        greet(where)
    pl.when(up_ok)(lambda: greet({"bank": bank + 1}))
    pl.when(down_ok)(lambda: greet({"bank": bank - 1}))
    met = 3 + lax.min(bank, 1) + lax.min(banks - 1 - bank, 1)
    started = []

    def push(describe, condition=None):
        def start():
            describe().start()

        def finish():
            describe().wait_send()

        if condition is None:
            start()
            started.append(finish)
        else:
            pl.when(condition)(start)
            started.append(lambda: pl.when(condition)(finish))

    def remote(src, dst, send, recv, where):
        return pltpu.make_async_remote_copy(
            src_ref=src, dst_ref=dst, send_sem=send, recv_sem=recv,
            device_id=where, device_id_type=mesh_id,
        )

    def landed(slot, recv):
        remote(slot, slot, recv, recv, to_near).wait_recv()

    def source(side, hops):
        return bank - hops if side == 0 else bank + hops

    def present(side, hops):
        return bank >= hops if side == 0 else bank + hops <= banks - 1

    def number(side, hops):
        return side * banks + hops

    def onward(side):
        return (up_ok, {"bank": bank + 1}) if side == 0 else (down_ok, {"bank": bank - 1})

    Z, X, X_OTHER, Y_OWN, Y_FAR, N_MINE, N_OTHER, N_FAR_MINE, N_FAR_OTHER = range(9)
    core, core_near = lax.rem(seg, half), lax.rem(near, half)
    holds = {
        Z: (tpl_own, core, mine), X: (tpl_far, core, mine), X_OTHER: (tpl_far, core, other),
        Y_OWN: (tpl_own, core, other), Y_FAR: (tpl_far, core, other),
        N_MINE: (tpl_own, core_near, mine), N_OTHER: (tpl_own, core_near, other),
        N_FAR_MINE: (tpl_far, core_near, mine), N_FAR_OTHER: (tpl_far, core_near, other),
    }
    relays = {
        Z: ((Y_OWN, to_twin), (X, to_far), (N_MINE, to_near)),
        X: ((Y_FAR, to_twin), (N_FAR_MINE, to_near)),
        X_OTHER: ((N_FAR_OTHER, to_near),),
        Y_OWN: ((N_OTHER, to_near),),
        Y_FAR: ((N_FAR_OTHER, to_near),),
    }
    P_Z, P_X, P_N, P_FAR_N = range(4)
    pow_holds = {P_Z: seg, P_X: far, P_N: near, P_FAR_N: far_near}
    pow_relays = {P_Z: ((P_X, to_far), (P_N, to_near)), P_X: ((P_FAR_N, to_near),)}

    def landing(way, kind, side, hops):
        ref, place, plane = holds[kind]
        if way in (X, X_OTHER):
            ref = tpl_far
        return ref.at[source(side, hops), place, plane]

    def tpl_slot(kind, side, hops):
        ref, place, plane = holds[kind]
        return ref.at[source(side, hops), place, plane]

    def pow_slot(kind, side, hops):
        return power_all.at[source(side, hops), pow_holds[kind]]

    def relay(kind, side=0, hops=0, table=(tpl_slot, tpl_send, tpl_recv, relays, Z)):
        slot, send, recv, ways, first = table
        at = number(side, hops)
        here = present(side, hops) if hops else None

        def wait():
            landed(slot(kind, side, hops), recv.at[kind, at])

        wait() if here is None else pl.when(here)(wait)
        if kind == first:
            more, where = onward(side)
            push(
                lambda: remote(
                    slot(kind, side, hops), slot(kind, side, hops),
                    send.at[kind, at], recv.at[kind, at + 1], where,
                ),
                here & more,
            )
        for way, where in ways.get(kind, ()):
            if hops or way != Y_FAR or slot is pow_slot:
                push(
                    lambda way=way, where=where: remote(
                        slot(kind, side, hops),
                        slot(kind, side, hops) if slot is pow_slot else landing(way, kind, side, hops),
                        send.at[way, at], recv.at[way, at], where,
                    ),
                    here,
                )

    def pow_relay(kind, side=0, hops=0):
        relay(kind, side, hops, (pow_slot, pow_send, pow_recv, pow_relays, P_Z))

    own_plane, other_plane = planes_ref.at[mine], planes_ref.at[other]
    own_slot, other_slot = tpl_own.at[bank, core, mine], tpl_own.at[bank, core, other]
    there, there_other = tpl_far.at[bank, core, mine], tpl_far.at[bank, core, other]
    own_strain = strain_all.at[seg]

    def both_ways(src, dst, send, recv, kind):
        for side in range(2):
            more, where = onward(side)
            push(
                lambda side=side, where=where: remote(
                    src, dst, send.at[kind, side * banks], recv.at[kind, number(side, 1)], where
                ),
                more,
            )

    own_copy = pltpu.make_async_copy(planes_ref, tpl_own.at[bank, core], local_sem.at[0])
    own_copy.start()

    def send_own():
        both_ways(own_plane, own_slot, tpl_send, tpl_recv, Z)
        send_power()
        push(lambda: remote(strain_ref, own_strain, str_send.at[0], str_recv.at[0], to_far))
        push(lambda: remote(strain_ref, own_strain, str_send.at[1], str_recv.at[1], to_near))
        push(lambda: remote(own_plane, own_slot, tpl_send.at[N_MINE, 0], tpl_recv.at[N_MINE, 0], to_near))
        push(lambda: remote(other_plane, other_slot, tpl_send.at[N_OTHER, 0], tpl_recv.at[N_OTHER, 0], to_near))

    for copy in small:
        copy.wait()

    total_rows = edges_ref.shape[1]
    upper = seg // half
    chunks = nfreq // CHUNK

    def fill_tables():
        eye = jnp.where(
            lax.broadcasted_iota(jnp.int32, (2 * TPL, 2 * TPL), 0)
            == lax.broadcasted_iota(jnp.int32, (2 * TPL, 2 * TPL), 1),
            1.0, 0.0,
        ).astype(BF16)
        row = lax.broadcasted_iota(jnp.int32, (2 * chunks, 2 * TPL), 0)
        mark = (jnp.where(row < chunks, row, row - chunks + 1) * CHUNK).astype(F32)
        low_lane = lax.broadcasted_iota(jnp.int32, (2 * chunks, 2 * TPL), 1) < TPL
        most = jnp.zeros((chunks, 2 * TPL), F32)
        down = upper.astype(F32)

        def turned(table):
            return lax.dot_general(eye, table.astype(BF16), NT, preferred_element_type=F32)

        for pair in range(total_rows // (2 * TPL)):
            group = slice(pair * 2 * TPL, (pair + 1) * 2 * TPL)
            edges = edges_ref[:, group].astype(F32)
            coarse = jnp.floor(edges * (1.0 / 16))
            bounds_ref[group, : BINS - 1] = turned(coarse) * 16.0 + turned(edges - coarse * 16.0)
            count = jnp.zeros((2 * chunks, 2 * TPL), F32)
            for level in range(BINS - 1):
                count = count + jnp.where(edges[level : level + 1] <= mark, 1.0, 0.0)
            first = count[:chunks]
            most = jnp.maximum(most, count[chunks:] - first)
            places = [first - SLOTS * jnp.floor(first * (1.0 / SLOTS))]
            for k in range(SLOTS - 1):
                place = jnp.full((chunks, 2 * TPL), float(CHUNK), F32)
                for level in range(k, BINS - 1):
                    place = jnp.where(
                        first == float(level - k),
                        jnp.minimum(edges[level : level + 1] - mark[:chunks], float(CHUNK)), place,
                    )
                places.append(place)
            column_ref[group, : SLOTS * chunks] = turned(jnp.concatenate(places, axis=0)).astype(BF16)
            count = jnp.where(row == 2 * chunks - 1, BINS - down, count)
            count = jnp.where(row == 0, -down, count)
            moved = pltpu.roll(count, TPL, 1)
            count_ref[2 * pair] = jnp.where(low_lane, count, moved)
            count_ref[2 * pair + 1] = jnp.where(low_lane, moved, count)
        most_ref[0] = jnp.max(most.astype(jnp.int32))

    def bin_index(bounds, first):
        freq = (
            lax.broadcasted_iota(jnp.int32, (bounds.shape[0], width), 1) + first
        ).astype(F32)
        bin_of = jnp.zeros((bounds.shape[0], width), F32)
        for level in range(BINS - 1):
            bin_of = jnp.where(freq >= bounds[:, level : level + 1], level + 1.0, bin_of)
        return bin_of

    own_power = pltpu.make_async_copy(power_own, power_all.at[bank, seg], local_sem.at[2])

    def fill_power():
        bin_of = bin_index(
            bounds_ref[pl.ds(pl.multiple_of(bank * rows, 8), rows), : BINS - 1], seg * width
        )
        real_part = planes_ref[0].reshape(rows, width).astype(F32)
        imag_part = planes_ref[1].reshape(rows, width).astype(F32)
        squares = real_part * real_part + imag_part * imag_part
        ones = jnp.ones((8, 3 * CHUNK), BF16)
        for pair in range(BINS // 2):
            sums = []
            for p in range(2):
                picked = jnp.where(bin_of == float(2 * pair + p), squares, 0.0)
                sums.append(
                    functools.reduce(
                        jnp.add,
                        [picked[:, c * CHUNK : (c + 1) * CHUNK] for c in range(width // CHUNK)],
                    )
                )
            value = jnp.concatenate(sums, axis=0)
            high = value.astype(BF16)
            left = value - high.astype(F32)
            middle = left.astype(BF16)
            low = (left - middle.astype(F32)).astype(BF16)
            line = lax.dot_general(
                ones, jnp.concatenate([high, middle, low], axis=1), NT, preferred_element_type=F32
            )
            power_own[pair : pair + 1, :] = line[0:1, :]

    def send_power():
        own_power.start()
        slot = power_all.at[bank, seg]
        both_ways(power_own, slot, pow_send, pow_recv, P_Z)
        push(lambda: remote(power_own, slot, pow_send.at[P_X, 0], pow_recv.at[P_X, 0], to_far))
        push(lambda: remote(power_own, slot, pow_send.at[P_N, 0], pow_recv.at[P_N, 0], to_near))

    def fill_codes(first, last):
        freq = lax.broadcasted_iota(jnp.int32, (BLOCK_TPL, CHUNK), 1).astype(F32).astype(BF16)
        one_b, zero_b, wrap = (jnp.asarray(v, BF16) for v in (1.0, 0.0, float(SLOTS)))

        def one(step, carry):
            at = pl.multiple_of(step * BLOCK_TPL, BLOCK_TPL)
            columns = column_ref[pl.ds(at, BLOCK_TPL), : SLOTS * chunks]
            for c in range(chunks):
                slot = columns[:, c : c + 1]
                for k in range(1, SLOTS):
                    place = columns[:, k * chunks + c : k * chunks + c + 1]
                    slot = slot + jnp.where(freq >= place, one_b, zero_b)
                slot = jnp.where(slot >= wrap, slot - wrap, slot)
                code_ref[step, :, c * CHUNK : (c + 1) * CHUNK] = slot
            return carry

        lax.fori_loop(first, last, one, 0)

    def fill_turns():
        shape = (8, nfreq)
        lag = seg * lags + lax.broadcasted_iota(jnp.int32, shape, 0) - LAGS // 2
        freq = lax.broadcasted_iota(jnp.int32, shape, 1)
        cos_own[...], sin_own[...] = turn(lag, freq, 2 * nfreq)

    def pick_lists():
        row_idx = lax.broadcasted_iota(jnp.int32, (rec, rec), 0)
        col_idx = lax.broadcasted_iota(jnp.int32, (rec, rec), 1)
        reg_row = reg_ref[0:1, :]
        reg_col = jnp.sum(jnp.where(row_idx == col_idx, reg_row, 0), axis=1, keepdims=True)
        count_row = jnp.sum(jnp.where(reg_col == reg_row, 1, 0), axis=0, keepdims=True)
        hot = jnp.min(jnp.where(count_row >= cap, reg_row, 1 << 20), axis=1, keepdims=True)
        is_hot_col = jnp.where(reg_col == hot, 1, 0)
        is_hot_row = jnp.where(reg_row == hot, 1, 0)
        rank_row = jnp.sum(jnp.where(row_idx < col_idx, is_hot_col, 0), axis=0, keepdims=True)
        rest_row = col_idx[0:1, :] - rank_row
        hot_ref[0] = jnp.min(jnp.where(count_row >= cap, reg_row, 1 << 20))
        hot_pick = jnp.where(
            (lax.broadcasted_iota(jnp.int32, (hot_pad, rec), 0) == rank_row) & (is_hot_row == 1), 1, 0
        )
        rest_pick = jnp.where(
            (lax.broadcasted_iota(jnp.int32, (rest_pad, rec), 0) == rest_row) & (is_hot_row == 0), 1, 0
        )
        hot_sel[...] = hot_pick.astype(F32)
        rest_sel[...] = rest_pick.astype(F32)
        rest_reg[...] = jnp.broadcast_to(
            jnp.sum(rest_pick * (reg_row + 1), axis=1, keepdims=True) - 1, rest_reg.shape
        )

    def fill_lhs(s, strain_at):
        lists = ((hot_sel, hot_lhs, hot_pad, 0), (rest_sel, rest_lhs, rest_pad, 2 * hot_pad))
        for sel_ref, _, pad, base in lists:
            sel = sel_ref[...].astype(BF16)
            for c in range(2):
                for d in range(2):
                    picked_ref[c, base + d * pad : base + (d + 1) * pad, :] = jnp.dot(
                        sel, strain_at(c, d), preferred_element_type=F32
                    )
        for q in range(width // CHUNK):
            here = slice(q * CHUNK, (q + 1) * CHUNK)
            at = pl.ds(pl.multiple_of(s * width + q * CHUNK, CHUNK), CHUNK)
            column = (s * (width // CHUNK) + q) * 2 * CHUNK
            re_at = pl.ds(pl.multiple_of(column, CHUNK), CHUNK)
            im_at = pl.ds(pl.multiple_of(column + CHUNK, CHUNK), CHUNK)
            for _, lhs_ref, pad, base in lists:
                real_part = picked_ref[0, base : base + 2 * pad, here]
                imag_part = picked_ref[1, base : base + 2 * pad, here]
                for lag in range(lags):
                    cosine = cos_own[lag : lag + 1, at]
                    sine = sin_own[lag : lag + 1, at]
                    rot_re = (real_part * cosine - imag_part * sine).astype(BF16)
                    rot_im = (real_part * sine + imag_part * cosine).astype(BF16)
                    top = (2 * lag) * 2 * pad
                    low = (2 * lag + 1) * 2 * pad
                    lhs_ref[top : top + 2 * pad, re_at] = rot_re
                    lhs_ref[top : top + 2 * pad, im_at] = rot_im
                    lhs_ref[low : low + 2 * pad, re_at] = rot_im
                    lhs_ref[low : low + 2 * pad, im_at] = -rot_re

    def landed_strain(s):
        return lambda c, d: strain_all[s, c, d * rec : (d + 1) * rec, :]

    blocks = total_rows // BLOCK_TPL

    def codes(part):
        fill_codes(part * blocks // (2 * banks), (part + 1) * blocks // (2 * banks))

    zero = jnp.zeros((), BF16)
    lane_c = lax.broadcasted_iota(jnp.int32, (2 * chunks, 2 * TPL), 1)
    second = jnp.where(lax.broadcasted_iota(jnp.int32, (chunks, 2 * TPL), 1) < TPL, 0.0, 1.0)

    def blocks_of(region):
        ids = [reads_ref[region, i] for i in range(4)]
        return [(b // held_blocks, b % held_blocks, b) for b in ids]

    def region_weights(region, close_ref):
        weight = jnp.zeros((8, 2 * TPL), F32)
        count = jnp.zeros((2 * chunks, 2 * TPL), F32)
        for i, (home, inner, _) in enumerate(blocks_of(region)):
            total = power_all[home, 0]
            for s in range(1, segs):
                total = total + power_all[home, s]
            edges_at = count_ref[home]
            for k in range(held_blocks):
                shift = (i - k + 2 * held_blocks) * BLOCK_TPL % (2 * TPL)
                wanted = jnp.where(lane_c % TPL // BLOCK_TPL == i, inner, held_blocks) == k
                weight = jnp.where(wanted[:8], pltpu.roll(total, shift, 1), weight)
                count = jnp.where(wanted, pltpu.roll(edges_at, shift, 1), count)
        weight = weight + 1e-06
        inv_weight = 1.0 / weight
        first = count[:chunks] + upper.astype(F32)
        last = count[chunks:] + upper.astype(F32)
        for a in range(2):
            close = jnp.zeros((chunks, 2 * TPL), F32)
            for m in range(BINS // SLOTS):
                level = second + float(SLOTS * m + 2 * a)
                close = jnp.where(
                    (level >= first) & (level < last), inv_weight[2 * m + a : 2 * m + a + 1], close
                )
            close_ref[a] = close
        norm = jnp.sum(weight, axis=0, keepdims=True)
        close_ref[2] = jnp.broadcast_to(
            1.0 / (norm + pltpu.roll(norm, TPL, 1)), (chunks, 2 * TPL)
        )

    def half_steps(which, region, lhs_ref, close_ref, acc_ref, sum_ref, total_ref):
        tpl_ref = tpl_own if which == 0 else tpl_far
        blocks = blocks_of(region)
        per_half = chunks // 2
        for step in range(per_half):
            at_step = which * per_half + step
            chunk = at_step + upper * (chunks - 1 - 2 * at_step)
            place = step + upper * (per_half - 1 - 2 * step)
            s, q = place // (width // CHUNK), lax.rem(place, width // CHUNK)
            at = pl.ds(pl.multiple_of(q * CHUNK, CHUNK), CHUNK)
            code_at = pl.ds(pl.multiple_of(chunk * CHUNK, CHUNK), CHUNK)
            lhs_at = pl.ds(pl.multiple_of(chunk * 2 * CHUNK, 2 * CHUNK), 2 * CHUNK)
            code = jnp.concatenate(
                [code_ref[b, :, code_at] for _, _, b in blocks], axis=0
            )
            planes = [
                jnp.concatenate(
                    [tpl_ref[home, s, c, inner, :, at] for home, inner, _ in blocks], axis=0
                )
                for c in range(2)
            ]
            matrix = []
            for slot in range(SLOTS):
                inside = code == jnp.asarray(slot, BF16)
                matrix.append(
                    jnp.concatenate([jnp.where(inside, plane, zero) for plane in planes], axis=1)
                )
            part = lax.dot_general(
                lhs_ref[:, lhs_at], jnp.concatenate(matrix, axis=0), NT, preferred_element_type=F32
            )
            fresh = at_step == 0
            both = part[:, : 2 * TPL] + part[:, 2 * TPL :]
            total_ref[...] = both if fresh else total_ref[...] + both
            for a in range(2):
                close = close_ref[a, pl.ds(chunk, 1), :]
                here = part[:, a * 2 * TPL : (a + 1) * 2 * TPL]
                if not fresh:
                    here = here + acc_ref[a]
                term = here * here * close
                sum_ref[a] = term if fresh else sum_ref[a] + term
                acc_ref[a] = jnp.where(close > 0.0, 0.0, here)

    def finish_list(pad, close_ref, sum_ref, total_ref, store):
        inv_norm = close_ref[2, 0:1, :]
        for lag in range(lags):
            top = lag * 4 * pad
            full = total_ref[top : top + 4 * pad]
            full = full + pltpu.roll(full, TPL, 1)
            energy = sum_ref[0, top : top + 4 * pad] + sum_ref[1, top : top + 4 * pad]
            signal = full * full * inv_norm
            signal = (signal[:pad] + signal[pad : 2 * pad]) + (
                signal[2 * pad : 3 * pad] + signal[3 * pad :]
            )
            energy = (energy[:pad] + energy[pad : 2 * pad]) + (
                energy[2 * pad : 3 * pad] + energy[3 * pad :]
            )
            energy = energy + pltpu.roll(energy, TPL, 1)
            store(lag, signal)
            store(lags + lag, (energy - signal) * (1.0 / (2 * BINS - 2)))

    kept = rest_acc.shape[0]

    def other_region(i):
        return lax.rem(hot_ref[0] + i, banks)

    def hot_half(which):
        if which == 0:
            region_weights(hot_ref[0], hot_close)
        half_steps(which, hot_ref[0], hot_lhs, hot_close, hot_acc, hot_sum, hot_total)

    def rest_half(which, i, at):
        if which == 0:
            region_weights(other_region(i), rest_close.at[at])
        half_steps(
            which, other_region(i), rest_lhs, rest_close.at[at],
            rest_acc.at[at], rest_sum.at[at], rest_total.at[at],
        )

    def rest_done(i, at):
        region = other_region(i)

        def store(where, value):
            rest_stat[where] = jnp.where(rest_reg[...] == region, value, rest_stat[where])

        finish_list(rest_pad, rest_close.at[at], rest_sum.at[at], rest_total.at[at], store)

    def each_other(body):
        def one(i, carry):
            body(i)
            return carry

        lax.fori_loop(1, banks, one, 0)

    split_rest = kept == banks - 1
    sides = [(side, hops) for hops in range(1, banks) for side in range(2)]
    every = [(0, 0)] + sides
    work = [functools.partial(codes, part) for part in range(2 * banks)]

    def some(count=1):
        for _ in range(min(count, len(work))):
            work.pop(0)()

    fill_tables()
    fill_power()
    pl.semaphore_wait(barrier, met)
    send_own()
    fill_turns()
    pick_lists()
    fill_lhs(seg, lambda c, d: strain_ref[c, d * rec : (d + 1) * rec, :])
    for hops in range(1, banks):
        for side in range(2):
            relay(Z, side, hops)
        for side in range(2):
            pow_relay(P_Z, side, hops)
        if hops == 1:
            push(lambda: remote(own_plane, there, tpl_send.at[X, 0], tpl_recv.at[X, 0], to_far))
        if hops == 2 or banks == 2:
            landed(strain_all.at[far], str_recv.at[0])
            push(
                lambda: remote(
                    strain_all.at[far], strain_all.at[far], str_send.at[2], str_recv.at[2], to_near
                )
            )
            landed(strain_all.at[near], str_recv.at[1])
            fill_lhs(near, landed_strain(near))
        some()
    push(
        lambda: remote(
            other_plane, there_other, tpl_send.at[X_OTHER, 0], tpl_recv.at[X_OTHER, 0], to_far
        )
    )
    for hops in range(1, banks):
        for side in range(2):
            relay(X, side, hops)
            relay(Y_OWN, side, hops)
        for side in range(2):
            pow_relay(P_X, side, hops)
        some(2 if hops > 1 else 1)
        if hops == 1:
            fill_lhs(far, landed_strain(far))
    some(len(work))
    landed(strain_all.at[far_near], str_recv.at[2])
    fill_lhs(far_near, landed_strain(far_near))
    pow_relay(P_X)
    for side, hops in every:
        for kind in (N_MINE, N_OTHER):
            relay(kind, side, hops)
        for kind in (P_N, P_FAR_N):
            pow_relay(kind, side, hops)
    own_copy.wait()
    own_power.wait()
    relay(X)
    for side in range(2):
        relay(Y_FAR, side, 1)
    hot_half(0)
    for hops in range(2, banks - 1):
        for side in range(2):
            relay(Y_FAR, side, hops)
    if split_rest:
        for i in range(1, banks - 1):
            rest_half(0, i, i - 1)
    relay(X_OTHER)
    if banks > 2:
        for side in range(2):
            relay(Y_FAR, side, banks - 1)
    if split_rest:
        rest_half(0, banks - 1, banks - 2)
    for side, hops in every:
        for kind in (N_FAR_MINE, N_FAR_OTHER):
            relay(kind, side, hops)
    rest_stat[...] = jnp.zeros_like(rest_stat)

    hot_half(1)

    def store_hot(at, value):
        hot_stat[at] = value

    finish_list(hot_pad, hot_close, hot_sum, hot_total, store_hot)
    if split_rest:
        for i in range(1, banks):
            rest_half(1, i, i - 1)
            rest_done(i, i - 1)
    else:

        def whole_region(i):
            rest_half(0, i, 0)
            rest_half(1, i, 0)
            rest_done(i, 0)

        each_other(whole_region)

    for which, out_ref in enumerate((snr_ref, chi_ref)):
        for lag in range(lags):
            at = which * lags + lag
            value = lax.dot_general(
                hot_sel[...], hot_stat[at], TN, precision=HIGH, preferred_element_type=F32
            ) + lax.dot_general(
                rest_sel[...], rest_stat[at], TN, precision=HIGH, preferred_element_type=F32
            )
            out_ref[lag] = value[:, :TPL]
    for finish in started:
        finish()


def any_phase_tables(seg_count, nfreq):
    period = 2 * nfreq
    lag = np.arange(LAGS, dtype=np.int64) - LAGS // 2
    turns = np.mod(lag[:, None] * np.arange(nfreq, dtype=np.int64)[None, :], period)
    angle = turns * (2.0 * math.pi / period)
    shape = (seg_count, LAGS // seg_count, nfreq)
    return (
        jnp.asarray(np.cos(angle).reshape(shape), F32),
        jnp.asarray(np.sin(angle).reshape(shape), F32),
    )


def any_exchange_kernel(
    cap, rec, hot_pad, rest_pad,
    planes_ref, strain_ref, reg_hbm, edges_hbm, cos_ref, sin_ref,
    tpl_all, power_all, bins_ref, hot_lhs, rest_lhs, hot_sel, rest_sel, rest_reg, hot_out,
    strain_all, power_own, bounds_ref, cos_own, sin_own, reg_ref, edges_ref,
    tpl_send, tpl_recv, pow_send, pow_recv, str_send, str_recv, local_sem,
):
    banks, segs = tpl_all.shape[:2]
    grp, bank, seg = lax.axis_index("grp"), lax.axis_index("bank"), lax.axis_index("seg")
    rows, width = planes_ref.shape[1:]
    nfreq = segs * width
    lags = cos_own.shape[0]
    mesh_id = pl.DeviceIdType.MESH
    half = segs // 2
    far = lax.rem(seg + half, segs)
    near = seg + 1 - 2 * lax.rem(seg, 2)
    far_near = lax.rem(near + half, segs)
    mine, other = grp, 1 - grp
    to_far, to_near, to_twin = {"seg": far}, {"seg": near}, {"grp": other}

    small = [
        pltpu.make_async_copy(cos_ref.at[seg], cos_own, local_sem.at[3]),
        pltpu.make_async_copy(sin_ref.at[seg], sin_own, local_sem.at[4]),
        pltpu.make_async_copy(edges_hbm, edges_ref, local_sem.at[5]),
        pltpu.make_async_copy(reg_hbm, reg_ref, local_sem.at[6]),
    ]
    for copy in small:
        copy.start()
    barrier = pltpu.get_barrier_semaphore()
    for off in range(1, banks):
        pl.semaphore_signal(
            barrier, inc=1, device_id={"bank": lax.rem(bank + off, banks)}, device_id_type=mesh_id
        )
    for where in (to_far, to_near, to_twin):
        pl.semaphore_signal(barrier, inc=1, device_id=where, device_id_type=mesh_id)
    pl.semaphore_wait(barrier, banks + 2)

    started = []

    def push(src, dst, send, recv, where):
        copy = pltpu.make_async_remote_copy(
            src_ref=src, dst_ref=dst, send_sem=send, recv_sem=recv,
            device_id=where, device_id_type=mesh_id,
        )
        copy.start()
        started.append(copy)

    def landed(slot, recv):
        pltpu.make_async_remote_copy(
            src_ref=slot, dst_ref=slot, send_sem=recv, recv_sem=recv,
            device_id=to_near, device_id_type=mesh_id,
        ).wait_recv()

    def source(off):
        return lax.rem(bank - off + banks, banks)

    Z, X, Y_OWN, Y_FAR, N_MINE, N_OTHER, N_FAR_MINE, N_FAR_OTHER = range(8)
    holds = {
        Z: (seg, mine), X: (far, mine), Y_OWN: (seg, other), Y_FAR: (far, other),
        N_MINE: (near, mine), N_OTHER: (near, other),
        N_FAR_MINE: (far_near, mine), N_FAR_OTHER: (far_near, other),
    }
    relays = {
        Z: ((X, to_far), (Y_OWN, to_twin), (N_MINE, to_near)),
        X: ((Y_FAR, to_twin), (N_FAR_MINE, to_near)),
        Y_OWN: ((N_OTHER, to_near),),
        Y_FAR: ((N_FAR_OTHER, to_near),),
    }

    def relay(kind, off):
        place, plane = holds[kind]
        slot = tpl_all.at[source(off), place, plane]
        landed(slot, tpl_recv.at[kind, off])
        for way, where in relays.get(kind, ()):
            push(slot, slot, tpl_send.at[way, off], tpl_recv.at[way, off], where)

    P_Z, P_X, P_N, P_FAR_N = range(4)
    pow_holds = {P_Z: seg, P_X: far, P_N: near, P_FAR_N: far_near}
    pow_relays = {P_Z: ((P_X, to_far), (P_N, to_near)), P_X: ((P_FAR_N, to_near),)}

    def pow_relay(kind, off):
        slot = power_all.at[source(off), pow_holds[kind]]
        landed(slot, pow_recv.at[kind, off])
        for way, where in pow_relays.get(kind, ()):
            push(slot, slot, pow_send.at[way, off], pow_recv.at[way, off], where)

    own_plane = planes_ref.at[mine]
    own_slot = tpl_all.at[bank, seg, mine]
    for off in range(1, banks):
        push(
            own_plane, own_slot, tpl_send.at[Z, off], tpl_recv.at[Z, off],
            {"bank": lax.rem(bank + off, banks)},
        )
    push(own_plane, own_slot, tpl_send.at[X, 0], tpl_recv.at[X, 0], to_far)
    own_strain = strain_all.at[0, seg]
    push(strain_ref, own_strain, str_send.at[0], str_recv.at[0], to_far)
    push(strain_ref, own_strain, str_send.at[1], str_recv.at[1], to_near)
    push(own_plane, own_slot, tpl_send.at[N_MINE, 0], tpl_recv.at[N_MINE, 0], to_near)
    push(
        planes_ref.at[other], tpl_all.at[bank, seg, other],
        tpl_send.at[N_OTHER, 0], tpl_recv.at[N_OTHER, 0], to_near,
    )
    own_copies = [
        pltpu.make_async_copy(planes_ref, tpl_all.at[bank, seg], local_sem.at[0]),
        pltpu.make_async_copy(strain_ref, own_strain, local_sem.at[1]),
    ]
    for copy in own_copies:
        copy.start()
    for copy in small:
        copy.wait()

    total_rows = edges_ref.shape[1]
    eye = jnp.where(
        lax.broadcasted_iota(jnp.int32, (128, 128), 0) == lax.broadcasted_iota(jnp.int32, (128, 128), 1),
        1.0, 0.0,
    )
    for first in range(0, total_rows, 128):
        bounds_ref[first : first + 128, :] = lax.dot_general(
            eye, edges_ref[:, first : first + 128].astype(F32), NT,
            precision=HIGH, preferred_element_type=F32,
        )

    def bin_index(bounds, first):
        freq = (
            lax.broadcasted_iota(jnp.int32, (bounds.shape[0], width), 1) + first
        ).astype(F32)
        bin_of = jnp.zeros((bounds.shape[0], width), F32)
        for level in range(BINS - 1):
            bin_of = bin_of + jnp.where(freq >= bounds[:, level : level + 1], 1.0, 0.0)
        return bin_of

    bin_of = bin_index(bounds_ref[pl.ds(pl.multiple_of(bank * rows, 8), rows), :], seg * width)
    real_part = planes_ref[0].astype(F32)
    imag_part = planes_ref[1].astype(F32)
    squares = real_part * real_part + imag_part * imag_part
    ones = jnp.ones((8, width), F32)
    for pair in range(BINS // 2):
        picked = jnp.concatenate(
            [jnp.where(bin_of == float(2 * pair + p), squares, 0.0) for p in range(2)], axis=0
        )
        line = lax.dot_general(ones, picked, NT, precision=HIGH, preferred_element_type=F32)
        power_own[pair : pair + 1, :] = line[0:1, :]
    own_power = pltpu.make_async_copy(power_own, power_all.at[bank, seg], local_sem.at[2])
    own_power.start()
    for off in range(1, banks):
        push(
            power_own, power_all.at[bank, seg], pow_send.at[P_Z, off], pow_recv.at[P_Z, off],
            {"bank": lax.rem(bank + off, banks)},
        )
    push(power_own, power_all.at[bank, seg], pow_send.at[P_X, 0], pow_recv.at[P_X, 0], to_far)
    push(power_own, power_all.at[bank, seg], pow_send.at[P_N, 0], pow_recv.at[P_N, 0], to_near)

    def fill_bins(first, last):
        def one(step, carry):
            at = pl.multiple_of(step * BLOCK_TPL, BLOCK_TPL)
            bounds = bounds_ref[pl.ds(at, BLOCK_TPL), :]
            for s in range(segs):
                bins_ref[pl.ds(at, BLOCK_TPL), s * width : (s + 1) * width] = bin_index(
                    bounds, s * width
                ).astype(BF16)
            return carry

        lax.fori_loop(first, last, one, 0)

    blocks = total_rows // BLOCK_TPL
    for off in range(banks):
        if off:
            relay(Z, off)
            relay(X, off - 1)
        if off == 1:
            landed(strain_all.at[0, far], str_recv.at[0])
            push(
                strain_all.at[0, far], strain_all.at[0, far], str_send.at[2], str_recv.at[2], to_near
            )
        if off > 1:
            relay(Y_OWN, off - 1)
            relay(Y_FAR, off - 2)
        fill_bins(off * blocks // banks, (off + 1) * blocks // banks)
    relay(X, banks - 1)
    relay(Y_OWN, banks - 1)
    relay(Y_FAR, banks - 2)
    for off in range(1, banks):
        pow_relay(P_Z, off)
    landed(strain_all.at[0, near], str_recv.at[1])
    landed(strain_all.at[0, far_near], str_recv.at[2])
    own_copies[1].wait()

    row_idx = lax.broadcasted_iota(jnp.int32, (rec, rec), 0)
    col_idx = lax.broadcasted_iota(jnp.int32, (rec, rec), 1)
    reg_row = reg_ref[0:1, :]
    reg_col = jnp.sum(jnp.where(row_idx == col_idx, reg_row, 0), axis=1, keepdims=True)
    count_row = jnp.sum(jnp.where(reg_col == reg_row, 1, 0), axis=0, keepdims=True)
    hot = jnp.min(jnp.where(count_row >= cap, reg_row, 1 << 20), axis=1, keepdims=True)
    is_hot_col = jnp.where(reg_col == hot, 1, 0)
    is_hot_row = jnp.where(reg_row == hot, 1, 0)
    rank_row = jnp.sum(jnp.where(row_idx < col_idx, is_hot_col, 0), axis=0, keepdims=True)
    rest_row = col_idx[0:1, :] - rank_row
    hot_out[0] = jnp.min(jnp.where(count_row >= cap, reg_row, 1 << 20))
    hot_pick = jnp.where(
        (lax.broadcasted_iota(jnp.int32, (hot_pad, rec), 0) == rank_row) & (is_hot_row == 1), 1, 0
    )
    rest_pick = jnp.where(
        (lax.broadcasted_iota(jnp.int32, (rest_pad, rec), 0) == rest_row) & (is_hot_row == 0), 1, 0
    )
    hot_sel[...] = hot_pick.astype(F32)
    rest_sel[...] = rest_pick.astype(F32)
    rest_reg[...] = jnp.broadcast_to(
        jnp.sum(rest_pick * (reg_row + 1), axis=1, keepdims=True) - 1, rest_reg.shape
    )
    lists = ((hot_pick, hot_lhs, hot_pad), (rest_pick, rest_lhs, rest_pad))
    for s in range(segs):
        if s == segs // 2:
            relay(Y_FAR, banks - 1)
            for off in range(banks):
                pow_relay(P_X, off)
        for pick, lhs_ref, pad in lists:
            sel = pick.astype(F32).astype(BF16)
            at = slice(s * width, (s + 1) * width)
            at_im = slice(nfreq + s * width, nfreq + (s + 1) * width)
            parts = []
            for c in range(2):
                parts.append(
                    jnp.concatenate(
                        [
                            jnp.dot(
                                sel,
                                strain_all[0, s, c, d * rec : (d + 1) * rec, :],
                                preferred_element_type=F32,
                            )
                            for d in range(2)
                        ],
                        axis=0,
                    )
                )
            real_part, imag_part = parts
            for lag in range(lags):
                cosine = cos_own[lag : lag + 1, at]
                sine = sin_own[lag : lag + 1, at]
                rot_re = (real_part * cosine - imag_part * sine).astype(BF16)
                rot_im = (real_part * sine + imag_part * cosine).astype(BF16)
                top = (2 * lag) * 2 * pad
                low = (2 * lag + 1) * 2 * pad
                lhs_ref[top : top + 2 * pad, at] = rot_re
                lhs_ref[top : top + 2 * pad, at_im] = rot_im
                lhs_ref[low : low + 2 * pad, at] = rot_im
                lhs_ref[low : low + 2 * pad, at_im] = -rot_re
    for off in range(banks):
        for kind in (N_MINE, N_OTHER, N_FAR_MINE, N_FAR_OTHER):
            relay(kind, off)
        for kind in (P_N, P_FAR_N):
            pow_relay(kind, off)
    own_copies[0].wait()
    own_power.wait()
    for copy in started:
        copy.wait_send()


def any_follow_kernel(
    held_blocks,
    reads_ref, hot_ref, hot_lhs, rest_lhs, hot_sel, rest_sel, rest_reg,
    t0_ref, t1_ref, t2_ref, t3_ref, b0_ref, b1_ref, b2_ref, b3_ref, power_ref,
    snr_ref, chi_ref,
    tmat, z_ref, hot_stat, rest_stat,
):
    region = pl.program_id(0)
    segs, _, _, width = t0_ref.shape[1:]
    nfreq = segs * width
    lags = snr_ref.shape[0]
    hot_pad, rest_pad = hot_sel.shape[0], rest_sel.shape[0]
    tpl_refs = (t0_ref, t1_ref, t2_ref, t3_ref)
    bin_refs = (b0_ref, b1_ref, b2_ref, b3_ref)

    @pl.when(region == 0)
    def prepare():
        hot_stat[...] = jnp.zeros_like(hot_stat)
        rest_stat[...] = jnp.zeros_like(rest_stat)

    lane = lax.broadcasted_iota(jnp.int32, (8, 2 * TPL), 1)
    weight = jnp.zeros((8, 2 * TPL), F32)
    for i in range(4):
        block_id = reads_ref[region, i]
        bank, inner = block_id // held_blocks, block_id % held_blocks
        total = power_ref[bank, 0]
        for s in range(1, segs):
            total = total + power_ref[bank, s]
        shift = (i - inner + 2 * held_blocks) * BLOCK_TPL % (2 * TPL)
        moved = pltpu.roll(total, shift, 1)
        weight = jnp.where((lane % TPL) // BLOCK_TPL == i, moved, weight)
    weight = weight + 1e-06
    norm = jnp.sum(weight, axis=0, keepdims=True)
    norm = norm + pltpu.roll(norm, TPL, 1)
    inv_norm = 1.0 / norm
    share = weight * inv_norm
    inv_weight = 1.0 / weight

    def run(lhs_ref, pad, store):
        rows = lhs_ref.shape[0]
        group = 4
        for q in range(BINS // group):
            for g in range(group):
                level = jnp.asarray(q * group + g, BF16)
                for i in range(4):
                    at_row = slice(g * TPL + i * BLOCK_TPL, g * TPL + (i + 1) * BLOCK_TPL)
                    for s in range(segs):
                        inside = (
                            bin_refs[i][:, s * width : (s + 1) * width] == level
                        )
                        for c in range(2):
                            at = slice(c * nfreq + s * width, c * nfreq + (s + 1) * width)
                            tmat[q, at_row, at] = jnp.where(
                                inside, tpl_refs[i][0, s, c], jnp.zeros((), BF16)
                            )
            z_ref[0:rows, q * group * TPL : (q + 1) * group * TPL] = lax.dot_general(
                lhs_ref[...], tmat[q], NT, preferred_element_type=F32
            )
        for lag in range(lags):
            top = (2 * lag) * 2 * pad
            low = (2 * lag + 1) * 2 * pad
            zr = [z_ref[top : top + 2 * pad, j * 128 : (j + 1) * 128] for j in range(BINS // 2)]
            zi = [z_ref[low : low + 2 * pad, j * 128 : (j + 1) * 128] for j in range(BINS // 2)]
            full_re = functools.reduce(jnp.add, zr)
            full_im = functools.reduce(jnp.add, zi)
            full_re = full_re + pltpu.roll(full_re, TPL, 1)
            full_im = full_im + pltpu.roll(full_im, TPL, 1)
            signal = (full_re * full_re + full_im * full_im) * inv_norm
            chi = jnp.zeros_like(signal)
            for j in range(BINS // 2):
                diff_re = zr[j] - share[j : j + 1] * full_re
                diff_im = zi[j] - share[j : j + 1] * full_im
                chi = chi + (diff_re * diff_re + diff_im * diff_im) * inv_weight[j : j + 1]
            chi = (chi + pltpu.roll(chi, TPL, 1)) * (1.0 / (2 * BINS - 2))
            store(lag, signal[:pad] + signal[pad:])
            store(lags + lag, chi[:pad] + chi[pad:])

    def store_hot(at, value):
        hot_stat[at] = value

    def store_rest(at, value):
        rest_stat[at] = jnp.where(rest_reg[...] == region, value, rest_stat[at])

    @pl.when(region == hot_ref[0])
    def on_hot():
        run(hot_lhs, hot_pad, store_hot)

    @pl.when(region != hot_ref[0])
    def on_rest():
        run(rest_lhs, rest_pad, store_rest)

    @pl.when(region == pl.num_programs(0) - 1)
    def finish():
        for which, out_ref in enumerate((snr_ref, chi_ref)):
            for lag in range(lags):
                at = which * lags + lag
                value = lax.dot_general(
                    hot_sel[...], hot_stat[at], TN, precision=HIGH, preferred_element_type=F32
                ) + lax.dot_general(
                    rest_sel[...], rest_stat[at], TN, precision=HIGH, preferred_element_type=F32
                )
                out_ref[lag] = value[:, :TPL]


def any_per_device(strain, region_of, templates, reads, edges):
    region_count = lax.axis_size("bank")
    seg_count = lax.axis_size("seg")
    rec, _, _, width = strain.shape
    nfreq = width * seg_count
    held_rows = templates.shape[0]
    held_blocks = held_rows // BLOCK_TPL
    cap = 3 * rec // region_count
    hot_pad, rest_pad = round_up(cap, 8), round_up(rec - cap, 8)
    lags = LAGS // seg_count
    planes = jnp.transpose(templates, (1, 0, 2))
    strain_planes = jnp.transpose(strain, (2, 1, 0, 3)).reshape(2, 2 * rec, width)
    cos_tab, sin_tab = any_phase_tables(seg_count, nfreq)
    reg = region_of.reshape(1, rec)
    rows_hot, rows_rest = lags * 4 * hot_pad, lags * 4 * rest_pad
    vmem = pl.BlockSpec(memory_space=pltpu.VMEM)
    anyw = pl.BlockSpec(memory_space=pl.ANY)
    hbm = pl.BlockSpec(memory_space=pltpu.HBM)
    total_rows = edges.shape[0]

    def struct(shape, dtype):
        return jax.ShapeDtypeStruct(shape, dtype)

    dma = pltpu.SemaphoreType.DMA
    exchanged = pl.pallas_call(
        functools.partial(any_exchange_kernel, cap, rec, hot_pad, rest_pad),
        out_shape=(
            struct((region_count, seg_count) + planes.shape, BF16),
            struct((region_count, seg_count, BINS // 2, 2 * TPL), F32),
            struct((total_rows, nfreq), BF16),
            struct((rows_hot, 2 * nfreq), BF16),
            struct((rows_rest, 2 * nfreq), BF16),
            struct((hot_pad, rec), F32),
            struct((rest_pad, rec), F32),
            struct((rest_pad, 2 * TPL), jnp.int32),
            struct((1,), jnp.int32),
        ),
        in_specs=[vmem, vmem, hbm, hbm, hbm, hbm],
        out_specs=(anyw, anyw) + (vmem,) * 6 + (pl.BlockSpec(memory_space=pltpu.SMEM),),
        scratch_shapes=[
            pltpu.VMEM((1, seg_count) + strain_planes.shape, BF16),
            pltpu.VMEM((BINS // 2, 2 * TPL), F32),
            pltpu.VMEM((total_rows, BINS - 1), F32),
            pltpu.VMEM((lags, nfreq), F32),
            pltpu.VMEM((lags, nfreq), F32),
            pltpu.VMEM((1, rec), jnp.int32),
            pltpu.VMEM((BINS - 1, total_rows), jnp.int32),
            dma((8, region_count)),
            dma((8, region_count)),
            dma((4, region_count)),
            dma((4, region_count)),
            dma((3,)),
            dma((3,)),
            dma((7,)),
        ],
        compiler_params=pltpu.CompilerParams(
            collective_id=1, has_side_effects=True, vmem_limit_bytes=50 * 1024 * 1024
        ),
        name="any_exchange",
    )(planes, strain_planes, reg, edges.T, cos_tab, sin_tab)
    tpl_all, power_all, bins_all, hot_lhs, rest_lhs, hot_sel, rest_sel, rest_reg, hot = exchanged

    def tpl_spec(i):
        def index(r, reads_ref, hot_ref):
            block_id = reads_ref[r, i]
            return (block_id // held_blocks, 0, 0, block_id % held_blocks, 0)

        return pl.BlockSpec((1, seg_count, 2, BLOCK_TPL, width), index)

    def bin_spec(i):
        return pl.BlockSpec((BLOCK_TPL, nfreq), lambda r, reads_ref, hot_ref: (reads_ref[r, i], 0))

    def whole(array):
        return pl.BlockSpec(
            array.shape, lambda r, a, b: (0,) * array.ndim, pipeline_mode=pl.Buffered(1)
        )

    out = struct((lags, rec, TPL), F32)
    resident = (hot_lhs, rest_lhs, hot_sel, rest_sel, rest_reg)
    snr, chi = pl.pallas_call(
        functools.partial(any_follow_kernel, held_blocks),
        out_shape=(out, out),
        grid_spec=pltpu.PrefetchScalarGridSpec(
            num_scalar_prefetch=2,
            grid=(region_count,),
            in_specs=[whole(x) for x in resident]
            + [tpl_spec(i) for i in range(4)]
            + [bin_spec(i) for i in range(4)]
            + [whole(power_all)],
            out_specs=(pl.BlockSpec(out.shape, lambda r, a, b: (0, 0, 0)),) * 2,
            scratch_shapes=[
                pltpu.VMEM((4, 4 * TPL, 2 * nfreq), BF16),
                pltpu.VMEM((max(rows_hot, rows_rest), BINS * TPL), F32),
                pltpu.VMEM((2 * lags, hot_pad, 2 * TPL), F32),
                pltpu.VMEM((2 * lags, rest_pad, 2 * TPL), F32),
            ],
        ),
        compiler_params=pltpu.CompilerParams(
            dimension_semantics=("arbitrary",), vmem_limit_bytes=50 * 1024 * 1024
        ),
        name="any_follow",
    )(
        reads, hot, *resident, tpl_all, tpl_all, tpl_all, tpl_all,
        bins_all, bins_all, bins_all, bins_all, power_all,
    )
    return jnp.transpose(snr, (0, 2, 1)), jnp.transpose(chi, (0, 2, 1))


def per_device(strain, region_of, templates, reads, edges):
    region_count = lax.axis_size("bank")
    seg_count = lax.axis_size("seg")
    rec, _, _, width = strain.shape
    nfreq = width * seg_count
    held_rows = templates.shape[0]
    held_blocks = held_rows // BLOCK_TPL
    cap = 3 * rec // region_count
    hot_pad, rest_pad = round_up(cap, 8), round_up(rec - cap, 8)
    lags = LAGS // seg_count
    planes = jnp.transpose(templates, (1, 0, 2)).reshape(2, held_blocks, BLOCK_TPL, width)
    strain_planes = jnp.transpose(strain, (2, 1, 0, 3)).reshape(2, 2 * rec, width)
    reg = region_of.reshape(1, rec)
    rows_hot, rows_rest = lags * 4 * hot_pad, lags * 4 * rest_pad
    vmem = pl.BlockSpec(memory_space=pltpu.VMEM)
    hbm = pl.BlockSpec(memory_space=pltpu.HBM)
    smem = pl.BlockSpec(memory_space=pltpu.SMEM)
    total_rows = edges.shape[0]
    chunks = nfreq // CHUNK
    kept = region_count - 1 if region_count <= 4 else 1

    def struct(shape, dtype):
        return jax.ShapeDtypeStruct(shape, dtype)

    dma = pltpu.SemaphoreType.DMA
    half_shape = (region_count, seg_count // 2) + planes.shape
    out = struct((lags, rec, TPL), F32)
    snr, chi, most = pl.pallas_call(
        functools.partial(follow_up_kernel, cap, rec, hot_pad, rest_pad, held_blocks),
        out_shape=(out, out, struct((1,), jnp.int32)),
        in_specs=[vmem, vmem, hbm, hbm, hbm],
        out_specs=(vmem, vmem, smem),
        scratch_shapes=[
            pltpu.VMEM(half_shape, BF16),
            pltpu.VMEM(half_shape, BF16),
            pltpu.VMEM((region_count, seg_count, BINS // 2, 2 * TPL), F32),
            pltpu.VMEM((total_rows // BLOCK_TPL, BLOCK_TPL, nfreq), BF16),
            pltpu.VMEM((total_rows, 2 * TPL), F32),
            pltpu.VMEM((region_count, 2 * chunks, 2 * TPL), F32),
            pltpu.VMEM((rows_hot, 2 * nfreq), BF16),
            pltpu.VMEM((rows_rest, 2 * nfreq), BF16),
            pltpu.VMEM((hot_pad, rec), F32),
            pltpu.VMEM((rest_pad, rec), F32),
            pltpu.VMEM((rest_pad, 2 * TPL), jnp.int32),
            pltpu.SMEM((1,), jnp.int32),
            pltpu.VMEM((seg_count,) + strain_planes.shape, BF16),
            pltpu.VMEM((BINS // 2, 2 * TPL), F32),
            pltpu.VMEM((total_rows, 2 * TPL), BF16),
            pltpu.VMEM((8, nfreq), F32),
            pltpu.VMEM((8, nfreq), F32),
            pltpu.VMEM((2, 2 * (hot_pad + rest_pad), width), F32),
            pltpu.VMEM((1, rec), jnp.int32),
            pltpu.VMEM((BINS - 1, total_rows), jnp.int32),
            pltpu.SMEM(reads.shape, jnp.int32),
            pltpu.VMEM((3, chunks, 2 * TPL), F32),
            pltpu.VMEM((kept, 3, chunks, 2 * TPL), F32),
            pltpu.VMEM((2, rows_hot, 2 * TPL), F32),
            pltpu.VMEM((2, rows_hot, 2 * TPL), F32),
            pltpu.VMEM((rows_hot, 2 * TPL), F32),
            pltpu.VMEM((kept, 2, rows_rest, 2 * TPL), F32),
            pltpu.VMEM((kept, 2, rows_rest, 2 * TPL), F32),
            pltpu.VMEM((kept, rows_rest, 2 * TPL), F32),
            pltpu.VMEM((2 * lags, hot_pad, 2 * TPL), F32),
            pltpu.VMEM((2 * lags, rest_pad, 2 * TPL), F32),
            dma((9, 2 * region_count)),
            dma((9, 2 * region_count)),
            dma((4, 2 * region_count)),
            dma((4, 2 * region_count)),
            dma((3,)),
            dma((3,)),
            dma((6,)),
        ],
        compiler_params=pltpu.CompilerParams(
            collective_id=0, has_side_effects=True, vmem_limit_bytes=48 * 1024 * 1024
        ),
        name="follow_up",
    )(planes, strain_planes, reg, edges.T, reads)
    done = jnp.transpose(snr, (0, 2, 1)), jnp.transpose(chi, (0, 2, 1))
    return lax.cond(
        most[0] < SLOTS, lambda: done,
        lambda: any_per_device(strain, region_of, templates, reads, edges),
    )


def solution(mesh):
    placed = (
        P(("grp", "bank"), None, None, "seg"),
        P(("grp", "bank")),
        P("bank", None, "seg"),
        P(),
        P(),
    )
    return jax.shard_map(
        per_device,
        mesh=mesh,
        in_specs=placed,
        out_specs=(P("seg", None, ("grp", "bank")), P("seg", None, ("grp", "bank"))),
        check_vma=False,
    )
```

```python
import functools
import math

import jax
import jax.numpy as jnp
import numpy as np
from jax import lax
from jax.experimental import pallas as pl
from jax.experimental.pallas import tpu as pltpu
from jax.sharding import PartitionSpec as P

BLOCK_TPL = 16
BINS = 16
LAGS = 16
TPL = 64
CHUNK = 128
SLOTS = 4
F32 = jnp.float32
BF16 = jnp.bfloat16
NT = (((1,), (1,)), ((), ()))
TN = (((0,), (0,)), ((), ()))
HIGH = lax.Precision.HIGHEST


def round_up(value, step):
    return -(-value // step) * step


def turn(lag, freq, period):
    quarter = period // 4
    moved = (freq * lag + quarter // 2) & (period - 1)
    quadrant = moved // quarter
    angle = (moved % quarter - quarter // 2).astype(F32) * (2.0 * math.pi / period)
    sq = angle * angle
    sine = angle * (1.0 + sq * (-1.0 / 6 + sq * (1.0 / 120 + sq * (-1.0 / 5040 + sq * (1.0 / 362880)))))
    cosine = 1.0 + sq * (-0.5 + sq * (1.0 / 24 + sq * (-1.0 / 720 + sq * (1.0 / 40320))))
    odd = quadrant % 2 == 1
    big, small = jnp.where(odd, sine, cosine), jnp.where(odd, cosine, sine)
    cos_out = jnp.where((quadrant == 1) | (quadrant == 2), -big, big)
    sin_out = jnp.where(quadrant >= 2, -small, small)
    return cos_out, sin_out


def follow_up_kernel(
    cap, rec, hot_pad, rest_pad, held_blocks,
    planes_ref, strain_ref, reg_hbm, edges_hbm, reads_hbm,
    snr_ref, chi_ref, most_ref,
    tpl_own, tpl_far, power_all, code_ref, bounds_ref, count_ref,
    hot_lhs, rest_lhs, hot_sel, rest_sel, rest_reg, hot_ref,
    strain_all, power_own, column_ref, cos_own, sin_own, picked_ref, reg_ref, edges_ref, reads_ref,
    hot_close, rest_close, hot_acc, hot_sum, hot_total, rest_acc, rest_sum, rest_total,
    stat_ref,
    tpl_send, tpl_recv, pow_send, pow_recv, str_send, str_recv, code_send, code_recv, local_sem,
):
    banks, segs = power_all.shape[:2]
    grp, bank, seg = lax.axis_index("grp"), lax.axis_index("bank"), lax.axis_index("seg")
    width = planes_ref.shape[3]
    rows = held_blocks * BLOCK_TPL
    nfreq = segs * width
    lags = LAGS // segs
    mesh_id = pl.DeviceIdType.MESH
    half = segs // 2
    far = lax.rem(seg + half, segs)
    near = seg + 1 - 2 * lax.rem(seg, 2)
    far_near = lax.rem(near + half, segs)
    mine, other = grp, 1 - grp
    to_far, to_near, to_twin = {"seg": far}, {"seg": near}, {"grp": other}

    up_ok, down_ok = bank < banks - 1, bank > 0

    small = [
        pltpu.make_async_copy(edges_hbm, edges_ref, local_sem.at[3]),
        pltpu.make_async_copy(reg_hbm, reg_ref, local_sem.at[4]),
        pltpu.make_async_copy(reads_hbm, reads_ref, local_sem.at[5]),
    ]
    for copy in small:
        copy.start()
    barrier = pltpu.get_barrier_semaphore()

    def greet(where):
        pl.semaphore_signal(barrier, inc=1, device_id=where, device_id_type=mesh_id)

    for where in (to_far, to_near, to_twin):
        greet(where)
    pl.when(up_ok)(lambda: greet({"bank": bank + 1}))
    pl.when(down_ok)(lambda: greet({"bank": bank - 1}))
    met = 3 + lax.min(bank, 1) + lax.min(banks - 1 - bank, 1)
    started = []

    def push(describe, condition=None):
        def start():
            describe().start()

        def finish():
            describe().wait_send()

        if condition is None:
            start()
            started.append(finish)
        else:
            pl.when(condition)(start)
            started.append(lambda: pl.when(condition)(finish))

    def remote(src, dst, send, recv, where):
        return pltpu.make_async_remote_copy(
            src_ref=src, dst_ref=dst, send_sem=send, recv_sem=recv,
            device_id=where, device_id_type=mesh_id,
        )

    def landed(slot, recv):
        remote(slot, slot, recv, recv, to_near).wait_recv()

    def source(side, hops):
        return bank - hops if side == 0 else bank + hops

    def present(side, hops):
        return bank >= hops if side == 0 else bank + hops <= banks - 1

    def number(side, hops):
        return side * banks + hops

    def onward(side):
        return (up_ok, {"bank": bank + 1}) if side == 0 else (down_ok, {"bank": bank - 1})

    Z, X, X_OTHER, Y_OWN, Y_FAR, N_MINE, N_OTHER, N_FAR_MINE, N_FAR_OTHER = range(9)
    core, core_near = lax.rem(seg, half), lax.rem(near, half)
    holds = {
        Z: (tpl_own, core, mine), X: (tpl_far, core, mine), X_OTHER: (tpl_far, core, other),
        Y_OWN: (tpl_own, core, other), Y_FAR: (tpl_far, core, other),
        N_MINE: (tpl_own, core_near, mine), N_OTHER: (tpl_own, core_near, other),
        N_FAR_MINE: (tpl_far, core_near, mine), N_FAR_OTHER: (tpl_far, core_near, other),
    }
    relays = {
        Z: ((Y_OWN, to_twin), (X, to_far), (N_MINE, to_near)),
        X: ((Y_FAR, to_twin), (N_FAR_MINE, to_near)),
        X_OTHER: ((N_FAR_OTHER, to_near),),
        Y_OWN: ((N_OTHER, to_near),),
        Y_FAR: ((N_FAR_OTHER, to_near),),
    }
    P_Z, P_X, P_N, P_FAR_N = range(4)
    pow_holds = {P_Z: seg, P_X: far, P_N: near, P_FAR_N: far_near}
    pow_relays = {P_Z: ((P_X, to_far), (P_N, to_near)), P_X: ((P_FAR_N, to_near),)}

    def landing(way, kind, side, hops):
        ref, place, plane = holds[kind]
        if way in (X, X_OTHER):
            ref = tpl_far
        return ref.at[source(side, hops), place, plane]

    def tpl_slot(kind, side, hops):
        ref, place, plane = holds[kind]
        return ref.at[source(side, hops), place, plane]

    def pow_slot(kind, side, hops):
        return power_all.at[source(side, hops), pow_holds[kind]]

    def relay(kind, side=0, hops=0, table=(tpl_slot, tpl_send, tpl_recv, relays, Z)):
        slot, send, recv, ways, first = table
        at = number(side, hops)
        here = present(side, hops) if hops else None

        def wait():
            landed(slot(kind, side, hops), recv.at[kind, at])

        wait() if here is None else pl.when(here)(wait)
        if kind == first:
            more, where = onward(side)
            push(
                lambda: remote(
                    slot(kind, side, hops), slot(kind, side, hops),
                    send.at[kind, at], recv.at[kind, at + 1], where,
                ),
                here & more,
            )
        for way, where in ways.get(kind, ()):
            if hops or way != Y_FAR or slot is pow_slot:
                push(
                    lambda way=way, where=where: remote(
                        slot(kind, side, hops),
                        slot(kind, side, hops) if slot is pow_slot else landing(way, kind, side, hops),
                        send.at[way, at], recv.at[way, at], where,
                    ),
                    here,
                )

    def pow_relay(kind, side=0, hops=0):
        relay(kind, side, hops, (pow_slot, pow_send, pow_recv, pow_relays, P_Z))

    own_plane, other_plane = planes_ref.at[mine], planes_ref.at[other]
    own_slot, other_slot = tpl_own.at[bank, core, mine], tpl_own.at[bank, core, other]
    there, there_other = tpl_far.at[bank, core, mine], tpl_far.at[bank, core, other]
    own_strain = strain_all.at[seg]

    def both_ways(src, dst, send, recv, kind):
        for side in range(2):
            more, where = onward(side)
            push(
                lambda side=side, where=where: remote(
                    src, dst, send.at[kind, side * banks], recv.at[kind, number(side, 1)], where
                ),
                more,
            )

    own_copy = pltpu.make_async_copy(planes_ref, tpl_own.at[bank, core], local_sem.at[0])
    own_copy.start()

    def send_own():
        both_ways(own_plane, own_slot, tpl_send, tpl_recv, Z)
        push(lambda: remote(strain_ref, own_strain, str_send.at[0], str_recv.at[0], to_far))
        push(lambda: remote(strain_ref, own_strain, str_send.at[1], str_recv.at[1], to_near))
        push(lambda: remote(own_plane, own_slot, tpl_send.at[N_MINE, 0], tpl_recv.at[N_MINE, 0], to_near))
        push(lambda: remote(other_plane, other_slot, tpl_send.at[N_OTHER, 0], tpl_recv.at[N_OTHER, 0], to_near))


    total_rows = edges_ref.shape[1]
    upper = seg // half
    chunks = nfreq // CHUNK

    def fill_tables():
        eye = jnp.where(
            lax.broadcasted_iota(jnp.int32, (2 * TPL, 2 * TPL), 0)
            == lax.broadcasted_iota(jnp.int32, (2 * TPL, 2 * TPL), 1),
            1.0, 0.0,
        ).astype(BF16)
        row = lax.broadcasted_iota(jnp.int32, (2 * chunks, 2 * TPL), 0)
        mark = (jnp.where(row < chunks, row, row - chunks + 1) * CHUNK).astype(F32)
        low_lane = lax.broadcasted_iota(jnp.int32, (2 * chunks, 2 * TPL), 1) < TPL
        most = jnp.zeros((chunks, 2 * TPL), F32)
        down = upper.astype(F32)

        def turned(table):
            return lax.dot_general(eye, table.astype(BF16), NT, preferred_element_type=F32)

        for pair in range(total_rows // (2 * TPL)):
            group = slice(pair * 2 * TPL, (pair + 1) * 2 * TPL)
            edges = edges_ref[:, group].astype(F32)
            coarse = jnp.floor(edges * (1.0 / 16))
            bounds_ref[group, : BINS - 1] = turned(coarse) * 16.0 + turned(edges - coarse * 16.0)
            count = jnp.zeros((2 * chunks, 2 * TPL), F32)
            for level in range(BINS - 1):
                count = count + jnp.where(edges[level : level + 1] <= mark, 1.0, 0.0)
            first = count[:chunks]
            most = jnp.maximum(most, count[chunks:] - first)
            places = [first - SLOTS * jnp.floor(first * (1.0 / SLOTS))]
            for k in range(SLOTS - 1):
                place = jnp.full((chunks, 2 * TPL), float(CHUNK), F32)
                for level in range(k, BINS - 1):
                    place = jnp.where(
                        first == float(level - k),
                        jnp.minimum(edges[level : level + 1] - mark[:chunks], float(CHUNK)), place,
                    )
                places.append(place)
            column_ref[group, : SLOTS * chunks] = turned(jnp.concatenate(places, axis=0)).astype(BF16)
            count = jnp.where(row == 2 * chunks - 1, BINS - down, count)
            count = jnp.where(row == 0, -down, count)
            moved = pltpu.roll(count, TPL, 1)
            count_ref[2 * pair] = jnp.where(low_lane, count, moved)
            count_ref[2 * pair + 1] = jnp.where(low_lane, moved, count)
        most_ref[0] = jnp.max(most.astype(jnp.int32))

    def bin_index(bounds, first):
        freq = (
            lax.broadcasted_iota(jnp.int32, (bounds.shape[0], width), 1) + first
        ).astype(F32)
        bin_of = jnp.zeros((bounds.shape[0], width), F32)
        for level in range(BINS - 1):
            bin_of = jnp.where(freq >= bounds[:, level : level + 1], level + 1.0, bin_of)
        return bin_of

    own_power = pltpu.make_async_copy(power_own, power_all.at[bank, seg], local_sem.at[2])

    def fill_power():
        bin_of = bin_index(
            bounds_ref[pl.ds(pl.multiple_of(bank * rows, 8), rows), : BINS - 1], seg * width
        )
        real_part = planes_ref[0].reshape(rows, width).astype(F32)
        imag_part = planes_ref[1].reshape(rows, width).astype(F32)
        squares = real_part * real_part + imag_part * imag_part
        ones = jnp.ones((8, 3 * CHUNK), BF16)
        for pair in range(BINS // 2):
            sums = []
            for p in range(2):
                picked = jnp.where(bin_of == float(2 * pair + p), squares, 0.0)
                sums.append(
                    functools.reduce(
                        jnp.add,
                        [picked[:, c * CHUNK : (c + 1) * CHUNK] for c in range(width // CHUNK)],
                    )
                )
            value = jnp.concatenate(sums, axis=0)
            high = value.astype(BF16)
            left = value - high.astype(F32)
            middle = left.astype(BF16)
            low = (left - middle.astype(F32)).astype(BF16)
            line = lax.dot_general(
                ones, jnp.concatenate([high, middle, low], axis=1), NT, preferred_element_type=F32
            )
            power_own[pair : pair + 1, :] = line[0:1, :]

    def send_power():
        own_power.start()
        slot = power_all.at[bank, seg]
        both_ways(power_own, slot, pow_send, pow_recv, P_Z)
        push(lambda: remote(power_own, slot, pow_send.at[P_X, 0], pow_recv.at[P_X, 0], to_far))
        push(lambda: remote(power_own, slot, pow_send.at[P_N, 0], pow_recv.at[P_N, 0], to_near))

    def fill_codes(first, count):
        freq = lax.broadcasted_iota(jnp.int32, (BLOCK_TPL, CHUNK), 1).astype(F32).astype(BF16)
        one_b, zero_b, wrap = (jnp.asarray(v, BF16) for v in (1.0, 0.0, float(SLOTS)))

        def one(step, carry):
            step = first + step
            at = pl.multiple_of(step * BLOCK_TPL, BLOCK_TPL)
            columns = column_ref[pl.ds(at, BLOCK_TPL), : SLOTS * chunks]
            for c in range(chunks):
                slot = columns[:, c : c + 1]
                for k in range(1, SLOTS):
                    place = columns[:, k * chunks + c : k * chunks + c + 1]
                    slot = slot + jnp.where(freq >= place, one_b, zero_b)
                slot = jnp.where(slot >= wrap, slot - wrap, slot)
                code_ref[step, :, c * CHUNK : (c + 1) * CHUNK] = slot
            return carry

        lax.fori_loop(0, count, one, 0)

    def fill_turns():
        shape = (8, nfreq)
        lag = seg * lags + lax.broadcasted_iota(jnp.int32, shape, 0) - LAGS // 2
        freq = lax.broadcasted_iota(jnp.int32, shape, 1)
        cos_own[...], sin_own[...] = turn(lag, freq, 2 * nfreq)

    def pick_lists():
        row_idx = lax.broadcasted_iota(jnp.int32, (rec, rec), 0)
        col_idx = lax.broadcasted_iota(jnp.int32, (rec, rec), 1)
        reg_row = reg_ref[0:1, :]
        reg_col = jnp.sum(jnp.where(row_idx == col_idx, reg_row, 0), axis=1, keepdims=True)
        count_row = jnp.sum(jnp.where(reg_col == reg_row, 1, 0), axis=0, keepdims=True)
        hot = jnp.min(jnp.where(count_row >= cap, reg_row, 1 << 20), axis=1, keepdims=True)
        is_hot_col = jnp.where(reg_col == hot, 1, 0)
        is_hot_row = jnp.where(reg_row == hot, 1, 0)
        rank_row = jnp.sum(jnp.where(row_idx < col_idx, is_hot_col, 0), axis=0, keepdims=True)
        rest_row = col_idx[0:1, :] - rank_row
        hot_ref[0] = jnp.min(jnp.where(count_row >= cap, reg_row, 1 << 20))
        hot_pick = jnp.where(
            (lax.broadcasted_iota(jnp.int32, (hot_pad, rec), 0) == rank_row) & (is_hot_row == 1), 1, 0
        )
        rest_pick = jnp.where(
            (lax.broadcasted_iota(jnp.int32, (rest_pad, rec), 0) == rest_row) & (is_hot_row == 0), 1, 0
        )
        hot_sel[...] = hot_pick.astype(F32)
        rest_sel[...] = rest_pick.astype(F32)
        rest_reg[...] = jnp.broadcast_to(
            jnp.sum(rest_pick * (reg_row + 1), axis=1, keepdims=True) - 1, rest_reg.shape
        )

    def fill_lhs(s, strain_at):
        lists = ((hot_sel, hot_lhs, hot_pad, 0), (rest_sel, rest_lhs, rest_pad, 2 * hot_pad))
        for sel_ref, _, pad, base in lists:
            sel = sel_ref[...].astype(BF16)
            for c in range(2):
                for d in range(2):
                    picked_ref[c, base + d * pad : base + (d + 1) * pad, :] = jnp.dot(
                        sel, strain_at(c, d), preferred_element_type=F32
                    )
        for q in range(width // CHUNK):
            here = slice(q * CHUNK, (q + 1) * CHUNK)
            at = pl.ds(pl.multiple_of(s * width + q * CHUNK, CHUNK), CHUNK)
            column = (s * (width // CHUNK) + q) * 2 * CHUNK
            re_at = pl.ds(pl.multiple_of(column, CHUNK), CHUNK)
            im_at = pl.ds(pl.multiple_of(column + CHUNK, CHUNK), CHUNK)
            for _, lhs_ref, pad, base in lists:
                real_part = picked_ref[0, base : base + 2 * pad, here]
                imag_part = picked_ref[1, base : base + 2 * pad, here]
                for lag in range(lags):
                    cosine = cos_own[lag : lag + 1, at]
                    sine = sin_own[lag : lag + 1, at]
                    rot_re = (real_part * cosine - imag_part * sine).astype(BF16)
                    rot_im = (real_part * sine + imag_part * cosine).astype(BF16)
                    top = (2 * lag) * 2 * pad
                    low = (2 * lag + 1) * 2 * pad
                    lhs_ref[top : top + 2 * pad, re_at] = rot_re
                    lhs_ref[top : top + 2 * pad, im_at] = rot_im
                    lhs_ref[low : low + 2 * pad, re_at] = rot_im
                    lhs_ref[low : low + 2 * pad, im_at] = -rot_re

    def landed_strain(s):
        return lambda c, d: strain_all[s, c, d * rec : (d + 1) * rec, :]

    blocks = total_rows // BLOCK_TPL

    per_part = blocks // (2 * banks)

    def codes_at(of, part):
        return code_ref.at[pl.ds((of * banks + part) * per_part, per_part)]

    def codes(part):
        fill_codes((core * banks + part) * per_part, per_part)
        if part:
            send_codes(part - 1)

    def send_codes(part):
        push(
            lambda: remote(
                codes_at(core, part), codes_at(core, part),
                code_send.at[part], code_recv.at[part], to_near,
            )
        )

    zero = jnp.zeros((), BF16)
    lane_c = lax.broadcasted_iota(jnp.int32, (2 * chunks, 2 * TPL), 1)
    second = jnp.where(lax.broadcasted_iota(jnp.int32, (chunks, 2 * TPL), 1) < TPL, 0.0, 1.0)

    def blocks_of(region):
        ids = [reads_ref[region, i] for i in range(4)]
        return [(b // held_blocks, b % held_blocks, b) for b in ids]

    def region_weights(region, close_ref):
        weight = jnp.zeros((8, 2 * TPL), F32)
        count = jnp.zeros((2 * chunks, 2 * TPL), F32)
        for i, (home, inner, _) in enumerate(blocks_of(region)):
            total = power_all[home, 0]
            for s in range(1, segs):
                total = total + power_all[home, s]
            edges_at = count_ref[home]
            for k in range(held_blocks):
                shift = (i - k + 2 * held_blocks) * BLOCK_TPL % (2 * TPL)
                wanted = jnp.where(lane_c % TPL // BLOCK_TPL == i, inner, held_blocks) == k
                weight = jnp.where(wanted[:8], pltpu.roll(total, shift, 1), weight)
                count = jnp.where(wanted, pltpu.roll(edges_at, shift, 1), count)
        weight = weight + 1e-06
        inv_weight = 1.0 / weight
        first = count[:chunks] + upper.astype(F32)
        last = count[chunks:] + upper.astype(F32)
        for a in range(2):
            close = jnp.zeros((chunks, 2 * TPL), F32)
            for m in range(BINS // SLOTS):
                level = second + float(SLOTS * m + 2 * a)
                close = jnp.where(
                    (level >= first) & (level < last), inv_weight[2 * m + a : 2 * m + a + 1], close
                )
            close_ref[a] = close
        norm = jnp.sum(weight, axis=0, keepdims=True)
        close_ref[2] = jnp.broadcast_to(
            1.0 / (norm + pltpu.roll(norm, TPL, 1)), (chunks, 2 * TPL)
        )

    def half_steps(which, region, lhs_ref, close_ref, acc_ref, sum_ref, total_ref):
        tpl_ref = tpl_own if which == 0 else tpl_far
        blocks = blocks_of(region)
        per_half = chunks // 2
        for step in range(per_half):
            at_step = which * per_half + step
            chunk = at_step + upper * (chunks - 1 - 2 * at_step)
            place = step + upper * (per_half - 1 - 2 * step)
            s, q = place // (width // CHUNK), lax.rem(place, width // CHUNK)
            at = pl.ds(pl.multiple_of(q * CHUNK, CHUNK), CHUNK)
            code_at = pl.ds(pl.multiple_of(chunk * CHUNK, CHUNK), CHUNK)
            lhs_at = pl.ds(pl.multiple_of(chunk * 2 * CHUNK, 2 * CHUNK), 2 * CHUNK)
            code = jnp.concatenate(
                [code_ref[b, :, code_at] for _, _, b in blocks], axis=0
            )
            planes = [
                jnp.concatenate(
                    [tpl_ref[home, s, c, inner, :, at] for home, inner, _ in blocks], axis=0
                )
                for c in range(2)
            ]
            matrix = []
            for slot in range(SLOTS):
                inside = code == jnp.asarray(slot, BF16)
                matrix.append(
                    jnp.concatenate([jnp.where(inside, plane, zero) for plane in planes], axis=1)
                )
            part = lax.dot_general(
                lhs_ref[:, lhs_at], jnp.concatenate(matrix, axis=0), NT, preferred_element_type=F32
            )
            fresh = at_step == 0
            both = part[:, : 2 * TPL] + part[:, 2 * TPL :]
            total_ref[...] = both if fresh else total_ref[...] + both
            for a in range(2):
                close = close_ref[a, pl.ds(chunk, 1), :]
                here = part[:, a * 2 * TPL : (a + 1) * 2 * TPL]
                if not fresh:
                    here = here + acc_ref[a]
                term = here * here * close
                sum_ref[a] = term if fresh else sum_ref[a] + term
                acc_ref[a] = jnp.where(close > 0.0, 0.0, here)

    def finish_list(pad, close_ref, sum_ref, total_ref, store):
        inv_norm = close_ref[2, 0:1, :]
        for lag in range(lags):
            top = lag * 4 * pad
            full = total_ref[top : top + 4 * pad]
            full = full + pltpu.roll(full, TPL, 1)
            energy = sum_ref[0, top : top + 4 * pad] + sum_ref[1, top : top + 4 * pad]
            signal = full * full * inv_norm
            signal = (signal[:pad] + signal[pad : 2 * pad]) + (
                signal[2 * pad : 3 * pad] + signal[3 * pad :]
            )
            energy = (energy[:pad] + energy[pad : 2 * pad]) + (
                energy[2 * pad : 3 * pad] + energy[3 * pad :]
            )
            energy = energy + pltpu.roll(energy, TPL, 1)
            store(lag, signal)
            store(lags + lag, (energy - signal) * (1.0 / (2 * BINS - 2)))

    kept = rest_acc.shape[0]

    def other_region(i):
        return lax.rem(hot_ref[0] + i, banks)

    def hot_half(which):
        if which == 0:
            region_weights(hot_ref[0], hot_close)
        half_steps(which, hot_ref[0], hot_lhs, hot_close, hot_acc, hot_sum, hot_total)

    def rest_half(which, i, at):
        if which == 0:
            region_weights(other_region(i), rest_close.at[at])
        half_steps(
            which, other_region(i), rest_lhs, rest_close.at[at],
            rest_acc.at[at], rest_sum.at[at], rest_total.at[at],
        )

    def rest_done(i, at):
        region = other_region(i)

        def store(where, value):
            at = slice(where * 2 * TPL, (where + 1) * 2 * TPL)
            stat_ref[hot_pad:, at] = jnp.where(rest_reg[...] == region, value, stat_ref[hot_pad:, at])

        finish_list(rest_pad, rest_close.at[at], rest_sum.at[at], rest_total.at[at], store)

    def each_other(body):
        def one(i, carry):
            body(i)
            return carry

        lax.fori_loop(1, banks, one, 0)

    split_rest = kept == banks - 1
    sides = [(side, hops) for hops in range(1, banks) for side in range(2)]
    every = [(0, 0)] + sides
    work = [functools.partial(codes, part) for part in range(banks)]

    def some(count=1):
        for _ in range(min(count, len(work))):
            work.pop(0)()

    pl.semaphore_wait(barrier, met)
    send_own()
    for copy in small:
        copy.wait()
    fill_tables()
    fill_power()
    send_power()
    fill_turns()
    pick_lists()
    fill_lhs(seg, lambda c, d: strain_ref[c, d * rec : (d + 1) * rec, :])
    for hops in range(1, banks):
        for side in range(2):
            relay(Z, side, hops)
        for side in range(2):
            pow_relay(P_Z, side, hops)
        if hops == 1:
            push(lambda: remote(own_plane, there, tpl_send.at[X, 0], tpl_recv.at[X, 0], to_far))
        if hops == 2 or banks == 2:
            landed(strain_all.at[far], str_recv.at[0])
            push(
                lambda: remote(
                    strain_all.at[far], strain_all.at[far], str_send.at[2], str_recv.at[2], to_near
                )
            )
            landed(strain_all.at[near], str_recv.at[1])
            fill_lhs(near, landed_strain(near))
        some()
    push(
        lambda: remote(
            other_plane, there_other, tpl_send.at[X_OTHER, 0], tpl_recv.at[X_OTHER, 0], to_far
        )
    )
    for hops in range(1, banks):
        for side in range(2):
            relay(X, side, hops)
            relay(Y_OWN, side, hops)
        for side in range(2):
            pow_relay(P_X, side, hops)
        some(2 if hops > 1 else 1)
        if hops == 1:
            fill_lhs(far, landed_strain(far))
    some(len(work))
    landed(strain_all.at[far_near], str_recv.at[2])
    fill_lhs(far_near, landed_strain(far_near))
    send_codes(banks - 1)
    pow_relay(P_X)
    for part in range(banks):
        landed(codes_at(core_near, part), code_recv.at[part])
    for side, hops in every:
        for kind in (N_MINE, N_OTHER):
            relay(kind, side, hops)
        for kind in (P_N, P_FAR_N):
            pow_relay(kind, side, hops)
    own_copy.wait()
    own_power.wait()
    relay(X)
    for side in range(2):
        relay(Y_FAR, side, 1)
    hot_half(0)
    for hops in range(2, banks - 1):
        for side in range(2):
            relay(Y_FAR, side, hops)
    if split_rest:
        for i in range(1, banks - 1):
            rest_half(0, i, i - 1)
    relay(X_OTHER)
    if banks > 2:
        for side in range(2):
            relay(Y_FAR, side, banks - 1)
    if split_rest:
        rest_half(0, banks - 1, banks - 2)
    for side, hops in every:
        for kind in (N_FAR_MINE, N_FAR_OTHER):
            relay(kind, side, hops)
    stat_ref[...] = jnp.zeros_like(stat_ref)

    hot_half(1)

    def store_hot(where, value):
        stat_ref[:hot_pad, where * 2 * TPL : (where + 1) * 2 * TPL] = value

    finish_list(hot_pad, hot_close, hot_sum, hot_total, store_hot)
    if split_rest:
        for i in range(1, banks):
            rest_half(1, i, i - 1)
            rest_done(i, i - 1)
    else:

        def whole_region(i):
            rest_half(0, i, 0)
            rest_half(1, i, 0)
            rest_done(i, 0)

        each_other(whole_region)

    placed = lax.dot_general(
        jnp.concatenate([hot_sel[...], rest_sel[...]], axis=0), stat_ref[...], TN,
        precision=HIGH, preferred_element_type=F32,
    )
    for which, out_ref in enumerate((snr_ref, chi_ref)):
        for lag in range(lags):
            at = (which * lags + lag) * 2 * TPL
            out_ref[lag] = placed[:, at : at + TPL]
    for finish in started:
        finish()


def any_phase_tables(seg_count, nfreq):
    period = 2 * nfreq
    lag = np.arange(LAGS, dtype=np.int64) - LAGS // 2
    turns = np.mod(lag[:, None] * np.arange(nfreq, dtype=np.int64)[None, :], period)
    angle = turns * (2.0 * math.pi / period)
    shape = (seg_count, LAGS // seg_count, nfreq)
    return (
        jnp.asarray(np.cos(angle).reshape(shape), F32),
        jnp.asarray(np.sin(angle).reshape(shape), F32),
    )


def any_exchange_kernel(
    cap, rec, hot_pad, rest_pad,
    planes_ref, strain_ref, reg_hbm, edges_hbm, cos_ref, sin_ref,
    tpl_all, power_all, bins_ref, hot_lhs, rest_lhs, hot_sel, rest_sel, rest_reg, hot_out,
    strain_all, power_own, bounds_ref, cos_own, sin_own, reg_ref, edges_ref,
    tpl_send, tpl_recv, pow_send, pow_recv, str_send, str_recv, local_sem,
):
    banks, segs = tpl_all.shape[:2]
    grp, bank, seg = lax.axis_index("grp"), lax.axis_index("bank"), lax.axis_index("seg")
    rows, width = planes_ref.shape[1:]
    nfreq = segs * width
    lags = cos_own.shape[0]
    mesh_id = pl.DeviceIdType.MESH
    half = segs // 2
    far = lax.rem(seg + half, segs)
    near = seg + 1 - 2 * lax.rem(seg, 2)
    far_near = lax.rem(near + half, segs)
    mine, other = grp, 1 - grp
    to_far, to_near, to_twin = {"seg": far}, {"seg": near}, {"grp": other}

    small = [
        pltpu.make_async_copy(cos_ref.at[seg], cos_own, local_sem.at[3]),
        pltpu.make_async_copy(sin_ref.at[seg], sin_own, local_sem.at[4]),
        pltpu.make_async_copy(edges_hbm, edges_ref, local_sem.at[5]),
        pltpu.make_async_copy(reg_hbm, reg_ref, local_sem.at[6]),
    ]
    for copy in small:
        copy.start()
    barrier = pltpu.get_barrier_semaphore()
    for off in range(1, banks):
        pl.semaphore_signal(
            barrier, inc=1, device_id={"bank": lax.rem(bank + off, banks)}, device_id_type=mesh_id
        )
    for where in (to_far, to_near, to_twin):
        pl.semaphore_signal(barrier, inc=1, device_id=where, device_id_type=mesh_id)
    pl.semaphore_wait(barrier, banks + 2)

    started = []

    def push(src, dst, send, recv, where):
        copy = pltpu.make_async_remote_copy(
            src_ref=src, dst_ref=dst, send_sem=send, recv_sem=recv,
            device_id=where, device_id_type=mesh_id,
        )
        copy.start()
        started.append(copy)

    def landed(slot, recv):
        pltpu.make_async_remote_copy(
            src_ref=slot, dst_ref=slot, send_sem=recv, recv_sem=recv,
            device_id=to_near, device_id_type=mesh_id,
        ).wait_recv()

    def source(off):
        return lax.rem(bank - off + banks, banks)

    Z, X, Y_OWN, Y_FAR, N_MINE, N_OTHER, N_FAR_MINE, N_FAR_OTHER = range(8)
    holds = {
        Z: (seg, mine), X: (far, mine), Y_OWN: (seg, other), Y_FAR: (far, other),
        N_MINE: (near, mine), N_OTHER: (near, other),
        N_FAR_MINE: (far_near, mine), N_FAR_OTHER: (far_near, other),
    }
    relays = {
        Z: ((X, to_far), (Y_OWN, to_twin), (N_MINE, to_near)),
        X: ((Y_FAR, to_twin), (N_FAR_MINE, to_near)),
        Y_OWN: ((N_OTHER, to_near),),
        Y_FAR: ((N_FAR_OTHER, to_near),),
    }

    def relay(kind, off):
        place, plane = holds[kind]
        slot = tpl_all.at[source(off), place, plane]
        landed(slot, tpl_recv.at[kind, off])
        for way, where in relays.get(kind, ()):
            push(slot, slot, tpl_send.at[way, off], tpl_recv.at[way, off], where)

    P_Z, P_X, P_N, P_FAR_N = range(4)
    pow_holds = {P_Z: seg, P_X: far, P_N: near, P_FAR_N: far_near}
    pow_relays = {P_Z: ((P_X, to_far), (P_N, to_near)), P_X: ((P_FAR_N, to_near),)}

    def pow_relay(kind, off):
        slot = power_all.at[source(off), pow_holds[kind]]
        landed(slot, pow_recv.at[kind, off])
        for way, where in pow_relays.get(kind, ()):
            push(slot, slot, pow_send.at[way, off], pow_recv.at[way, off], where)

    own_plane = planes_ref.at[mine]
    own_slot = tpl_all.at[bank, seg, mine]
    for off in range(1, banks):
        push(
            own_plane, own_slot, tpl_send.at[Z, off], tpl_recv.at[Z, off],
            {"bank": lax.rem(bank + off, banks)},
        )
    push(own_plane, own_slot, tpl_send.at[X, 0], tpl_recv.at[X, 0], to_far)
    own_strain = strain_all.at[0, seg]
    push(strain_ref, own_strain, str_send.at[0], str_recv.at[0], to_far)
    push(strain_ref, own_strain, str_send.at[1], str_recv.at[1], to_near)
    push(own_plane, own_slot, tpl_send.at[N_MINE, 0], tpl_recv.at[N_MINE, 0], to_near)
    push(
        planes_ref.at[other], tpl_all.at[bank, seg, other],
        tpl_send.at[N_OTHER, 0], tpl_recv.at[N_OTHER, 0], to_near,
    )
    own_copies = [
        pltpu.make_async_copy(planes_ref, tpl_all.at[bank, seg], local_sem.at[0]),
        pltpu.make_async_copy(strain_ref, own_strain, local_sem.at[1]),
    ]
    for copy in own_copies:
        copy.start()
    for copy in small:
        copy.wait()

    total_rows = edges_ref.shape[1]
    eye = jnp.where(
        lax.broadcasted_iota(jnp.int32, (128, 128), 0) == lax.broadcasted_iota(jnp.int32, (128, 128), 1),
        1.0, 0.0,
    )
    for first in range(0, total_rows, 128):
        bounds_ref[first : first + 128, :] = lax.dot_general(
            eye, edges_ref[:, first : first + 128].astype(F32), NT,
            precision=HIGH, preferred_element_type=F32,
        )

    def bin_index(bounds, first):
        freq = (
            lax.broadcasted_iota(jnp.int32, (bounds.shape[0], width), 1) + first
        ).astype(F32)
        bin_of = jnp.zeros((bounds.shape[0], width), F32)
        for level in range(BINS - 1):
            bin_of = bin_of + jnp.where(freq >= bounds[:, level : level + 1], 1.0, 0.0)
        return bin_of

    bin_of = bin_index(bounds_ref[pl.ds(pl.multiple_of(bank * rows, 8), rows), :], seg * width)
    real_part = planes_ref[0].astype(F32)
    imag_part = planes_ref[1].astype(F32)
    squares = real_part * real_part + imag_part * imag_part
    ones = jnp.ones((8, width), F32)
    for pair in range(BINS // 2):
        picked = jnp.concatenate(
            [jnp.where(bin_of == float(2 * pair + p), squares, 0.0) for p in range(2)], axis=0
        )
        line = lax.dot_general(ones, picked, NT, precision=HIGH, preferred_element_type=F32)
        power_own[pair : pair + 1, :] = line[0:1, :]
    own_power = pltpu.make_async_copy(power_own, power_all.at[bank, seg], local_sem.at[2])
    own_power.start()
    for off in range(1, banks):
        push(
            power_own, power_all.at[bank, seg], pow_send.at[P_Z, off], pow_recv.at[P_Z, off],
            {"bank": lax.rem(bank + off, banks)},
        )
    push(power_own, power_all.at[bank, seg], pow_send.at[P_X, 0], pow_recv.at[P_X, 0], to_far)
    push(power_own, power_all.at[bank, seg], pow_send.at[P_N, 0], pow_recv.at[P_N, 0], to_near)

    def fill_bins(first, last):
        def one(step, carry):
            at = pl.multiple_of(step * BLOCK_TPL, BLOCK_TPL)
            bounds = bounds_ref[pl.ds(at, BLOCK_TPL), :]
            for s in range(segs):
                bins_ref[pl.ds(at, BLOCK_TPL), s * width : (s + 1) * width] = bin_index(
                    bounds, s * width
                ).astype(BF16)
            return carry

        lax.fori_loop(first, last, one, 0)

    blocks = total_rows // BLOCK_TPL
    for off in range(banks):
        if off:
            relay(Z, off)
            relay(X, off - 1)
        if off == 1:
            landed(strain_all.at[0, far], str_recv.at[0])
            push(
                strain_all.at[0, far], strain_all.at[0, far], str_send.at[2], str_recv.at[2], to_near
            )
        if off > 1:
            relay(Y_OWN, off - 1)
            relay(Y_FAR, off - 2)
        fill_bins(off * blocks // banks, (off + 1) * blocks // banks)
    relay(X, banks - 1)
    relay(Y_OWN, banks - 1)
    relay(Y_FAR, banks - 2)
    for off in range(1, banks):
        pow_relay(P_Z, off)
    landed(strain_all.at[0, near], str_recv.at[1])
    landed(strain_all.at[0, far_near], str_recv.at[2])
    own_copies[1].wait()

    row_idx = lax.broadcasted_iota(jnp.int32, (rec, rec), 0)
    col_idx = lax.broadcasted_iota(jnp.int32, (rec, rec), 1)
    reg_row = reg_ref[0:1, :]
    reg_col = jnp.sum(jnp.where(row_idx == col_idx, reg_row, 0), axis=1, keepdims=True)
    count_row = jnp.sum(jnp.where(reg_col == reg_row, 1, 0), axis=0, keepdims=True)
    hot = jnp.min(jnp.where(count_row >= cap, reg_row, 1 << 20), axis=1, keepdims=True)
    is_hot_col = jnp.where(reg_col == hot, 1, 0)
    is_hot_row = jnp.where(reg_row == hot, 1, 0)
    rank_row = jnp.sum(jnp.where(row_idx < col_idx, is_hot_col, 0), axis=0, keepdims=True)
    rest_row = col_idx[0:1, :] - rank_row
    hot_out[0] = jnp.min(jnp.where(count_row >= cap, reg_row, 1 << 20))
    hot_pick = jnp.where(
        (lax.broadcasted_iota(jnp.int32, (hot_pad, rec), 0) == rank_row) & (is_hot_row == 1), 1, 0
    )
    rest_pick = jnp.where(
        (lax.broadcasted_iota(jnp.int32, (rest_pad, rec), 0) == rest_row) & (is_hot_row == 0), 1, 0
    )
    hot_sel[...] = hot_pick.astype(F32)
    rest_sel[...] = rest_pick.astype(F32)
    rest_reg[...] = jnp.broadcast_to(
        jnp.sum(rest_pick * (reg_row + 1), axis=1, keepdims=True) - 1, rest_reg.shape
    )
    lists = ((hot_pick, hot_lhs, hot_pad), (rest_pick, rest_lhs, rest_pad))
    for s in range(segs):
        if s == segs // 2:
            relay(Y_FAR, banks - 1)
            for off in range(banks):
                pow_relay(P_X, off)
        for pick, lhs_ref, pad in lists:
            sel = pick.astype(F32).astype(BF16)
            at = slice(s * width, (s + 1) * width)
            at_im = slice(nfreq + s * width, nfreq + (s + 1) * width)
            parts = []
            for c in range(2):
                parts.append(
                    jnp.concatenate(
                        [
                            jnp.dot(
                                sel,
                                strain_all[0, s, c, d * rec : (d + 1) * rec, :],
                                preferred_element_type=F32,
                            )
                            for d in range(2)
                        ],
                        axis=0,
                    )
                )
            real_part, imag_part = parts
            for lag in range(lags):
                cosine = cos_own[lag : lag + 1, at]
                sine = sin_own[lag : lag + 1, at]
                rot_re = (real_part * cosine - imag_part * sine).astype(BF16)
                rot_im = (real_part * sine + imag_part * cosine).astype(BF16)
                top = (2 * lag) * 2 * pad
                low = (2 * lag + 1) * 2 * pad
                lhs_ref[top : top + 2 * pad, at] = rot_re
                lhs_ref[top : top + 2 * pad, at_im] = rot_im
                lhs_ref[low : low + 2 * pad, at] = rot_im
                lhs_ref[low : low + 2 * pad, at_im] = -rot_re
    for off in range(banks):
        for kind in (N_MINE, N_OTHER, N_FAR_MINE, N_FAR_OTHER):
            relay(kind, off)
        for kind in (P_N, P_FAR_N):
            pow_relay(kind, off)
    own_copies[0].wait()
    own_power.wait()
    for copy in started:
        copy.wait_send()


def any_follow_kernel(
    held_blocks,
    reads_ref, hot_ref, hot_lhs, rest_lhs, hot_sel, rest_sel, rest_reg,
    t0_ref, t1_ref, t2_ref, t3_ref, b0_ref, b1_ref, b2_ref, b3_ref, power_ref,
    snr_ref, chi_ref,
    tmat, z_ref, hot_stat, rest_stat,
):
    region = pl.program_id(0)
    segs, _, _, width = t0_ref.shape[1:]
    nfreq = segs * width
    lags = snr_ref.shape[0]
    hot_pad, rest_pad = hot_sel.shape[0], rest_sel.shape[0]
    tpl_refs = (t0_ref, t1_ref, t2_ref, t3_ref)
    bin_refs = (b0_ref, b1_ref, b2_ref, b3_ref)

    @pl.when(region == 0)
    def prepare():
        hot_stat[...] = jnp.zeros_like(hot_stat)
        rest_stat[...] = jnp.zeros_like(rest_stat)

    lane = lax.broadcasted_iota(jnp.int32, (8, 2 * TPL), 1)
    weight = jnp.zeros((8, 2 * TPL), F32)
    for i in range(4):
        block_id = reads_ref[region, i]
        bank, inner = block_id // held_blocks, block_id % held_blocks
        total = power_ref[bank, 0]
        for s in range(1, segs):
            total = total + power_ref[bank, s]
        shift = (i - inner + 2 * held_blocks) * BLOCK_TPL % (2 * TPL)
        moved = pltpu.roll(total, shift, 1)
        weight = jnp.where((lane % TPL) // BLOCK_TPL == i, moved, weight)
    weight = weight + 1e-06
    norm = jnp.sum(weight, axis=0, keepdims=True)
    norm = norm + pltpu.roll(norm, TPL, 1)
    inv_norm = 1.0 / norm
    share = weight * inv_norm
    inv_weight = 1.0 / weight

    def run(lhs_ref, pad, store):
        rows = lhs_ref.shape[0]
        group = 4
        for q in range(BINS // group):
            for g in range(group):
                level = jnp.asarray(q * group + g, BF16)
                for i in range(4):
                    at_row = slice(g * TPL + i * BLOCK_TPL, g * TPL + (i + 1) * BLOCK_TPL)
                    for s in range(segs):
                        inside = (
                            bin_refs[i][:, s * width : (s + 1) * width] == level
                        )
                        for c in range(2):
                            at = slice(c * nfreq + s * width, c * nfreq + (s + 1) * width)
                            tmat[q, at_row, at] = jnp.where(
                                inside, tpl_refs[i][0, s, c], jnp.zeros((), BF16)
                            )
            z_ref[0:rows, q * group * TPL : (q + 1) * group * TPL] = lax.dot_general(
                lhs_ref[...], tmat[q], NT, preferred_element_type=F32
            )
        for lag in range(lags):
            top = (2 * lag) * 2 * pad
            low = (2 * lag + 1) * 2 * pad
            zr = [z_ref[top : top + 2 * pad, j * 128 : (j + 1) * 128] for j in range(BINS // 2)]
            zi = [z_ref[low : low + 2 * pad, j * 128 : (j + 1) * 128] for j in range(BINS // 2)]
            full_re = functools.reduce(jnp.add, zr)
            full_im = functools.reduce(jnp.add, zi)
            full_re = full_re + pltpu.roll(full_re, TPL, 1)
            full_im = full_im + pltpu.roll(full_im, TPL, 1)
            signal = (full_re * full_re + full_im * full_im) * inv_norm
            chi = jnp.zeros_like(signal)
            for j in range(BINS // 2):
                diff_re = zr[j] - share[j : j + 1] * full_re
                diff_im = zi[j] - share[j : j + 1] * full_im
                chi = chi + (diff_re * diff_re + diff_im * diff_im) * inv_weight[j : j + 1]
            chi = (chi + pltpu.roll(chi, TPL, 1)) * (1.0 / (2 * BINS - 2))
            store(lag, signal[:pad] + signal[pad:])
            store(lags + lag, chi[:pad] + chi[pad:])

    def store_hot(at, value):
        hot_stat[at] = value

    def store_rest(at, value):
        rest_stat[at] = jnp.where(rest_reg[...] == region, value, rest_stat[at])

    @pl.when(region == hot_ref[0])
    def on_hot():
        run(hot_lhs, hot_pad, store_hot)

    @pl.when(region != hot_ref[0])
    def on_rest():
        run(rest_lhs, rest_pad, store_rest)

    @pl.when(region == pl.num_programs(0) - 1)
    def finish():
        for which, out_ref in enumerate((snr_ref, chi_ref)):
            for lag in range(lags):
                at = which * lags + lag
                value = lax.dot_general(
                    hot_sel[...], hot_stat[at], TN, precision=HIGH, preferred_element_type=F32
                ) + lax.dot_general(
                    rest_sel[...], rest_stat[at], TN, precision=HIGH, preferred_element_type=F32
                )
                out_ref[lag] = value[:, :TPL]


def any_per_device(strain, region_of, templates, reads, edges):
    region_count = lax.axis_size("bank")
    seg_count = lax.axis_size("seg")
    rec, _, _, width = strain.shape
    nfreq = width * seg_count
    held_rows = templates.shape[0]
    held_blocks = held_rows // BLOCK_TPL
    cap = 3 * rec // region_count
    hot_pad, rest_pad = round_up(cap, 8), round_up(rec - cap, 8)
    lags = LAGS // seg_count
    planes = jnp.transpose(templates, (1, 0, 2))
    strain_planes = jnp.transpose(strain, (2, 1, 0, 3)).reshape(2, 2 * rec, width)
    cos_tab, sin_tab = any_phase_tables(seg_count, nfreq)
    reg = region_of.reshape(1, rec)
    rows_hot, rows_rest = lags * 4 * hot_pad, lags * 4 * rest_pad
    vmem = pl.BlockSpec(memory_space=pltpu.VMEM)
    anyw = pl.BlockSpec(memory_space=pl.ANY)
    hbm = pl.BlockSpec(memory_space=pltpu.HBM)
    total_rows = edges.shape[0]

    def struct(shape, dtype):
        return jax.ShapeDtypeStruct(shape, dtype)

    dma = pltpu.SemaphoreType.DMA
    exchanged = pl.pallas_call(
        functools.partial(any_exchange_kernel, cap, rec, hot_pad, rest_pad),
        out_shape=(
            struct((region_count, seg_count) + planes.shape, BF16),
            struct((region_count, seg_count, BINS // 2, 2 * TPL), F32),
            struct((total_rows, nfreq), BF16),
            struct((rows_hot, 2 * nfreq), BF16),
            struct((rows_rest, 2 * nfreq), BF16),
            struct((hot_pad, rec), F32),
            struct((rest_pad, rec), F32),
            struct((rest_pad, 2 * TPL), jnp.int32),
            struct((1,), jnp.int32),
        ),
        in_specs=[vmem, vmem, hbm, hbm, hbm, hbm],
        out_specs=(anyw, anyw) + (vmem,) * 6 + (pl.BlockSpec(memory_space=pltpu.SMEM),),
        scratch_shapes=[
            pltpu.VMEM((1, seg_count) + strain_planes.shape, BF16),
            pltpu.VMEM((BINS // 2, 2 * TPL), F32),
            pltpu.VMEM((total_rows, BINS - 1), F32),
            pltpu.VMEM((lags, nfreq), F32),
            pltpu.VMEM((lags, nfreq), F32),
            pltpu.VMEM((1, rec), jnp.int32),
            pltpu.VMEM((BINS - 1, total_rows), jnp.int32),
            dma((8, region_count)),
            dma((8, region_count)),
            dma((4, region_count)),
            dma((4, region_count)),
            dma((3,)),
            dma((3,)),
            dma((7,)),
        ],
        compiler_params=pltpu.CompilerParams(
            collective_id=1, has_side_effects=True, vmem_limit_bytes=50 * 1024 * 1024
        ),
        name="any_exchange",
    )(planes, strain_planes, reg, edges.T, cos_tab, sin_tab)
    tpl_all, power_all, bins_all, hot_lhs, rest_lhs, hot_sel, rest_sel, rest_reg, hot = exchanged

    def tpl_spec(i):
        def index(r, reads_ref, hot_ref):
            block_id = reads_ref[r, i]
            return (block_id // held_blocks, 0, 0, block_id % held_blocks, 0)

        return pl.BlockSpec((1, seg_count, 2, BLOCK_TPL, width), index)

    def bin_spec(i):
        return pl.BlockSpec((BLOCK_TPL, nfreq), lambda r, reads_ref, hot_ref: (reads_ref[r, i], 0))

    def whole(array):
        return pl.BlockSpec(
            array.shape, lambda r, a, b: (0,) * array.ndim, pipeline_mode=pl.Buffered(1)
        )

    out = struct((lags, rec, TPL), F32)
    resident = (hot_lhs, rest_lhs, hot_sel, rest_sel, rest_reg)
    snr, chi = pl.pallas_call(
        functools.partial(any_follow_kernel, held_blocks),
        out_shape=(out, out),
        grid_spec=pltpu.PrefetchScalarGridSpec(
            num_scalar_prefetch=2,
            grid=(region_count,),
            in_specs=[whole(x) for x in resident]
            + [tpl_spec(i) for i in range(4)]
            + [bin_spec(i) for i in range(4)]
            + [whole(power_all)],
            out_specs=(pl.BlockSpec(out.shape, lambda r, a, b: (0, 0, 0)),) * 2,
            scratch_shapes=[
                pltpu.VMEM((4, 4 * TPL, 2 * nfreq), BF16),
                pltpu.VMEM((max(rows_hot, rows_rest), BINS * TPL), F32),
                pltpu.VMEM((2 * lags, hot_pad, 2 * TPL), F32),
                pltpu.VMEM((2 * lags, rest_pad, 2 * TPL), F32),
            ],
        ),
        compiler_params=pltpu.CompilerParams(
            dimension_semantics=("arbitrary",), vmem_limit_bytes=50 * 1024 * 1024
        ),
        name="any_follow",
    )(
        reads, hot, *resident, tpl_all, tpl_all, tpl_all, tpl_all,
        bins_all, bins_all, bins_all, bins_all, power_all,
    )
    return jnp.transpose(snr, (0, 2, 1)), jnp.transpose(chi, (0, 2, 1))


def per_device(strain, region_of, templates, reads, edges):
    region_count = lax.axis_size("bank")
    seg_count = lax.axis_size("seg")
    rec, _, _, width = strain.shape
    nfreq = width * seg_count
    held_rows = templates.shape[0]
    held_blocks = held_rows // BLOCK_TPL
    cap = 3 * rec // region_count
    hot_pad, rest_pad = round_up(cap, 8), round_up(rec - cap, 8)
    lags = LAGS // seg_count
    planes = jnp.transpose(templates, (1, 0, 2)).reshape(2, held_blocks, BLOCK_TPL, width)
    strain_planes = jnp.transpose(strain, (2, 1, 0, 3)).reshape(2, 2 * rec, width)
    reg = region_of.reshape(1, rec)
    rows_hot, rows_rest = lags * 4 * hot_pad, lags * 4 * rest_pad
    vmem = pl.BlockSpec(memory_space=pltpu.VMEM)
    hbm = pl.BlockSpec(memory_space=pltpu.HBM)
    smem = pl.BlockSpec(memory_space=pltpu.SMEM)
    total_rows = edges.shape[0]
    chunks = nfreq // CHUNK
    kept = region_count - 1 if region_count <= 4 else 1

    def struct(shape, dtype):
        return jax.ShapeDtypeStruct(shape, dtype)

    dma = pltpu.SemaphoreType.DMA
    half_shape = (region_count, seg_count // 2) + planes.shape
    out = struct((lags, rec, TPL), F32)
    snr, chi, most = pl.pallas_call(
        functools.partial(follow_up_kernel, cap, rec, hot_pad, rest_pad, held_blocks),
        out_shape=(out, out, struct((1,), jnp.int32)),
        in_specs=[vmem, vmem, hbm, hbm, hbm],
        out_specs=(vmem, vmem, smem),
        scratch_shapes=[
            pltpu.VMEM(half_shape, BF16),
            pltpu.VMEM(half_shape, BF16),
            pltpu.VMEM((region_count, seg_count, BINS // 2, 2 * TPL), F32),
            pltpu.VMEM((total_rows // BLOCK_TPL, BLOCK_TPL, nfreq), BF16),
            pltpu.VMEM((total_rows, 2 * TPL), F32),
            pltpu.VMEM((region_count, 2 * chunks, 2 * TPL), F32),
            pltpu.VMEM((rows_hot, 2 * nfreq), BF16),
            pltpu.VMEM((rows_rest, 2 * nfreq), BF16),
            pltpu.VMEM((hot_pad, rec), F32),
            pltpu.VMEM((rest_pad, rec), F32),
            pltpu.VMEM((rest_pad, 2 * TPL), jnp.int32),
            pltpu.SMEM((1,), jnp.int32),
            pltpu.VMEM((seg_count,) + strain_planes.shape, BF16),
            pltpu.VMEM((BINS // 2, 2 * TPL), F32),
            pltpu.VMEM((total_rows, 2 * TPL), BF16),
            pltpu.VMEM((8, nfreq), F32),
            pltpu.VMEM((8, nfreq), F32),
            pltpu.VMEM((2, 2 * (hot_pad + rest_pad), width), F32),
            pltpu.VMEM((1, rec), jnp.int32),
            pltpu.VMEM((BINS - 1, total_rows), jnp.int32),
            pltpu.SMEM(reads.shape, jnp.int32),
            pltpu.VMEM((3, chunks, 2 * TPL), F32),
            pltpu.VMEM((kept, 3, chunks, 2 * TPL), F32),
            pltpu.VMEM((2, rows_hot, 2 * TPL), F32),
            pltpu.VMEM((2, rows_hot, 2 * TPL), F32),
            pltpu.VMEM((rows_hot, 2 * TPL), F32),
            pltpu.VMEM((kept, 2, rows_rest, 2 * TPL), F32),
            pltpu.VMEM((kept, 2, rows_rest, 2 * TPL), F32),
            pltpu.VMEM((kept, rows_rest, 2 * TPL), F32),
            pltpu.VMEM((hot_pad + rest_pad, 2 * lags * 2 * TPL), F32),
            dma((9, 2 * region_count)),
            dma((9, 2 * region_count)),
            dma((4, 2 * region_count)),
            dma((4, 2 * region_count)),
            dma((3,)),
            dma((3,)),
            dma((region_count,)),
            dma((region_count,)),
            dma((6,)),
        ],
        compiler_params=pltpu.CompilerParams(
            collective_id=0, has_side_effects=True, vmem_limit_bytes=48 * 1024 * 1024
        ),
        name="follow_up",
    )(planes, strain_planes, reg, edges.T, reads)
    done = jnp.transpose(snr, (0, 2, 1)), jnp.transpose(chi, (0, 2, 1))
    return lax.cond(
        most[0] < SLOTS, lambda: done,
        lambda: any_per_device(strain, region_of, templates, reads, edges),
    )


def solution(mesh):
    placed = (
        P(("grp", "bank"), None, None, "seg"),
        P(("grp", "bank")),
        P("bank", None, "seg"),
        P(),
        P(),
    )
    return jax.shard_map(
        per_device,
        mesh=mesh,
        in_specs=placed,
        out_specs=(P("seg", None, ("grp", "bank")), P("seg", None, ("grp", "bank"))),
        check_vma=False,
    )
```

```python
import functools
import math

import jax
import jax.numpy as jnp
import numpy as np
from jax import lax
from jax.experimental import pallas as pl
from jax.experimental.pallas import tpu as pltpu
from jax.sharding import PartitionSpec as P

BLOCK_TPL = 16
BINS = 16
LAGS = 16
TPL = 64
CHUNK = 128
SLOTS = 4
F32 = jnp.float32
BF16 = jnp.bfloat16
NT = (((1,), (1,)), ((), ()))
TN = (((0,), (0,)), ((), ()))
HIGH = lax.Precision.HIGHEST


def round_up(value, step):
    return -(-value // step) * step


def turn(lag, freq, period):
    quarter = period // 4
    moved = (freq * lag + quarter // 2) & (period - 1)
    quadrant = moved // quarter
    angle = (moved % quarter - quarter // 2).astype(F32) * (2.0 * math.pi / period)
    sq = angle * angle
    sine = angle * (1.0 + sq * (-1.0 / 6 + sq * (1.0 / 120 + sq * (-1.0 / 5040 + sq * (1.0 / 362880)))))
    cosine = 1.0 + sq * (-0.5 + sq * (1.0 / 24 + sq * (-1.0 / 720 + sq * (1.0 / 40320))))
    odd = quadrant % 2 == 1
    big, small = jnp.where(odd, sine, cosine), jnp.where(odd, cosine, sine)
    cos_out = jnp.where((quadrant == 1) | (quadrant == 2), -big, big)
    sin_out = jnp.where(quadrant >= 2, -small, small)
    return cos_out, sin_out


def follow_up_kernel(
    cap, rec, hot_pad, rest_pad, held_blocks,
    planes_ref, strain_ref, reg_hbm, edges_hbm, reads_hbm,
    snr_ref, chi_ref, most_ref,
    tpl_own, tpl_far, power_all, code_ref, bounds_ref, count_ref,
    hot_lhs, rest_lhs, hot_sel, rest_sel, rest_reg, hot_ref,
    strain_all, power_own, column_ref, cos_own, sin_own, picked_ref, reg_ref, edges_ref, reads_ref,
    hot_close, rest_close, hot_acc, hot_sum, hot_total, rest_acc, rest_sum, rest_total,
    stat_ref,
    tpl_send, tpl_recv, pow_send, pow_recv, str_send, str_recv, code_send, code_recv, local_sem,
):
    banks, segs = power_all.shape[:2]
    grp, bank, seg = lax.axis_index("grp"), lax.axis_index("bank"), lax.axis_index("seg")
    width = planes_ref.shape[3]
    rows = held_blocks * BLOCK_TPL
    nfreq = segs * width
    lags = LAGS // segs
    mesh_id = pl.DeviceIdType.MESH
    half = segs // 2
    far = lax.rem(seg + half, segs)
    near = seg + 1 - 2 * lax.rem(seg, 2)
    far_near = lax.rem(near + half, segs)
    mine, other = grp, 1 - grp
    to_far, to_near, to_twin = {"seg": far}, {"seg": near}, {"grp": other}

    up_ok, down_ok = bank < banks - 1, bank > 0

    small = [
        pltpu.make_async_copy(edges_hbm, edges_ref, local_sem.at[3]),
        pltpu.make_async_copy(reg_hbm, reg_ref, local_sem.at[4]),
        pltpu.make_async_copy(reads_hbm, reads_ref, local_sem.at[5]),
    ]
    for copy in small:
        copy.start()
    barrier = pltpu.get_barrier_semaphore()

    def greet(where):
        pl.semaphore_signal(barrier, inc=1, device_id=where, device_id_type=mesh_id)

    for where in (to_far, to_near, to_twin):
        greet(where)
    pl.when(up_ok)(lambda: greet({"bank": bank + 1}))
    pl.when(down_ok)(lambda: greet({"bank": bank - 1}))
    met = 3 + lax.min(bank, 1) + lax.min(banks - 1 - bank, 1)
    started = []

    def push(describe, condition=None):
        def start():
            describe().start()

        def finish():
            describe().wait_send()

        if condition is None:
            start()
            started.append(finish)
        else:
            pl.when(condition)(start)
            started.append(lambda: pl.when(condition)(finish))

    def remote(src, dst, send, recv, where):
        return pltpu.make_async_remote_copy(
            src_ref=src, dst_ref=dst, send_sem=send, recv_sem=recv,
            device_id=where, device_id_type=mesh_id,
        )

    def landed(slot, recv):
        remote(slot, slot, recv, recv, to_near).wait_recv()

    def source(side, hops):
        return bank - hops if side == 0 else bank + hops

    def present(side, hops):
        return bank >= hops if side == 0 else bank + hops <= banks - 1

    def number(side, hops):
        return side * banks + hops

    def onward(side):
        return (up_ok, {"bank": bank + 1}) if side == 0 else (down_ok, {"bank": bank - 1})

    Z, X, X_OTHER, Y_OWN, Y_FAR, N_MINE, N_OTHER, N_FAR_MINE, N_FAR_OTHER = range(9)
    core, core_near = lax.rem(seg, half), lax.rem(near, half)
    holds = {
        Z: (tpl_own, core, mine), X: (tpl_far, core, mine), X_OTHER: (tpl_far, core, other),
        Y_OWN: (tpl_own, core, other), Y_FAR: (tpl_far, core, other),
        N_MINE: (tpl_own, core_near, mine), N_OTHER: (tpl_own, core_near, other),
        N_FAR_MINE: (tpl_far, core_near, mine), N_FAR_OTHER: (tpl_far, core_near, other),
    }
    relays = {
        Z: ((Y_OWN, to_twin), (X, to_far), (N_MINE, to_near)),
        X: ((Y_FAR, to_twin), (N_FAR_MINE, to_near)),
        X_OTHER: ((N_FAR_OTHER, to_near),),
        Y_OWN: ((N_OTHER, to_near),),
        Y_FAR: ((N_FAR_OTHER, to_near),),
    }
    P_Z, P_X, P_N, P_FAR_N = range(4)
    pow_holds = {P_Z: seg, P_X: far, P_N: near, P_FAR_N: far_near}
    pow_relays = {P_Z: ((P_X, to_far), (P_N, to_near)), P_X: ((P_FAR_N, to_near),)}

    def landing(way, kind, side, hops):
        ref, place, plane = holds[kind]
        if way in (X, X_OTHER):
            ref = tpl_far
        return ref.at[source(side, hops), place, plane]

    def tpl_slot(kind, side, hops):
        ref, place, plane = holds[kind]
        return ref.at[source(side, hops), place, plane]

    def pow_slot(kind, side, hops):
        return power_all.at[source(side, hops), pow_holds[kind]]

    def relay(kind, side=0, hops=0, table=(tpl_slot, tpl_send, tpl_recv, relays, Z)):
        slot, send, recv, ways, first = table
        at = number(side, hops)
        here = present(side, hops) if hops else None

        def wait():
            landed(slot(kind, side, hops), recv.at[kind, at])

        wait() if here is None else pl.when(here)(wait)
        if kind == first:
            more, where = onward(side)
            push(
                lambda: remote(
                    slot(kind, side, hops), slot(kind, side, hops),
                    send.at[kind, at], recv.at[kind, at + 1], where,
                ),
                here & more,
            )
        for way, where in ways.get(kind, ()):
            if hops or way != Y_FAR or slot is pow_slot:
                push(
                    lambda way=way, where=where: remote(
                        slot(kind, side, hops),
                        slot(kind, side, hops) if slot is pow_slot else landing(way, kind, side, hops),
                        send.at[way, at], recv.at[way, at], where,
                    ),
                    here,
                )

    def pow_relay(kind, side=0, hops=0):
        relay(kind, side, hops, (pow_slot, pow_send, pow_recv, pow_relays, P_Z))

    own_plane, other_plane = planes_ref.at[mine], planes_ref.at[other]
    own_slot, other_slot = tpl_own.at[bank, core, mine], tpl_own.at[bank, core, other]
    there, there_other = tpl_far.at[bank, core, mine], tpl_far.at[bank, core, other]
    own_strain = strain_all.at[seg]

    def both_ways(src, dst, send, recv, kind):
        for side in range(2):
            more, where = onward(side)
            push(
                lambda side=side, where=where: remote(
                    src, dst, send.at[kind, side * banks], recv.at[kind, number(side, 1)], where
                ),
                more,
            )

    own_copy = pltpu.make_async_copy(planes_ref, tpl_own.at[bank, core], local_sem.at[0])
    own_copy.start()

    def send_own():
        both_ways(own_plane, own_slot, tpl_send, tpl_recv, Z)
        push(lambda: remote(strain_ref, own_strain, str_send.at[0], str_recv.at[0], to_far))
        push(lambda: remote(strain_ref, own_strain, str_send.at[1], str_recv.at[1], to_near))
        push(lambda: remote(own_plane, own_slot, tpl_send.at[N_MINE, 0], tpl_recv.at[N_MINE, 0], to_near))
        push(lambda: remote(other_plane, other_slot, tpl_send.at[N_OTHER, 0], tpl_recv.at[N_OTHER, 0], to_near))


    total_rows = edges_ref.shape[1]
    upper = seg // half
    chunks = nfreq // CHUNK

    def fill_tables():
        eye = jnp.where(
            lax.broadcasted_iota(jnp.int32, (2 * TPL, 2 * TPL), 0)
            == lax.broadcasted_iota(jnp.int32, (2 * TPL, 2 * TPL), 1),
            1.0, 0.0,
        ).astype(BF16)
        row = lax.broadcasted_iota(jnp.int32, (2 * chunks, 2 * TPL), 0)
        mark = (jnp.where(row < chunks, row, row - chunks + 1) * CHUNK).astype(F32)
        low_lane = lax.broadcasted_iota(jnp.int32, (2 * chunks, 2 * TPL), 1) < TPL
        most = jnp.zeros((chunks, 2 * TPL), F32)
        down = upper.astype(F32)

        def turned(table):
            return lax.dot_general(eye, table.astype(BF16), NT, preferred_element_type=F32)

        for pair in range(total_rows // (2 * TPL)):
            group = slice(pair * 2 * TPL, (pair + 1) * 2 * TPL)
            edges = edges_ref[:, group].astype(F32)
            coarse = jnp.floor(edges * (1.0 / 16))
            bounds_ref[group, : BINS - 1] = turned(coarse) * 16.0 + turned(edges - coarse * 16.0)
            count = jnp.zeros((2 * chunks, 2 * TPL), F32)
            for level in range(BINS - 1):
                count = count + jnp.where(edges[level : level + 1] <= mark, 1.0, 0.0)
            first = count[:chunks]
            most = jnp.maximum(most, count[chunks:] - first)
            places = [first - SLOTS * jnp.floor(first * (1.0 / SLOTS))]
            for k in range(SLOTS - 1):
                place = jnp.full((chunks, 2 * TPL), float(CHUNK), F32)
                for level in range(k, BINS - 1):
                    place = jnp.where(
                        first == float(level - k),
                        jnp.minimum(edges[level : level + 1] - mark[:chunks], float(CHUNK)), place,
                    )
                places.append(place)
            column_ref[group, : SLOTS * chunks] = turned(jnp.concatenate(places, axis=0)).astype(BF16)
            count = jnp.where(row == 2 * chunks - 1, BINS - down, count)
            count = jnp.where(row == 0, -down, count)
            moved = pltpu.roll(count, TPL, 1)
            count_ref[2 * pair] = jnp.where(low_lane, count, moved)
            count_ref[2 * pair + 1] = jnp.where(low_lane, moved, count)
        most_ref[0] = jnp.max(most.astype(jnp.int32))

    def bin_index(bounds, first):
        freq = (
            lax.broadcasted_iota(jnp.int32, (bounds.shape[0], width), 1) + first
        ).astype(F32)
        bin_of = jnp.zeros((bounds.shape[0], width), F32)
        for level in range(BINS - 1):
            bin_of = jnp.where(freq >= bounds[:, level : level + 1], level + 1.0, bin_of)
        return bin_of

    own_power = pltpu.make_async_copy(power_own, power_all.at[bank, seg], local_sem.at[2])

    def fill_power():
        bin_of = bin_index(
            bounds_ref[pl.ds(pl.multiple_of(bank * rows, 8), rows), : BINS - 1], seg * width
        )
        real_part = planes_ref[0].reshape(rows, width).astype(F32)
        imag_part = planes_ref[1].reshape(rows, width).astype(F32)
        squares = real_part * real_part + imag_part * imag_part
        ones = jnp.ones((8, 3 * CHUNK), BF16)
        for pair in range(BINS // 2):
            sums = []
            for p in range(2):
                picked = jnp.where(bin_of == float(2 * pair + p), squares, 0.0)
                sums.append(
                    functools.reduce(
                        jnp.add,
                        [picked[:, c * CHUNK : (c + 1) * CHUNK] for c in range(width // CHUNK)],
                    )
                )
            value = jnp.concatenate(sums, axis=0)
            high = value.astype(BF16)
            left = value - high.astype(F32)
            middle = left.astype(BF16)
            low = (left - middle.astype(F32)).astype(BF16)
            line = lax.dot_general(
                ones, jnp.concatenate([high, middle, low], axis=1), NT, preferred_element_type=F32
            )
            power_own[pair : pair + 1, :] = line[0:1, :]

    def send_power():
        own_power.start()
        slot = power_all.at[bank, seg]
        both_ways(power_own, slot, pow_send, pow_recv, P_Z)
        push(lambda: remote(power_own, slot, pow_send.at[P_X, 0], pow_recv.at[P_X, 0], to_far))
        push(lambda: remote(power_own, slot, pow_send.at[P_N, 0], pow_recv.at[P_N, 0], to_near))

    def fill_codes(first, count):
        freq = lax.broadcasted_iota(jnp.int32, (BLOCK_TPL, CHUNK), 1).astype(F32).astype(BF16)
        one_b, zero_b, wrap = (jnp.asarray(v, BF16) for v in (1.0, 0.0, float(SLOTS)))

        def one(step, carry):
            step = first + step
            at = pl.multiple_of(step * BLOCK_TPL, BLOCK_TPL)
            columns = column_ref[pl.ds(at, BLOCK_TPL), : SLOTS * chunks]
            for c in range(chunks):
                slot = columns[:, c : c + 1]
                for k in range(1, SLOTS):
                    place = columns[:, k * chunks + c : k * chunks + c + 1]
                    slot = slot + jnp.where(freq >= place, one_b, zero_b)
                slot = jnp.where(slot >= wrap, slot - wrap, slot)
                code_ref[step, :, c * CHUNK : (c + 1) * CHUNK] = slot
            return carry

        lax.fori_loop(0, count, one, 0)

    def fill_turns():
        shape = (8, nfreq)
        lag = seg * lags + lax.broadcasted_iota(jnp.int32, shape, 0) - LAGS // 2
        freq = lax.broadcasted_iota(jnp.int32, shape, 1)
        cos_own[...], sin_own[...] = turn(lag, freq, 2 * nfreq)

    def pick_lists():
        row_idx = lax.broadcasted_iota(jnp.int32, (rec, rec), 0)
        col_idx = lax.broadcasted_iota(jnp.int32, (rec, rec), 1)
        reg_row = reg_ref[0:1, :]
        reg_col = jnp.sum(jnp.where(row_idx == col_idx, reg_row, 0), axis=1, keepdims=True)
        count_row = jnp.sum(jnp.where(reg_col == reg_row, 1, 0), axis=0, keepdims=True)
        hot = jnp.min(jnp.where(count_row >= cap, reg_row, 1 << 20), axis=1, keepdims=True)
        is_hot_col = jnp.where(reg_col == hot, 1, 0)
        is_hot_row = jnp.where(reg_row == hot, 1, 0)
        rank_row = jnp.sum(jnp.where(row_idx < col_idx, is_hot_col, 0), axis=0, keepdims=True)
        rest_row = col_idx[0:1, :] - rank_row
        hot_ref[0] = jnp.min(jnp.where(count_row >= cap, reg_row, 1 << 20))
        hot_pick = jnp.where(
            (lax.broadcasted_iota(jnp.int32, (hot_pad, rec), 0) == rank_row) & (is_hot_row == 1), 1, 0
        )
        rest_pick = jnp.where(
            (lax.broadcasted_iota(jnp.int32, (rest_pad, rec), 0) == rest_row) & (is_hot_row == 0), 1, 0
        )
        hot_sel[...] = hot_pick.astype(F32)
        rest_sel[...] = rest_pick.astype(F32)
        rest_reg[...] = jnp.broadcast_to(
            jnp.sum(rest_pick * (reg_row + 1), axis=1, keepdims=True) - 1, rest_reg.shape
        )

    def fill_lhs(s, strain_at):
        lists = ((hot_sel, hot_lhs, hot_pad, 0), (rest_sel, rest_lhs, rest_pad, 2 * hot_pad))
        for sel_ref, _, pad, base in lists:
            sel = sel_ref[...].astype(BF16)
            for c in range(2):
                for d in range(2):
                    picked_ref[c, base + d * pad : base + (d + 1) * pad, :] = jnp.dot(
                        sel, strain_at(c, d), preferred_element_type=F32
                    )
        for q in range(width // CHUNK):
            here = slice(q * CHUNK, (q + 1) * CHUNK)
            at = pl.ds(pl.multiple_of(s * width + q * CHUNK, CHUNK), CHUNK)
            column = (s * (width // CHUNK) + q) * 2 * CHUNK
            re_at = pl.ds(pl.multiple_of(column, CHUNK), CHUNK)
            im_at = pl.ds(pl.multiple_of(column + CHUNK, CHUNK), CHUNK)
            for _, lhs_ref, pad, base in lists:
                real_part = picked_ref[0, base : base + 2 * pad, here]
                imag_part = picked_ref[1, base : base + 2 * pad, here]
                for lag in range(lags):
                    cosine = cos_own[lag : lag + 1, at]
                    sine = sin_own[lag : lag + 1, at]
                    rot_re = (real_part * cosine - imag_part * sine).astype(BF16)
                    rot_im = (real_part * sine + imag_part * cosine).astype(BF16)
                    top = (2 * lag) * 2 * pad
                    low = (2 * lag + 1) * 2 * pad
                    lhs_ref[top : top + 2 * pad, re_at] = rot_re
                    lhs_ref[top : top + 2 * pad, im_at] = rot_im
                    lhs_ref[low : low + 2 * pad, re_at] = rot_im
                    lhs_ref[low : low + 2 * pad, im_at] = -rot_re

    def landed_strain(s):
        return lambda c, d: strain_all[s, c, d * rec : (d + 1) * rec, :]

    blocks = total_rows // BLOCK_TPL

    per_part = blocks // (2 * banks)

    def codes_at(of, part):
        return code_ref.at[pl.ds((of * banks + part) * per_part, per_part)]

    def codes(part):
        fill_codes((core * banks + part) * per_part, per_part)
        if part:
            send_codes(part - 1)

    def send_codes(part):
        push(
            lambda: remote(
                codes_at(core, part), codes_at(core, part),
                code_send.at[part], code_recv.at[part], to_near,
            )
        )

    zero = jnp.zeros((), BF16)
    lane_c = lax.broadcasted_iota(jnp.int32, (2 * chunks, 2 * TPL), 1)
    second = jnp.where(lax.broadcasted_iota(jnp.int32, (chunks, 2 * TPL), 1) < TPL, 0.0, 1.0)

    def blocks_of(region):
        ids = [reads_ref[region, i] for i in range(4)]
        return [(b // held_blocks, b % held_blocks, b) for b in ids]

    def region_weights(region, close_ref):
        weight = jnp.zeros((8, 2 * TPL), F32)
        count = jnp.zeros((2 * chunks, 2 * TPL), F32)
        for i, (home, inner, _) in enumerate(blocks_of(region)):
            total = power_all[home, 0]
            for s in range(1, segs):
                total = total + power_all[home, s]
            edges_at = count_ref[home]
            for k in range(held_blocks):
                shift = (i - k + 2 * held_blocks) * BLOCK_TPL % (2 * TPL)
                wanted = jnp.where(lane_c % TPL // BLOCK_TPL == i, inner, held_blocks) == k
                weight = jnp.where(wanted[:8], pltpu.roll(total, shift, 1), weight)
                count = jnp.where(wanted, pltpu.roll(edges_at, shift, 1), count)
        weight = weight + 1e-06
        inv_weight = 1.0 / weight
        first = count[:chunks] + upper.astype(F32)
        last = count[chunks:] + upper.astype(F32)
        for a in range(2):
            close = jnp.zeros((chunks, 2 * TPL), F32)
            for m in range(BINS // SLOTS):
                level = second + float(SLOTS * m + 2 * a)
                close = jnp.where(
                    (level >= first) & (level < last), inv_weight[2 * m + a : 2 * m + a + 1], close
                )
            close_ref[a] = close
        norm = jnp.sum(weight, axis=0, keepdims=True)
        close_ref[2] = jnp.broadcast_to(
            1.0 / (norm + pltpu.roll(norm, TPL, 1)), (chunks, 2 * TPL)
        )

    def half_steps(which, region, lhs_ref, close_ref, acc_ref, sum_ref, total_ref):
        tpl_ref = tpl_own if which == 0 else tpl_far
        blocks = blocks_of(region)
        per_half = chunks // 2
        for step in range(per_half):
            at_step = which * per_half + step
            chunk = at_step + upper * (chunks - 1 - 2 * at_step)
            place = step + upper * (per_half - 1 - 2 * step)
            s, q = place // (width // CHUNK), lax.rem(place, width // CHUNK)
            at = pl.ds(pl.multiple_of(q * CHUNK, CHUNK), CHUNK)
            code_at = pl.ds(pl.multiple_of(chunk * CHUNK, CHUNK), CHUNK)
            lhs_at = pl.ds(pl.multiple_of(chunk * 2 * CHUNK, 2 * CHUNK), 2 * CHUNK)
            code = jnp.concatenate(
                [code_ref[b, :, code_at] for _, _, b in blocks], axis=0
            )
            planes = [
                jnp.concatenate(
                    [tpl_ref[home, s, c, inner, :, at] for home, inner, _ in blocks], axis=0
                )
                for c in range(2)
            ]
            matrix = []
            for slot in range(SLOTS):
                inside = code == jnp.asarray(slot, BF16)
                matrix.append(
                    jnp.concatenate([jnp.where(inside, plane, zero) for plane in planes], axis=1)
                )
            part = lax.dot_general(
                lhs_ref[:, lhs_at], jnp.concatenate(matrix, axis=0), NT, preferred_element_type=F32
            )
            fresh = at_step == 0
            both = part[:, : 2 * TPL] + part[:, 2 * TPL :]
            total_ref[...] = both if fresh else total_ref[...] + both
            for a in range(2):
                close = close_ref[a, pl.ds(chunk, 1), :]
                here = part[:, a * 2 * TPL : (a + 1) * 2 * TPL]
                if not fresh:
                    here = here + acc_ref[a]
                term = here * here * close
                sum_ref[a] = term if fresh else sum_ref[a] + term
                acc_ref[a] = jnp.where(close > 0.0, 0.0, here)

    def finish_list(pad, close_ref, sum_ref, total_ref, store):
        inv_norm = close_ref[2, 0:1, :]
        for lag in range(lags):
            top = lag * 4 * pad
            full = total_ref[top : top + 4 * pad]
            full = full + pltpu.roll(full, TPL, 1)
            energy = sum_ref[0, top : top + 4 * pad] + sum_ref[1, top : top + 4 * pad]
            signal = full * full * inv_norm
            signal = (signal[:pad] + signal[pad : 2 * pad]) + (
                signal[2 * pad : 3 * pad] + signal[3 * pad :]
            )
            energy = (energy[:pad] + energy[pad : 2 * pad]) + (
                energy[2 * pad : 3 * pad] + energy[3 * pad :]
            )
            energy = energy + pltpu.roll(energy, TPL, 1)
            store(lag, signal)
            store(lags + lag, (energy - signal) * (1.0 / (2 * BINS - 2)))

    kept = rest_acc.shape[0]

    def other_region(i):
        return lax.rem(hot_ref[0] + i, banks)

    def hot_half(which):
        if which == 0:
            region_weights(hot_ref[0], hot_close)
        half_steps(which, hot_ref[0], hot_lhs, hot_close, hot_acc, hot_sum, hot_total)

    def rest_half(which, i, at):
        if which == 0:
            region_weights(other_region(i), rest_close.at[at])
        half_steps(
            which, other_region(i), rest_lhs, rest_close.at[at],
            rest_acc.at[at], rest_sum.at[at], rest_total.at[at],
        )

    def rest_done(i, at):
        region = other_region(i)

        def store(where, value):
            at = slice(where * 2 * TPL, (where + 1) * 2 * TPL)
            stat_ref[hot_pad:, at] = jnp.where(rest_reg[...] == region, value, stat_ref[hot_pad:, at])

        finish_list(rest_pad, rest_close.at[at], rest_sum.at[at], rest_total.at[at], store)

    def each_other(body):
        def one(i, carry):
            body(i)
            return carry

        lax.fori_loop(1, banks, one, 0)

    split_rest = kept == banks - 1
    sides = [(side, hops) for hops in range(1, banks) for side in range(2)]
    every = [(0, 0)] + sides
    work = [functools.partial(codes, part) for part in range(banks)]

    def some(count=1):
        for _ in range(min(count, len(work))):
            work.pop(0)()

    pl.semaphore_wait(barrier, met)
    send_own()
    for copy in small:
        copy.wait()
    fill_tables()
    fill_power()
    send_power()
    fill_turns()
    pick_lists()
    fill_lhs(seg, lambda c, d: strain_ref[c, d * rec : (d + 1) * rec, :])
    for hops in range(1, banks):
        for side in range(2):
            relay(Z, side, hops)
        for side in range(2):
            pow_relay(P_Z, side, hops)
        if hops == 1:
            push(lambda: remote(own_plane, there, tpl_send.at[X, 0], tpl_recv.at[X, 0], to_far))
        if hops == 2 or banks == 2:
            landed(strain_all.at[far], str_recv.at[0])
            push(
                lambda: remote(
                    strain_all.at[far], strain_all.at[far], str_send.at[2], str_recv.at[2], to_near
                )
            )
            landed(strain_all.at[near], str_recv.at[1])
            fill_lhs(near, landed_strain(near))
        some()
    push(
        lambda: remote(
            other_plane, there_other, tpl_send.at[X_OTHER, 0], tpl_recv.at[X_OTHER, 0], to_far
        )
    )
    for hops in range(1, banks):
        for side in range(2):
            relay(X, side, hops)
            relay(Y_OWN, side, hops)
        for side in range(2):
            pow_relay(P_X, side, hops)
        some(2 if hops > 1 else 1)
        if hops == 1:
            fill_lhs(far, landed_strain(far))
    some(len(work))
    landed(strain_all.at[far_near], str_recv.at[2])
    fill_lhs(far_near, landed_strain(far_near))
    send_codes(banks - 1)
    pow_relay(P_X)
    for part in range(banks):
        landed(codes_at(core_near, part), code_recv.at[part])
    for side, hops in every:
        for kind in (N_MINE, N_OTHER):
            relay(kind, side, hops)
        for kind in (P_N, P_FAR_N):
            pow_relay(kind, side, hops)
    own_copy.wait()
    own_power.wait()
    relay(X)
    for side in range(2):
        relay(Y_FAR, side, 1)
    hot_half(0)
    relay(X_OTHER)
    for hops in range(2, banks):
        for side in range(2):
            relay(Y_FAR, side, hops)
    if split_rest:
        for i in range(1, banks):
            rest_half(0, i, i - 1)
    for side, hops in every:
        for kind in (N_FAR_MINE, N_FAR_OTHER):
            relay(kind, side, hops)
    stat_ref[...] = jnp.zeros_like(stat_ref)

    hot_half(1)

    def store_hot(where, value):
        stat_ref[:hot_pad, where * 2 * TPL : (where + 1) * 2 * TPL] = value

    finish_list(hot_pad, hot_close, hot_sum, hot_total, store_hot)
    if split_rest:
        for i in range(1, banks):
            rest_half(1, i, i - 1)
            rest_done(i, i - 1)
    else:

        def whole_region(i):
            rest_half(0, i, 0)
            rest_half(1, i, 0)
            rest_done(i, 0)

        each_other(whole_region)

    placed = lax.dot_general(
        jnp.concatenate([hot_sel[...], rest_sel[...]], axis=0), stat_ref[...], TN,
        precision=HIGH, preferred_element_type=F32,
    )
    for which, out_ref in enumerate((snr_ref, chi_ref)):
        for lag in range(lags):
            at = (which * lags + lag) * 2 * TPL
            out_ref[lag] = placed[:, at : at + TPL]
    for finish in started:
        finish()


def any_phase_tables(seg_count, nfreq):
    period = 2 * nfreq
    lag = np.arange(LAGS, dtype=np.int64) - LAGS // 2
    turns = np.mod(lag[:, None] * np.arange(nfreq, dtype=np.int64)[None, :], period)
    angle = turns * (2.0 * math.pi / period)
    shape = (seg_count, LAGS // seg_count, nfreq)
    return (
        jnp.asarray(np.cos(angle).reshape(shape), F32),
        jnp.asarray(np.sin(angle).reshape(shape), F32),
    )


def any_exchange_kernel(
    cap, rec, hot_pad, rest_pad,
    planes_ref, strain_ref, reg_hbm, edges_hbm, cos_ref, sin_ref,
    tpl_all, power_all, bins_ref, hot_lhs, rest_lhs, hot_sel, rest_sel, rest_reg, hot_out,
    strain_all, power_own, bounds_ref, cos_own, sin_own, reg_ref, edges_ref,
    tpl_send, tpl_recv, pow_send, pow_recv, str_send, str_recv, local_sem,
):
    banks, segs = tpl_all.shape[:2]
    grp, bank, seg = lax.axis_index("grp"), lax.axis_index("bank"), lax.axis_index("seg")
    rows, width = planes_ref.shape[1:]
    nfreq = segs * width
    lags = cos_own.shape[0]
    mesh_id = pl.DeviceIdType.MESH
    half = segs // 2
    far = lax.rem(seg + half, segs)
    near = seg + 1 - 2 * lax.rem(seg, 2)
    far_near = lax.rem(near + half, segs)
    mine, other = grp, 1 - grp
    to_far, to_near, to_twin = {"seg": far}, {"seg": near}, {"grp": other}

    small = [
        pltpu.make_async_copy(cos_ref.at[seg], cos_own, local_sem.at[3]),
        pltpu.make_async_copy(sin_ref.at[seg], sin_own, local_sem.at[4]),
        pltpu.make_async_copy(edges_hbm, edges_ref, local_sem.at[5]),
        pltpu.make_async_copy(reg_hbm, reg_ref, local_sem.at[6]),
    ]
    for copy in small:
        copy.start()
    barrier = pltpu.get_barrier_semaphore()
    for off in range(1, banks):
        pl.semaphore_signal(
            barrier, inc=1, device_id={"bank": lax.rem(bank + off, banks)}, device_id_type=mesh_id
        )
    for where in (to_far, to_near, to_twin):
        pl.semaphore_signal(barrier, inc=1, device_id=where, device_id_type=mesh_id)
    pl.semaphore_wait(barrier, banks + 2)

    started = []

    def push(src, dst, send, recv, where):
        copy = pltpu.make_async_remote_copy(
            src_ref=src, dst_ref=dst, send_sem=send, recv_sem=recv,
            device_id=where, device_id_type=mesh_id,
        )
        copy.start()
        started.append(copy)

    def landed(slot, recv):
        pltpu.make_async_remote_copy(
            src_ref=slot, dst_ref=slot, send_sem=recv, recv_sem=recv,
            device_id=to_near, device_id_type=mesh_id,
        ).wait_recv()

    def source(off):
        return lax.rem(bank - off + banks, banks)

    Z, X, Y_OWN, Y_FAR, N_MINE, N_OTHER, N_FAR_MINE, N_FAR_OTHER = range(8)
    holds = {
        Z: (seg, mine), X: (far, mine), Y_OWN: (seg, other), Y_FAR: (far, other),
        N_MINE: (near, mine), N_OTHER: (near, other),
        N_FAR_MINE: (far_near, mine), N_FAR_OTHER: (far_near, other),
    }
    relays = {
        Z: ((X, to_far), (Y_OWN, to_twin), (N_MINE, to_near)),
        X: ((Y_FAR, to_twin), (N_FAR_MINE, to_near)),
        Y_OWN: ((N_OTHER, to_near),),
        Y_FAR: ((N_FAR_OTHER, to_near),),
    }

    def relay(kind, off):
        place, plane = holds[kind]
        slot = tpl_all.at[source(off), place, plane]
        landed(slot, tpl_recv.at[kind, off])
        for way, where in relays.get(kind, ()):
            push(slot, slot, tpl_send.at[way, off], tpl_recv.at[way, off], where)

    P_Z, P_X, P_N, P_FAR_N = range(4)
    pow_holds = {P_Z: seg, P_X: far, P_N: near, P_FAR_N: far_near}
    pow_relays = {P_Z: ((P_X, to_far), (P_N, to_near)), P_X: ((P_FAR_N, to_near),)}

    def pow_relay(kind, off):
        slot = power_all.at[source(off), pow_holds[kind]]
        landed(slot, pow_recv.at[kind, off])
        for way, where in pow_relays.get(kind, ()):
            push(slot, slot, pow_send.at[way, off], pow_recv.at[way, off], where)

    own_plane = planes_ref.at[mine]
    own_slot = tpl_all.at[bank, seg, mine]
    for off in range(1, banks):
        push(
            own_plane, own_slot, tpl_send.at[Z, off], tpl_recv.at[Z, off],
            {"bank": lax.rem(bank + off, banks)},
        )
    push(own_plane, own_slot, tpl_send.at[X, 0], tpl_recv.at[X, 0], to_far)
    own_strain = strain_all.at[0, seg]
    push(strain_ref, own_strain, str_send.at[0], str_recv.at[0], to_far)
    push(strain_ref, own_strain, str_send.at[1], str_recv.at[1], to_near)
    push(own_plane, own_slot, tpl_send.at[N_MINE, 0], tpl_recv.at[N_MINE, 0], to_near)
    push(
        planes_ref.at[other], tpl_all.at[bank, seg, other],
        tpl_send.at[N_OTHER, 0], tpl_recv.at[N_OTHER, 0], to_near,
    )
    own_copies = [
        pltpu.make_async_copy(planes_ref, tpl_all.at[bank, seg], local_sem.at[0]),
        pltpu.make_async_copy(strain_ref, own_strain, local_sem.at[1]),
    ]
    for copy in own_copies:
        copy.start()
    for copy in small:
        copy.wait()

    total_rows = edges_ref.shape[1]
    eye = jnp.where(
        lax.broadcasted_iota(jnp.int32, (128, 128), 0) == lax.broadcasted_iota(jnp.int32, (128, 128), 1),
        1.0, 0.0,
    )
    for first in range(0, total_rows, 128):
        bounds_ref[first : first + 128, :] = lax.dot_general(
            eye, edges_ref[:, first : first + 128].astype(F32), NT,
            precision=HIGH, preferred_element_type=F32,
        )

    def bin_index(bounds, first):
        freq = (
            lax.broadcasted_iota(jnp.int32, (bounds.shape[0], width), 1) + first
        ).astype(F32)
        bin_of = jnp.zeros((bounds.shape[0], width), F32)
        for level in range(BINS - 1):
            bin_of = bin_of + jnp.where(freq >= bounds[:, level : level + 1], 1.0, 0.0)
        return bin_of

    bin_of = bin_index(bounds_ref[pl.ds(pl.multiple_of(bank * rows, 8), rows), :], seg * width)
    real_part = planes_ref[0].astype(F32)
    imag_part = planes_ref[1].astype(F32)
    squares = real_part * real_part + imag_part * imag_part
    ones = jnp.ones((8, width), F32)
    for pair in range(BINS // 2):
        picked = jnp.concatenate(
            [jnp.where(bin_of == float(2 * pair + p), squares, 0.0) for p in range(2)], axis=0
        )
        line = lax.dot_general(ones, picked, NT, precision=HIGH, preferred_element_type=F32)
        power_own[pair : pair + 1, :] = line[0:1, :]
    own_power = pltpu.make_async_copy(power_own, power_all.at[bank, seg], local_sem.at[2])
    own_power.start()
    for off in range(1, banks):
        push(
            power_own, power_all.at[bank, seg], pow_send.at[P_Z, off], pow_recv.at[P_Z, off],
            {"bank": lax.rem(bank + off, banks)},
        )
    push(power_own, power_all.at[bank, seg], pow_send.at[P_X, 0], pow_recv.at[P_X, 0], to_far)
    push(power_own, power_all.at[bank, seg], pow_send.at[P_N, 0], pow_recv.at[P_N, 0], to_near)

    def fill_bins(first, last):
        def one(step, carry):
            at = pl.multiple_of(step * BLOCK_TPL, BLOCK_TPL)
            bounds = bounds_ref[pl.ds(at, BLOCK_TPL), :]
            for s in range(segs):
                bins_ref[pl.ds(at, BLOCK_TPL), s * width : (s + 1) * width] = bin_index(
                    bounds, s * width
                ).astype(BF16)
            return carry

        lax.fori_loop(first, last, one, 0)

    blocks = total_rows // BLOCK_TPL
    for off in range(banks):
        if off:
            relay(Z, off)
            relay(X, off - 1)
        if off == 1:
            landed(strain_all.at[0, far], str_recv.at[0])
            push(
                strain_all.at[0, far], strain_all.at[0, far], str_send.at[2], str_recv.at[2], to_near
            )
        if off > 1:
            relay(Y_OWN, off - 1)
            relay(Y_FAR, off - 2)
        fill_bins(off * blocks // banks, (off + 1) * blocks // banks)
    relay(X, banks - 1)
    relay(Y_OWN, banks - 1)
    relay(Y_FAR, banks - 2)
    for off in range(1, banks):
        pow_relay(P_Z, off)
    landed(strain_all.at[0, near], str_recv.at[1])
    landed(strain_all.at[0, far_near], str_recv.at[2])
    own_copies[1].wait()

    row_idx = lax.broadcasted_iota(jnp.int32, (rec, rec), 0)
    col_idx = lax.broadcasted_iota(jnp.int32, (rec, rec), 1)
    reg_row = reg_ref[0:1, :]
    reg_col = jnp.sum(jnp.where(row_idx == col_idx, reg_row, 0), axis=1, keepdims=True)
    count_row = jnp.sum(jnp.where(reg_col == reg_row, 1, 0), axis=0, keepdims=True)
    hot = jnp.min(jnp.where(count_row >= cap, reg_row, 1 << 20), axis=1, keepdims=True)
    is_hot_col = jnp.where(reg_col == hot, 1, 0)
    is_hot_row = jnp.where(reg_row == hot, 1, 0)
    rank_row = jnp.sum(jnp.where(row_idx < col_idx, is_hot_col, 0), axis=0, keepdims=True)
    rest_row = col_idx[0:1, :] - rank_row
    hot_out[0] = jnp.min(jnp.where(count_row >= cap, reg_row, 1 << 20))
    hot_pick = jnp.where(
        (lax.broadcasted_iota(jnp.int32, (hot_pad, rec), 0) == rank_row) & (is_hot_row == 1), 1, 0
    )
    rest_pick = jnp.where(
        (lax.broadcasted_iota(jnp.int32, (rest_pad, rec), 0) == rest_row) & (is_hot_row == 0), 1, 0
    )
    hot_sel[...] = hot_pick.astype(F32)
    rest_sel[...] = rest_pick.astype(F32)
    rest_reg[...] = jnp.broadcast_to(
        jnp.sum(rest_pick * (reg_row + 1), axis=1, keepdims=True) - 1, rest_reg.shape
    )
    lists = ((hot_pick, hot_lhs, hot_pad), (rest_pick, rest_lhs, rest_pad))
    for s in range(segs):
        if s == segs // 2:
            relay(Y_FAR, banks - 1)
            for off in range(banks):
                pow_relay(P_X, off)
        for pick, lhs_ref, pad in lists:
            sel = pick.astype(F32).astype(BF16)
            at = slice(s * width, (s + 1) * width)
            at_im = slice(nfreq + s * width, nfreq + (s + 1) * width)
            parts = []
            for c in range(2):
                parts.append(
                    jnp.concatenate(
                        [
                            jnp.dot(
                                sel,
                                strain_all[0, s, c, d * rec : (d + 1) * rec, :],
                                preferred_element_type=F32,
                            )
                            for d in range(2)
                        ],
                        axis=0,
                    )
                )
            real_part, imag_part = parts
            for lag in range(lags):
                cosine = cos_own[lag : lag + 1, at]
                sine = sin_own[lag : lag + 1, at]
                rot_re = (real_part * cosine - imag_part * sine).astype(BF16)
                rot_im = (real_part * sine + imag_part * cosine).astype(BF16)
                top = (2 * lag) * 2 * pad
                low = (2 * lag + 1) * 2 * pad
                lhs_ref[top : top + 2 * pad, at] = rot_re
                lhs_ref[top : top + 2 * pad, at_im] = rot_im
                lhs_ref[low : low + 2 * pad, at] = rot_im
                lhs_ref[low : low + 2 * pad, at_im] = -rot_re
    for off in range(banks):
        for kind in (N_MINE, N_OTHER, N_FAR_MINE, N_FAR_OTHER):
            relay(kind, off)
        for kind in (P_N, P_FAR_N):
            pow_relay(kind, off)
    own_copies[0].wait()
    own_power.wait()
    for copy in started:
        copy.wait_send()


def any_follow_kernel(
    held_blocks,
    reads_ref, hot_ref, hot_lhs, rest_lhs, hot_sel, rest_sel, rest_reg,
    t0_ref, t1_ref, t2_ref, t3_ref, b0_ref, b1_ref, b2_ref, b3_ref, power_ref,
    snr_ref, chi_ref,
    tmat, z_ref, hot_stat, rest_stat,
):
    region = pl.program_id(0)
    segs, _, _, width = t0_ref.shape[1:]
    nfreq = segs * width
    lags = snr_ref.shape[0]
    hot_pad, rest_pad = hot_sel.shape[0], rest_sel.shape[0]
    tpl_refs = (t0_ref, t1_ref, t2_ref, t3_ref)
    bin_refs = (b0_ref, b1_ref, b2_ref, b3_ref)

    @pl.when(region == 0)
    def prepare():
        hot_stat[...] = jnp.zeros_like(hot_stat)
        rest_stat[...] = jnp.zeros_like(rest_stat)

    lane = lax.broadcasted_iota(jnp.int32, (8, 2 * TPL), 1)
    weight = jnp.zeros((8, 2 * TPL), F32)
    for i in range(4):
        block_id = reads_ref[region, i]
        bank, inner = block_id // held_blocks, block_id % held_blocks
        total = power_ref[bank, 0]
        for s in range(1, segs):
            total = total + power_ref[bank, s]
        shift = (i - inner + 2 * held_blocks) * BLOCK_TPL % (2 * TPL)
        moved = pltpu.roll(total, shift, 1)
        weight = jnp.where((lane % TPL) // BLOCK_TPL == i, moved, weight)
    weight = weight + 1e-06
    norm = jnp.sum(weight, axis=0, keepdims=True)
    norm = norm + pltpu.roll(norm, TPL, 1)
    inv_norm = 1.0 / norm
    share = weight * inv_norm
    inv_weight = 1.0 / weight

    def run(lhs_ref, pad, store):
        rows = lhs_ref.shape[0]
        group = 4
        for q in range(BINS // group):
            for g in range(group):
                level = jnp.asarray(q * group + g, BF16)
                for i in range(4):
                    at_row = slice(g * TPL + i * BLOCK_TPL, g * TPL + (i + 1) * BLOCK_TPL)
                    for s in range(segs):
                        inside = (
                            bin_refs[i][:, s * width : (s + 1) * width] == level
                        )
                        for c in range(2):
                            at = slice(c * nfreq + s * width, c * nfreq + (s + 1) * width)
                            tmat[q, at_row, at] = jnp.where(
                                inside, tpl_refs[i][0, s, c], jnp.zeros((), BF16)
                            )
            z_ref[0:rows, q * group * TPL : (q + 1) * group * TPL] = lax.dot_general(
                lhs_ref[...], tmat[q], NT, preferred_element_type=F32
            )
        for lag in range(lags):
            top = (2 * lag) * 2 * pad
            low = (2 * lag + 1) * 2 * pad
            zr = [z_ref[top : top + 2 * pad, j * 128 : (j + 1) * 128] for j in range(BINS // 2)]
            zi = [z_ref[low : low + 2 * pad, j * 128 : (j + 1) * 128] for j in range(BINS // 2)]
            full_re = functools.reduce(jnp.add, zr)
            full_im = functools.reduce(jnp.add, zi)
            full_re = full_re + pltpu.roll(full_re, TPL, 1)
            full_im = full_im + pltpu.roll(full_im, TPL, 1)
            signal = (full_re * full_re + full_im * full_im) * inv_norm
            chi = jnp.zeros_like(signal)
            for j in range(BINS // 2):
                diff_re = zr[j] - share[j : j + 1] * full_re
                diff_im = zi[j] - share[j : j + 1] * full_im
                chi = chi + (diff_re * diff_re + diff_im * diff_im) * inv_weight[j : j + 1]
            chi = (chi + pltpu.roll(chi, TPL, 1)) * (1.0 / (2 * BINS - 2))
            store(lag, signal[:pad] + signal[pad:])
            store(lags + lag, chi[:pad] + chi[pad:])

    def store_hot(at, value):
        hot_stat[at] = value

    def store_rest(at, value):
        rest_stat[at] = jnp.where(rest_reg[...] == region, value, rest_stat[at])

    @pl.when(region == hot_ref[0])
    def on_hot():
        run(hot_lhs, hot_pad, store_hot)

    @pl.when(region != hot_ref[0])
    def on_rest():
        run(rest_lhs, rest_pad, store_rest)

    @pl.when(region == pl.num_programs(0) - 1)
    def finish():
        for which, out_ref in enumerate((snr_ref, chi_ref)):
            for lag in range(lags):
                at = which * lags + lag
                value = lax.dot_general(
                    hot_sel[...], hot_stat[at], TN, precision=HIGH, preferred_element_type=F32
                ) + lax.dot_general(
                    rest_sel[...], rest_stat[at], TN, precision=HIGH, preferred_element_type=F32
                )
                out_ref[lag] = value[:, :TPL]


def any_per_device(strain, region_of, templates, reads, edges):
    region_count = lax.axis_size("bank")
    seg_count = lax.axis_size("seg")
    rec, _, _, width = strain.shape
    nfreq = width * seg_count
    held_rows = templates.shape[0]
    held_blocks = held_rows // BLOCK_TPL
    cap = 3 * rec // region_count
    hot_pad, rest_pad = round_up(cap, 8), round_up(rec - cap, 8)
    lags = LAGS // seg_count
    planes = jnp.transpose(templates, (1, 0, 2))
    strain_planes = jnp.transpose(strain, (2, 1, 0, 3)).reshape(2, 2 * rec, width)
    cos_tab, sin_tab = any_phase_tables(seg_count, nfreq)
    reg = region_of.reshape(1, rec)
    rows_hot, rows_rest = lags * 4 * hot_pad, lags * 4 * rest_pad
    vmem = pl.BlockSpec(memory_space=pltpu.VMEM)
    anyw = pl.BlockSpec(memory_space=pl.ANY)
    hbm = pl.BlockSpec(memory_space=pltpu.HBM)
    total_rows = edges.shape[0]

    def struct(shape, dtype):
        return jax.ShapeDtypeStruct(shape, dtype)

    dma = pltpu.SemaphoreType.DMA
    exchanged = pl.pallas_call(
        functools.partial(any_exchange_kernel, cap, rec, hot_pad, rest_pad),
        out_shape=(
            struct((region_count, seg_count) + planes.shape, BF16),
            struct((region_count, seg_count, BINS // 2, 2 * TPL), F32),
            struct((total_rows, nfreq), BF16),
            struct((rows_hot, 2 * nfreq), BF16),
            struct((rows_rest, 2 * nfreq), BF16),
            struct((hot_pad, rec), F32),
            struct((rest_pad, rec), F32),
            struct((rest_pad, 2 * TPL), jnp.int32),
            struct((1,), jnp.int32),
        ),
        in_specs=[vmem, vmem, hbm, hbm, hbm, hbm],
        out_specs=(anyw, anyw) + (vmem,) * 6 + (pl.BlockSpec(memory_space=pltpu.SMEM),),
        scratch_shapes=[
            pltpu.VMEM((1, seg_count) + strain_planes.shape, BF16),
            pltpu.VMEM((BINS // 2, 2 * TPL), F32),
            pltpu.VMEM((total_rows, BINS - 1), F32),
            pltpu.VMEM((lags, nfreq), F32),
            pltpu.VMEM((lags, nfreq), F32),
            pltpu.VMEM((1, rec), jnp.int32),
            pltpu.VMEM((BINS - 1, total_rows), jnp.int32),
            dma((8, region_count)),
            dma((8, region_count)),
            dma((4, region_count)),
            dma((4, region_count)),
            dma((3,)),
            dma((3,)),
            dma((7,)),
        ],
        compiler_params=pltpu.CompilerParams(
            collective_id=1, has_side_effects=True, vmem_limit_bytes=50 * 1024 * 1024
        ),
        name="any_exchange",
    )(planes, strain_planes, reg, edges.T, cos_tab, sin_tab)
    tpl_all, power_all, bins_all, hot_lhs, rest_lhs, hot_sel, rest_sel, rest_reg, hot = exchanged

    def tpl_spec(i):
        def index(r, reads_ref, hot_ref):
            block_id = reads_ref[r, i]
            return (block_id // held_blocks, 0, 0, block_id % held_blocks, 0)

        return pl.BlockSpec((1, seg_count, 2, BLOCK_TPL, width), index)

    def bin_spec(i):
        return pl.BlockSpec((BLOCK_TPL, nfreq), lambda r, reads_ref, hot_ref: (reads_ref[r, i], 0))

    def whole(array):
        return pl.BlockSpec(
            array.shape, lambda r, a, b: (0,) * array.ndim, pipeline_mode=pl.Buffered(1)
        )

    out = struct((lags, rec, TPL), F32)
    resident = (hot_lhs, rest_lhs, hot_sel, rest_sel, rest_reg)
    snr, chi = pl.pallas_call(
        functools.partial(any_follow_kernel, held_blocks),
        out_shape=(out, out),
        grid_spec=pltpu.PrefetchScalarGridSpec(
            num_scalar_prefetch=2,
            grid=(region_count,),
            in_specs=[whole(x) for x in resident]
            + [tpl_spec(i) for i in range(4)]
            + [bin_spec(i) for i in range(4)]
            + [whole(power_all)],
            out_specs=(pl.BlockSpec(out.shape, lambda r, a, b: (0, 0, 0)),) * 2,
            scratch_shapes=[
                pltpu.VMEM((4, 4 * TPL, 2 * nfreq), BF16),
                pltpu.VMEM((max(rows_hot, rows_rest), BINS * TPL), F32),
                pltpu.VMEM((2 * lags, hot_pad, 2 * TPL), F32),
                pltpu.VMEM((2 * lags, rest_pad, 2 * TPL), F32),
            ],
        ),
        compiler_params=pltpu.CompilerParams(
            dimension_semantics=("arbitrary",), vmem_limit_bytes=50 * 1024 * 1024
        ),
        name="any_follow",
    )(
        reads, hot, *resident, tpl_all, tpl_all, tpl_all, tpl_all,
        bins_all, bins_all, bins_all, bins_all, power_all,
    )
    return jnp.transpose(snr, (0, 2, 1)), jnp.transpose(chi, (0, 2, 1))


def per_device(strain, region_of, templates, reads, edges):
    region_count = lax.axis_size("bank")
    seg_count = lax.axis_size("seg")
    rec, _, _, width = strain.shape
    nfreq = width * seg_count
    held_rows = templates.shape[0]
    held_blocks = held_rows // BLOCK_TPL
    cap = 3 * rec // region_count
    hot_pad, rest_pad = round_up(cap, 8), round_up(rec - cap, 8)
    lags = LAGS // seg_count
    planes = jnp.transpose(templates, (1, 0, 2)).reshape(2, held_blocks, BLOCK_TPL, width)
    strain_planes = jnp.transpose(strain, (2, 1, 0, 3)).reshape(2, 2 * rec, width)
    reg = region_of.reshape(1, rec)
    rows_hot, rows_rest = lags * 4 * hot_pad, lags * 4 * rest_pad
    vmem = pl.BlockSpec(memory_space=pltpu.VMEM)
    hbm = pl.BlockSpec(memory_space=pltpu.HBM)
    smem = pl.BlockSpec(memory_space=pltpu.SMEM)
    total_rows = edges.shape[0]
    chunks = nfreq // CHUNK
    kept = region_count - 1 if region_count <= 4 else 1

    def struct(shape, dtype):
        return jax.ShapeDtypeStruct(shape, dtype)

    dma = pltpu.SemaphoreType.DMA
    half_shape = (region_count, seg_count // 2) + planes.shape
    out = struct((lags, rec, TPL), F32)
    snr, chi, most = pl.pallas_call(
        functools.partial(follow_up_kernel, cap, rec, hot_pad, rest_pad, held_blocks),
        out_shape=(out, out, struct((1,), jnp.int32)),
        in_specs=[vmem, vmem, hbm, hbm, hbm],
        out_specs=(vmem, vmem, smem),
        scratch_shapes=[
            pltpu.VMEM(half_shape, BF16),
            pltpu.VMEM(half_shape, BF16),
            pltpu.VMEM((region_count, seg_count, BINS // 2, 2 * TPL), F32),
            pltpu.VMEM((total_rows // BLOCK_TPL, BLOCK_TPL, nfreq), BF16),
            pltpu.VMEM((total_rows, 2 * TPL), F32),
            pltpu.VMEM((region_count, 2 * chunks, 2 * TPL), F32),
            pltpu.VMEM((rows_hot, 2 * nfreq), BF16),
            pltpu.VMEM((rows_rest, 2 * nfreq), BF16),
            pltpu.VMEM((hot_pad, rec), F32),
            pltpu.VMEM((rest_pad, rec), F32),
            pltpu.VMEM((rest_pad, 2 * TPL), jnp.int32),
            pltpu.SMEM((1,), jnp.int32),
            pltpu.VMEM((seg_count,) + strain_planes.shape, BF16),
            pltpu.VMEM((BINS // 2, 2 * TPL), F32),
            pltpu.VMEM((total_rows, 2 * TPL), BF16),
            pltpu.VMEM((8, nfreq), F32),
            pltpu.VMEM((8, nfreq), F32),
            pltpu.VMEM((2, 2 * (hot_pad + rest_pad), width), F32),
            pltpu.VMEM((1, rec), jnp.int32),
            pltpu.VMEM((BINS - 1, total_rows), jnp.int32),
            pltpu.SMEM(reads.shape, jnp.int32),
            pltpu.VMEM((3, chunks, 2 * TPL), F32),
            pltpu.VMEM((kept, 3, chunks, 2 * TPL), F32),
            pltpu.VMEM((2, rows_hot, 2 * TPL), F32),
            pltpu.VMEM((2, rows_hot, 2 * TPL), F32),
            pltpu.VMEM((rows_hot, 2 * TPL), F32),
            pltpu.VMEM((kept, 2, rows_rest, 2 * TPL), F32),
            pltpu.VMEM((kept, 2, rows_rest, 2 * TPL), F32),
            pltpu.VMEM((kept, rows_rest, 2 * TPL), F32),
            pltpu.VMEM((hot_pad + rest_pad, 2 * lags * 2 * TPL), F32),
            dma((9, 2 * region_count)),
            dma((9, 2 * region_count)),
            dma((4, 2 * region_count)),
            dma((4, 2 * region_count)),
            dma((3,)),
            dma((3,)),
            dma((region_count,)),
            dma((region_count,)),
            dma((6,)),
        ],
        compiler_params=pltpu.CompilerParams(
            collective_id=0, has_side_effects=True, vmem_limit_bytes=48 * 1024 * 1024
        ),
        name="follow_up",
    )(planes, strain_planes, reg, edges.T, reads)
    done = jnp.transpose(snr, (0, 2, 1)), jnp.transpose(chi, (0, 2, 1))
    return lax.cond(
        most[0] < SLOTS, lambda: done,
        lambda: any_per_device(strain, region_of, templates, reads, edges),
    )


def solution(mesh):
    placed = (
        P(("grp", "bank"), None, None, "seg"),
        P(("grp", "bank")),
        P("bank", None, "seg"),
        P(),
        P(),
    )
    return jax.shard_map(
        per_device,
        mesh=mesh,
        in_specs=placed,
        out_specs=(P("seg", None, ("grp", "bank")), P("seg", None, ("grp", "bank"))),
        check_vma=False,
    )
```
